256 devices in a mesh: gx: 4 (over y_lo, core), gy: 8 (over z), gz: 8 (over y_hi, x).
Axes of the slice: x: 4, y: 4 (y_hi: 2, y_lo: 2; y = y_hi * 2 + y_lo), z: 8, core: 2. Of those that a mesh axis runs over, the one named last changes fastest.
Arguments:
- block: float32 [32, 64, 64, 256], P('gx', 'gy', 'gz'), may hold values from -8 to 8
- onsite: float32 [32, 64, 64], P('gx', 'gy', 'gz'), may hold values from -8 to 8
- hopping: float32 [13], replicated, may hold values from -1 to 1
- cut_frac: float32 [1], replicated, may hold values from -0.5 to 0
Outputs:
- states: float32 [32, 64, 64, 256], P('gx', 'gy', 'gz')
- projected: float32 [256, 256], replicated
- factor: float32 [256, 256], replicated
The draws below stay inside these ranges and needn't reach their ends.
All inputs are finite; a program needn't handle non-finite values. Where the reference program divides by a largest or mean magnitude, that divisor is 1e-20 or more.
Results may differ from the reference program's by a relative error of at most 0.0008.
Values sent between devices are 32-bit elements; how exact they have to be, the bound alone decides.
A program may use at most 64 MiB of HBM per device.

```python
import jax
import jax.numpy as jnp
from jax import lax

M = 256
DEG = 4
NX = 32
NY = 64
NZ = 64
SITES = 131072


def draw_block(key, part):
    key_fields = jax.random.fold_in(key, 11)
    key_scales = jax.random.fold_in(key, 12)
    key_noise = jax.random.fold_in(key, 13)
    place = jnp.arange(NX, dtype=jnp.float32) / (NX - 1)
    fields = jax.random.truncated_normal(key_fields, -5.0, 5.0, (NX, NY, NZ, 8), jnp.float32)
    noise = jax.random.truncated_normal(key_noise, -5.0, 5.0, (NX, NY, NZ, M), jnp.float32)
    rise = 0.25 + 0.75 * place
    scales = jax.random.uniform(key_scales, (M,), jnp.float32, 0.5, 1.5)
    shared = jnp.tile(fields, (1, 1, 1, M // 8))
    return (shared * scales + 0.006 * noise) * rise[:, None, None, None]


def level_of(key, extent, cuts, least, high):
    factor_of = 1.0
    for position, blocks in cuts:
        draws = jax.random.uniform(jax.random.fold_in(jax.random.fold_in(key, 6), position), (blocks,), jnp.float32, least / len(cuts), high / len(cuts))
        factor_of = factor_of * jnp.repeat(jnp.exp(draws), extent[position] // blocks).reshape((-1,) + (1,) * (len(extent) - 1 - position))
    return factor_of


def setup_inputs(seed: int = 0) -> dict:
    key_list = jax.random.split(jax.random.key(seed), 5)
    return {
        "block": draw_block(jax.random.fold_in(key_list[4], 71), 0),
        "onsite": jnp.clip(jax.random.uniform(key_list[1], (NX, NY, NZ), jnp.float32, -8.0, 8.0) * level_of(key_list[1], (NX, NY, NZ), ((0, 4), (1, 8), (2, 8)), -0.4, 0.0), -8.0, 8.0),
        "hopping": jnp.clip(jax.random.uniform(key_list[2], (13,), jnp.float32, -1.0, 1.0), -1.0, 1.0),
        "cut_frac": jnp.clip(jax.random.uniform(key_list[3], (1,), jnp.float32, -0.5, 0.0), -0.5, 0.0),
    }


def half_offsets():
    result = []
    for dx in (-1, 0, 1):
        for dy in (-1, 0, 1):
            for dz in (-1, 0, 1):
                if (dx, dy, dz) > (0, 0, 0):
                    result.append((dx, dy, dz))
    return result

def stencil(padded, field, onsite, hopping):
    size_x, size_y, size_z = (field.shape[0], field.shape[1], field.shape[2])
    total = onsite[:, :, :, None] * field
    for index, offset in enumerate(half_offsets()):
        for sign in (1, -1):
            ax_x, ax_y, ax_z = (1 + sign * offset[0], 1 + sign * offset[1], 1 + sign * offset[2])
            total = total + hopping[index] * padded[ax_x:ax_x + size_x, ax_y:ax_y + size_y, ax_z:ax_z + size_z]
    return total

def apply_ham(field, onsite, hopping):
    padded = jnp.pad(field, ((1, 1), (1, 1), (1, 1), (0, 0)))
    return stencil(padded, field, onsite, hopping)

def cheb_filter(field, onsite, hopping, bound, cut):
    half_width = (bound - cut) / 2.0
    center = (bound + cut) / 2.0
    sigma = half_width / (-bound - center)
    sigma_one = sigma
    older = field
    newer = sigma / half_width * (apply_ham(older, onsite, hopping) - center * older)
    for step in range(DEG - 1):
        sigma_next = 1.0 / (2.0 / sigma_one - sigma)
        nextone = 2.0 * sigma_next / half_width * (apply_ham(newer, onsite, hopping) - center * newer) - sigma * sigma_next * older
        older, newer, sigma = (newer, nextone, sigma_next)
    return newer

def block_map(function, field):
    count = field.shape[3] // 32
    parts = lax.map(lambda j: function(lax.dynamic_slice_in_dim(field, (j * 32).astype(jnp.int32), 32, 3)), jnp.arange(count, dtype=jnp.int32))
    moved = jnp.moveaxis(parts, 0, 3)
    return moved.reshape(field.shape)

def gram_of(left, right):
    return lax.dot_general(left.astype(jnp.float32), right.astype(jnp.float32), (((0,), (0,)), ((), ())), precision=lax.Precision.HIGHEST, preferred_element_type=jnp.float32)

def lower_and_inverse(gram):
    lower = jnp.linalg.cholesky(gram)
    ident = jnp.eye(gram.shape[0], dtype=jnp.float32)
    return (lower, jax.scipy.linalg.solve_triangular(lower, ident, lower=True))

def reference(block, onsite, hopping, cut_frac):
    bound = jnp.max(jnp.abs(onsite)) + 2.0 * jnp.sum(jnp.abs(hopping))
    cut = cut_frac[0] * bound
    filtered = block_map(lambda part: cheb_filter(part, onsite, hopping, bound, cut), block)
    flat = filtered.reshape(-1, M)
    lower_one, factor_one = lower_and_inverse(gram_of(flat, flat) / SITES)
    first = jnp.dot(flat.astype(jnp.float32), factor_one.T.astype(jnp.float32), precision=lax.Precision.HIGHEST, preferred_element_type=jnp.float32)
    lower_two, factor_two = lower_and_inverse(gram_of(first, first) / SITES)
    states = jnp.dot(first.astype(jnp.float32), factor_two.T.astype(jnp.float32), precision=lax.Precision.HIGHEST, preferred_element_type=jnp.float32)
    field = states.reshape(block.shape)
    image = block_map(lambda part: apply_ham(part, onsite, hopping), field).reshape(-1, M)
    projected = gram_of(states, image) / SITES
    return (field, projected, lower_one)
```

```python
import functools

import jax
import jax.numpy as jnp
from jax import lax
from jax.experimental import pallas as pl
from jax.experimental.pallas import tpu as pltpu
from jax.sharding import PartitionSpec as P

DEG = 4
MESH = pl.DeviceIdType.MESH
HIGHEST = lax.Precision.HIGHEST


def extended(block, sides, width):
    for axis, dim in sides:
        count = lax.axis_size(axis)
        forward = [(i, i + 1) for i in range(count - 1)]
        backward = [(target, source) for source, target in forward]
        low = lax.ppermute(
            lax.slice_in_dim(block, block.shape[dim] - width, None, axis=dim), axis, forward
        )
        high = lax.ppermute(lax.slice_in_dim(block, 0, width, axis=dim), axis, backward)
        block = jnp.concatenate([low, block, high], axis=dim)
    return block


def half_offsets():
    result = []
    for dx in (-1, 0, 1):
        for dy in (-1, 0, 1):
            for dz in (-1, 0, 1):
                if (dx, dy, dz) > (0, 0, 0):
                    result.append((dx, dy, dz))
    return result


def stencil(padded, field, onsite, hopping):
    size_x, size_y, size_z = (field.shape[0], field.shape[1], field.shape[2])
    total = onsite[:, :, :, None] * field
    for index, offset in enumerate(half_offsets()):
        for sign in (1, -1):
            ax_x, ax_y, ax_z = (1 + sign * offset[0], 1 + sign * offset[1], 1 + sign * offset[2])
            total = (
                total
                + hopping[index]
                * padded[ax_x : ax_x + size_x, ax_y : ax_y + size_y, ax_z : ax_z + size_z]
            )
    return total


def apply_ham(field, onsite, hopping):
    padded = extended(field, (("gx", 0), ("gy", 1), ("gz", 2)), 1)
    return stencil(padded, field, onsite, hopping)


def cheb_filter(field, operate, bound, cut):
    half_width = (bound - cut) / 2.0
    center = (bound + cut) / 2.0
    sigma = half_width / (-bound - center)
    sigma_one = sigma
    older = field
    newer = sigma / half_width * (operate(older) - center * older)
    for step in range(DEG - 1):
        sigma_next = 1.0 / (2.0 / sigma_one - sigma)
        nextone = (
            2.0 * sigma_next / half_width * (operate(newer) - center * newer)
            - sigma * sigma_next * older
        )
        older, newer, sigma = (newer, nextone, sigma_next)
    return newer


def plane_peer(dims, offset):
    size_x, _, size_z = dims
    place = lax.axis_index("gx") * size_z + lax.axis_index("gz")
    peer = lax.rem(place + offset, size_x * size_z)
    return peer, {"gx": peer // size_z, "gz": lax.rem(peer, size_z)}


def column_peer(dims, offset):
    peer = lax.rem(lax.axis_index("gy") + offset, dims[1])
    return peer, {"gy": peer}


def enter(dims):
    barrier = pltpu.get_barrier_semaphore()
    plane, column = dims[0] * dims[2], dims[1]

    @pl.loop(1, plane)
    def _(k):
        pl.semaphore_signal(barrier, inc=1, device_id=plane_peer(dims, k)[1], device_id_type=MESH)

    @pl.loop(1, column)
    def _(k):
        pl.semaphore_signal(barrier, inc=1, device_id=column_peer(dims, k)[1], device_id_type=MESH)


def entered(dims):
    pl.semaphore_wait(pltpu.get_barrier_semaphore(), dims[0] * dims[2] + dims[1] - 2)


def wait_bytes(ref, sem):
    pltpu.make_async_copy(ref, ref, sem).wait()


def send(src, dst, send_sem, recv_sem, device):
    pltpu.make_async_remote_copy(
        src_ref=src,
        dst_ref=dst,
        send_sem=send_sem,
        recv_sem=recv_sem,
        device_id=device,
        device_id_type=MESH,
    ).start()


def all_reduce(dims, local, total, plane_buf, column_buf, sems):
    plane, column = dims[0] * dims[2], dims[1]
    rows = local.shape[0] // plane
    place = lax.axis_index("gx") * dims[2] + lax.axis_index("gz")
    level = lax.axis_index("gy")
    mine = pl.ds(pl.multiple_of(place * rows, rows), rows)

    @pl.loop(1, plane)
    def _(k):
        peer, device = plane_peer(dims, k)
        theirs = pl.ds(pl.multiple_of(peer * rows, rows), rows)
        send(local.at[theirs], plane_buf.at[k - 1], sems.at[0], sems.at[1], device)

    wait_bytes(plane_buf, sems.at[1])
    column_buf[level] = lax.fori_loop(
        0, plane - 1, lambda k, acc: acc + plane_buf[k], local[mine]
    )

    @pl.loop(1, column)
    def _(k):
        _, device = column_peer(dims, k)
        send(column_buf.at[level], column_buf.at[level], sems.at[2], sems.at[3], device)

    wait_bytes(column_buf.at[pl.ds(0, column - 1)], sems.at[3])
    part = column_buf[0]
    for k in range(1, column):
        part = part + column_buf[k]
    total[mine] = part

    @pl.loop(1, plane)
    def _(k):
        _, device = plane_peer(dims, k)
        send(total.at[mine], total.at[mine], sems.at[4], sems.at[5], device)

    wait_bytes(total.at[pl.ds(0, (plane - 1) * rows)], sems.at[5])
    wait_bytes(plane_buf, sems.at[0])
    wait_bytes(column_buf.at[pl.ds(0, column - 1)], sems.at[2])
    wait_bytes(total.at[pl.ds(0, (plane - 1) * rows)], sems.at[4])


def reduce_scratch(dims, size):
    plane, column = dims[0] * dims[2], dims[1]
    rows = size // plane
    return [
        pltpu.VMEM((plane - 1, rows, size), jnp.float32),
        pltpu.VMEM((column, rows, size), jnp.float32),
        pltpu.SemaphoreType.DMA((6,)),
    ]


def gram_kernel(dims, sites, left, right, out, local, total, plane_buf, column_buf, sems):
    enter(dims)
    local[...] = lax.dot_general(
        left[...],
        right[...],
        (((0,), (0,)), ((), ())),
        precision=HIGHEST,
        preferred_element_type=jnp.float32,
    )
    entered(dims)
    all_reduce(dims, local, total, plane_buf, column_buf, sems)
    out[...] = total[...] / sites


def gram_sum(dims, sites, left, right, ident):
    size = left.shape[1]
    vmem = pl.BlockSpec(memory_space=pltpu.VMEM)
    return pl.pallas_call(
        functools.partial(gram_kernel, dims, sites),
        out_shape=jax.ShapeDtypeStruct((size, size), jnp.float32),
        in_specs=[vmem, vmem],
        out_specs=vmem,
        scratch_shapes=[pltpu.VMEM((size, size), jnp.float32)] * 2 + reduce_scratch(dims, size),
        compiler_params=pltpu.CompilerParams(
            collective_id=ident, has_side_effects=True, vmem_limit_bytes=32 << 20
        ),
    )(left, right)


def max_kernel(dims, onsite, out, plane_buf, column_buf, sems):
    enter(dims)
    plane, column = dims[0] * dims[2], dims[1]
    place = lax.axis_index("gx") * dims[2] + lax.axis_index("gz")
    level = lax.axis_index("gy")
    plane_buf[place] = jnp.full(plane_buf.shape[1:], jnp.max(jnp.abs(onsite[...])), jnp.float32)
    entered(dims)

    @pl.loop(1, plane)
    def _(k):
        _, device = plane_peer(dims, k)
        send(plane_buf.at[place], plane_buf.at[place], sems.at[0], sems.at[1], device)

    wait_bytes(plane_buf.at[pl.ds(0, plane - 1)], sems.at[1])
    column_buf[level] = jnp.max(plane_buf[...], axis=0)

    @pl.loop(1, column)
    def _(k):
        _, device = column_peer(dims, k)
        send(column_buf.at[level], column_buf.at[level], sems.at[2], sems.at[3], device)

    wait_bytes(column_buf.at[pl.ds(0, column - 1)], sems.at[3])
    out[...] = jnp.max(column_buf[...], axis=0)
    wait_bytes(plane_buf.at[pl.ds(0, plane - 1)], sems.at[0])
    wait_bytes(column_buf.at[pl.ds(0, column - 1)], sems.at[2])


def max_all(dims, onsite):
    vmem = pl.BlockSpec(memory_space=pltpu.VMEM)
    plane, column = dims[0] * dims[2], dims[1]
    out = pl.pallas_call(
        functools.partial(max_kernel, dims),
        out_shape=jax.ShapeDtypeStruct((8, 128), jnp.float32),
        in_specs=[vmem],
        out_specs=vmem,
        scratch_shapes=[
            pltpu.VMEM((plane, 8, 128), jnp.float32),
            pltpu.VMEM((column, 8, 128), jnp.float32),
            pltpu.SemaphoreType.DMA((4,)),
        ],
        compiler_params=pltpu.CompilerParams(collective_id=0, has_side_effects=True),
    )(onsite.reshape(-1, onsite.shape[-1]))
    return out[0, 0]


def lower_and_inverse(gram):
    lower = jnp.linalg.cholesky(gram)
    ident = jnp.eye(gram.shape[0], dtype=jnp.float32)
    return (lower, jax.scipy.linalg.solve_triangular(lower, ident, lower=True))


def rotate(flat, factor):
    return jnp.dot(flat, factor.T, precision=HIGHEST, preferred_element_type=jnp.float32)


def body(dims, block, onsite, hopping, cut_frac):
    shape = block.shape
    size_x, size_y, size_z, columns = shape
    total_sites = size_x * size_y * size_z * dims[0] * dims[1] * dims[2]
    largest = max_all(dims, onsite)
    bound = largest + 2.0 * jnp.sum(jnp.abs(hopping))
    cut = cut_frac[0] * bound
    filtered = cheb_filter(block, lambda field: apply_ham(field, onsite, hopping), bound, cut)
    flat = filtered.reshape(-1, columns)
    gram_one = gram_sum(dims, total_sites, flat, flat, 1)
    lower_one, inverse_one = lower_and_inverse(gram_one)
    first = rotate(flat, inverse_one)
    gram_two = gram_sum(dims, total_sites, first, first, 2)
    lower_two, factor_two = lower_and_inverse(gram_two)
    states = rotate(first, factor_two)
    image = apply_ham(states.reshape(shape), onsite, hopping).reshape(-1, columns)
    projected = gram_sum(dims, total_sites, states, image, 3)
    return (states.reshape(shape), projected, lower_one)


def solution(mesh):
    dims = (mesh.shape["gx"], mesh.shape["gy"], mesh.shape["gz"])
    return jax.shard_map(
        functools.partial(body, dims),
        mesh=mesh,
        in_specs=(P("gx", "gy", "gz", None), P("gx", "gy", "gz"), P(), P()),
        out_specs=(P("gx", "gy", "gz", None), P(), P()),
        check_vma=False,
    )
```

```python
import functools

import jax
import jax.numpy as jnp
from jax import lax
from jax.experimental import pallas as pl
from jax.experimental.pallas import tpu as pltpu
from jax.sharding import PartitionSpec as P

DEG = 4
MESH = pl.DeviceIdType.MESH
HIGHEST = lax.Precision.HIGHEST
AXES = ("gx", "gy", "gz")
OFFSETS = [
    (dx, dy, dz)
    for dx in (-1, 0, 1)
    for dy in (-1, 0, 1)
    for dz in (-1, 0, 1)
    if (dx, dy, dz) != (0, 0, 0)
]
POSITIVE = [offset for offset in OFFSETS if offset > (0, 0, 0)]


def hop_index(offset):
    return POSITIVE.index(max(offset, tuple(-d for d in offset)))


def plane_peer(dims, offset):
    size_x, _, size_z = dims
    place = lax.axis_index("gx") * size_z + lax.axis_index("gz")
    peer = lax.rem(place + offset, size_x * size_z)
    return peer, {"gx": peer // size_z, "gz": lax.rem(peer, size_z)}


def column_peer(dims, offset):
    peer = lax.rem(lax.axis_index("gy") + offset, dims[1])
    return peer, {"gy": peer}


def has_neighbour(dims, offset):
    valid = None
    for axis, size, step in zip(AXES, dims, offset):
        if step:
            place = lax.axis_index(axis)
            here = place < size - 1 if step > 0 else place > 0
            valid = here if valid is None else jnp.logical_and(valid, here)
    return valid


def neighbour(offset):
    return {axis: lax.axis_index(axis) + step for axis, step in zip(AXES, offset) if step}


def enter(dims, halo):
    barrier = pltpu.get_barrier_semaphore()

    @pl.loop(1, dims[0] * dims[2])
    def _(k):
        pl.semaphore_signal(barrier, inc=1, device_id=plane_peer(dims, k)[1], device_id_type=MESH)

    @pl.loop(1, dims[1])
    def _(k):
        pl.semaphore_signal(barrier, inc=1, device_id=column_peer(dims, k)[1], device_id_type=MESH)

    if halo:
        for offset in OFFSETS:

            @pl.when(has_neighbour(dims, offset))
            def _():
                pl.semaphore_signal(
                    barrier, inc=1, device_id=neighbour(offset), device_id_type=MESH
                )


def entered(dims, halo):
    count = dims[0] * dims[2] + dims[1] - 2
    if halo:
        boxes = 1
        for axis, size in zip(AXES, dims):
            place = lax.axis_index(axis)
            boxes = boxes * (3 - (place == 0).astype(jnp.int32) - (place == size - 1).astype(jnp.int32))
        count = count + boxes - 1
    pl.semaphore_wait(pltpu.get_barrier_semaphore(), count)


def wait_bytes(ref, sem):
    pltpu.make_async_copy(ref, ref, sem).wait()


def send(src, dst, send_sem, recv_sem, device):
    pltpu.make_async_remote_copy(
        src_ref=src,
        dst_ref=dst,
        send_sem=send_sem,
        recv_sem=recv_sem,
        device_id=device,
        device_id_type=MESH,
    ).start()


def all_reduce(dims, local, total, plane_buf, column_buf, sems):
    plane, column = dims[0] * dims[2], dims[1]
    rows = local.shape[0] // plane
    place = lax.axis_index("gx") * dims[2] + lax.axis_index("gz")
    level = lax.axis_index("gy")
    mine = pl.ds(pl.multiple_of(place * rows, rows), rows)

    @pl.loop(1, plane)
    def _(k):
        peer, device = plane_peer(dims, k)
        theirs = pl.ds(pl.multiple_of(peer * rows, rows), rows)
        send(local.at[theirs], plane_buf.at[k - 1], sems.at[0], sems.at[1], device)

    wait_bytes(plane_buf, sems.at[1])
    column_buf[level] = lax.fori_loop(
        0, plane - 1, lambda k, acc: acc + plane_buf[k], local[mine]
    )

    @pl.loop(1, column)
    def _(k):
        _, device = column_peer(dims, k)
        send(column_buf.at[level], column_buf.at[level], sems.at[2], sems.at[3], device)

    wait_bytes(column_buf.at[pl.ds(0, column - 1)], sems.at[3])
    part = column_buf[0]
    for k in range(1, column):
        part = part + column_buf[k]
    total[mine] = part

    @pl.loop(1, plane)
    def _(k):
        _, device = plane_peer(dims, k)
        send(total.at[mine], total.at[mine], sems.at[4], sems.at[5], device)

    wait_bytes(total.at[pl.ds(0, (plane - 1) * rows)], sems.at[5])
    wait_bytes(plane_buf, sems.at[0])
    wait_bytes(column_buf.at[pl.ds(0, column - 1)], sems.at[2])
    wait_bytes(total.at[pl.ds(0, (plane - 1) * rows)], sems.at[4])


def reduce_scratch(dims, size):
    plane, column = dims[0] * dims[2], dims[1]
    rows = size // plane
    return [
        pltpu.VMEM((size, size), jnp.float32),
        pltpu.VMEM((size, size), jnp.float32),
        pltpu.VMEM((plane - 1, rows, size), jnp.float32),
        pltpu.VMEM((column, rows, size), jnp.float32),
        pltpu.SemaphoreType.DMA((6,)),
    ]


def max_start(dims, value, plane_buf, sems):
    plane = dims[0] * dims[2]
    place = lax.axis_index("gx") * dims[2] + lax.axis_index("gz")

    @pl.loop(1, plane)
    def _(k):
        _, device = plane_peer(dims, k)
        send(plane_buf.at[place], plane_buf.at[place], sems.at[0], sems.at[1], device)


def max_middle(dims, plane_buf, column_buf, sems):
    plane, column = dims[0] * dims[2], dims[1]
    level = lax.axis_index("gy")
    wait_bytes(plane_buf.at[pl.ds(0, plane - 1)], sems.at[1])
    column_buf[level] = jnp.max(plane_buf[...], axis=0)

    @pl.loop(1, column)
    def _(k):
        _, device = column_peer(dims, k)
        send(column_buf.at[level], column_buf.at[level], sems.at[2], sems.at[3], device)


def max_end(dims, plane_buf, column_buf, sems):
    plane, column = dims[0] * dims[2], dims[1]
    wait_bytes(column_buf.at[pl.ds(0, column - 1)], sems.at[3])
    wait_bytes(plane_buf.at[pl.ds(0, plane - 1)], sems.at[0])
    wait_bytes(column_buf.at[pl.ds(0, column - 1)], sems.at[2])
    return jnp.max(column_buf[...], axis=0)


def halo_scratch(shape, slots):
    size_x, size_y, size_z, columns = shape
    f32 = jnp.float32
    return [
        pltpu.VMEM((slots, size_x + 2, size_y + 2, size_z, columns), f32),
        pltpu.VMEM((slots, 2, size_x + 2, size_y, columns), f32),
        pltpu.VMEM((slots, 2, 2, size_x, columns), f32),
        pltpu.VMEM((slots, 2, 2, 2, 8, columns), f32),
        pltpu.VMEM((slots, 2, size_x, size_y, columns), f32),
        pltpu.VMEM((slots, 2, 2, size_x, columns), f32),
        pltpu.VMEM((slots, 2, 2, 2, 8, columns), f32),
        pltpu.VMEM((2, size_x + 2, size_y + 2, size_z, columns), f32),
        pltpu.SemaphoreType.DMA((slots, 2, len(OFFSETS))),
    ]


def halo_parts(shape, slot, offset, field, face, edge, corner, face_out, edge_out, corner_out):
    size_x, size_y, _, _ = shape
    sx, sy, sz = offset
    low = {1: 0, -1: 1}

    def ends(step, size):
        if step == 0:
            return pl.ds(1, size), pl.ds(1, size)
        return (size, 0) if step > 0 else (1, size + 1)

    from_x, to_x = ends(sx, size_x)
    from_y, to_y = ends(sy, size_y)
    if sz == 0:
        return field.at[slot, from_x, from_y], field.at[slot, to_x, to_y]
    top = 1 if sz > 0 else 0
    if sy == 0:
        source = pl.ds(0, size_x) if sx == 0 else from_x - 1
        return face_out.at[slot, top, source], face.at[slot, 1 - top, to_x]
    far = 1 if sy > 0 else 0
    if sx == 0:
        return edge_out.at[slot, top, far], edge.at[slot, 1 - top, 1 - far]
    right = 1 if sx > 0 else 0
    return (
        corner_out.at[slot, top, far, right],
        corner.at[slot, 1 - top, 1 - far, 1 - right],
    )


def zero_border(dims, shape, slots, field, face, edge, corner):
    size_x, size_y, size_z, columns = shape
    for slot in range(slots):
        for side in (0, 1):
            step = 1 if side else -1
            row = size_x + 1 if side else 0

            @pl.when(jnp.logical_not(has_neighbour(dims, (step, 0, 0))))
            def _():
                field[slot, row] = jnp.zeros((size_y + 2, size_z, columns), jnp.float32)
                for top in (0, 1):
                    face[slot, top, row] = jnp.zeros((size_y, columns), jnp.float32)
                    for far in (0, 1):
                        corner[slot, top, far, side] = jnp.zeros((8, columns), jnp.float32)

            row_y = size_y + 1 if side else 0

            @pl.when(jnp.logical_not(has_neighbour(dims, (0, step, 0))))
            def _():
                field[slot, :, row_y] = jnp.zeros((size_x + 2, size_z, columns), jnp.float32)
                for top in (0, 1):
                    edge[slot, top, side] = jnp.zeros((size_x, columns), jnp.float32)
                    for right in (0, 1):
                        corner[slot, top, side, right] = jnp.zeros((8, columns), jnp.float32)

            @pl.when(jnp.logical_not(has_neighbour(dims, (0, 0, step))))
            def _():
                face[slot, side] = jnp.zeros((size_x + 2, size_y, columns), jnp.float32)
                edge[slot, side] = jnp.zeros((2, size_x, columns), jnp.float32)
                corner[slot, side] = jnp.zeros((2, 2, 8, columns), jnp.float32)


def pack_column(shape, slot, x, y, value, face_out, edge_out):
    size_y, size_z = shape[1], shape[2]
    for top, z in ((0, 0), (1, size_z - 1)):
        row = value[z : z + 1]
        face_out[slot, top, x, y : y + 1] = row
        if y in (0, size_y - 1):
            edge_out[slot, top, 1 if y else 0, pl.ds(x, 1)] = row


def pack_corners(shape, slot, field, corner_out):
    size_x, size_y, size_z, columns = shape
    for top in (0, 1):
        for far in (0, 1):
            for right in (0, 1):
                z = (size_z - 1) * top
                corner_out[slot, top, far, right] = jnp.broadcast_to(
                    field[slot, size_x if right else 1, size_y if far else 1, z : z + 1],
                    (8, columns),
                )


def halo_send(dims, shape, slot, refs, sems):
    for index, offset in enumerate(OFFSETS):

        @pl.when(has_neighbour(dims, offset))
        def _():
            src, dst = halo_parts(shape, slot, offset, *refs)
            send(src, dst, sems.at[slot, 0, index], sems.at[slot, 1, index], neighbour(offset))


def halo_wait(dims, shape, slot, refs, sems, received):
    for index, offset in enumerate(OFFSETS):
        from_there = tuple(-step for step in offset)

        @pl.when(has_neighbour(dims, from_there if received else offset))
        def _():
            src, dst = halo_parts(shape, slot, offset, *refs)
            if received:
                wait_bytes(dst, sems.at[slot, 1, index])
            else:
                wait_bytes(src, sems.at[slot, 0, index])


def shift_columns(shape, slot, field, face, edge, corner, shifted):
    size_x, size_y, size_z, columns = shape
    place = lax.broadcasted_iota(jnp.int32, (size_z, columns), 0)

    def put(x, y, below, above):
        value = field[slot, x, y]
        shifted[0, x, y] = jnp.where(place == 0, below, pltpu.roll(value, 1, 0))
        shifted[1, x, y] = jnp.where(place == size_z - 1, above, pltpu.roll(value, size_z - 1, 0))

    @pl.loop(0, size_x + 2)
    def _(x):
        for y in range(size_y):
            put(x, y + 1, face[slot, 0, x, y : y + 1], face[slot, 1, x, y : y + 1])

    for far in (0, 1):
        y = size_y + 1 if far else 0

        @pl.loop(0, size_x)
        def _(x):
            put(x + 1, y, edge[slot, 0, far, pl.ds(x, 1)], edge[slot, 1, far, pl.ds(x, 1)])

        for right in (0, 1):
            x = size_x + 1 if right else 0
            put(x, y, corner[slot, 0, far, right], corner[slot, 1, far, right])


def apply_rows(shape, slot, x, field, shifted, onsite, hopping):
    size_y, columns = shape[1], shape[3]
    totals = [None] * size_y
    centres = [None] * size_y
    for dx in (-1, 0, 1):
        for y in range(-1, size_y + 1):
            for dz in (-1, 0, 1):
                if dz == 0:
                    value = field[slot, x + 1 + dx, y + 1]
                else:
                    value = shifted[0 if dz < 0 else 1, x + 1 + dx, y + 1]
                for dy in (-1, 0, 1):
                    target = y - dy
                    if not 0 <= target < size_y:
                        continue
                    if (dx, dy, dz) == (0, 0, 0):
                        centres[target] = value
                        level = onsite[x, target]
                        term = jnp.concatenate([level] * (columns // level.shape[1]), 1) * value
                    else:
                        term = hopping[hop_index((dx, dy, dz))] * value
                    totals[target] = term if totals[target] is None else totals[target] + term
    return totals, centres


def filter_kernel(
    dims, shape, sites,
    block, onsite, hopping, cut_frac,
    flat, gram,
    field, face, edge, corner, face_out, edge_out, corner_out, shifted, halo_sems,
    max_plane, max_column, max_sems, coef,
    local, total, plane_buf, column_buf, sums_sems,
):
    size_x, size_y, size_z, columns = shape
    refs = (field, face, edge, corner, face_out, edge_out, corner_out)
    zero_border(dims, shape, 2, field, face, edge, corner)
    enter(dims, True)
    place = lax.axis_index("gx") * dims[2] + lax.axis_index("gz")
    max_plane[place] = jnp.full((8, 128), jnp.max(jnp.abs(onsite[...])), jnp.float32)

    @pl.loop(0, size_x)
    def _(x):
        for y in range(size_y):
            value = block[x, y]
            field[0, x + 1, y + 1] = value
            pack_column(shape, 0, x, y, value, face_out, edge_out)

    pack_corners(shape, 0, field, corner_out)
    entered(dims, True)
    for step in range(DEG):
        slot, after = step % 2, (step + 1) % 2
        halo_send(dims, shape, slot, refs, halo_sems)
        if step == 0:
            max_start(dims, None, max_plane, max_sems)
            max_middle(dims, max_plane, max_column, max_sems)
        halo_wait(dims, shape, slot, refs, halo_sems, True)
        shift_columns(shape, slot, field, face, edge, corner, shifted)
        if step == 0:
            bound = max_end(dims, max_plane, max_column, max_sems)
            reach = jnp.abs(hopping[0])
            for k in range(1, len(POSITIVE)):
                reach = reach + jnp.abs(hopping[k])
            bound = bound + 2.0 * reach
            cut = cut_frac[0] * bound
            half_width = (bound - cut) / 2.0
            center = (bound + cut) / 2.0
            sigma_one = half_width / (-bound - center)
            sigma = sigma_one
            coef[0] = center
            coef[1] = sigma / half_width
            for k in range(1, DEG):
                sigma_next = 1.0 / (2.0 / sigma_one - sigma)
                coef[2 * k] = 2.0 * sigma_next / half_width
                coef[2 * k + 1] = sigma * sigma_next
                sigma = sigma_next
        if step:
            halo_wait(dims, shape, after, refs, halo_sems, False)

        @pl.loop(0, size_x)
        def _(x):
            wide = lambda k: jnp.concatenate([coef[k]] * (columns // 128), 1)
            totals, centres = apply_rows(shape, slot, x, field, shifted, onsite, hopping)
            for y in range(size_y):
                value = totals[y] - wide(0) * centres[y]
                if step == 0:
                    value = wide(1) * value
                else:
                    older = field[after, x + 1, y + 1]
                    value = wide(2 * step) * value - wide(2 * step + 1) * older
                if step == DEG - 1:
                    flat[pl.ds(pl.multiple_of((x * size_y + y) * size_z, size_z), size_z)] = value
                else:
                    field[after, x + 1, y + 1] = value
                    pack_column(shape, after, x, y, value, face_out, edge_out)

        if step < DEG - 1:
            pack_corners(shape, after, field, corner_out)
    halo_wait(dims, shape, (DEG - 1) % 2, refs, halo_sems, False)
    local[...] = product(flat[...], flat[...])
    all_reduce(dims, local, total, plane_buf, column_buf, sums_sems)
    gram[...] = total[...] / sites


def product(left, right):
    return lax.dot_general(
        left,
        right,
        (((0,), (0,)), ((), ())),
        precision=HIGHEST,
        preferred_element_type=jnp.float32,
    )


def rotated(flat, factor):
    return lax.dot_general(
        flat,
        factor,
        (((1,), (1,)), ((), ())),
        precision=HIGHEST,
        preferred_element_type=jnp.float32,
    )


def rotate_kernel(
    dims, sites, flat, factor, first, gram, local, total, plane_buf, column_buf, sums_sems
):
    enter(dims, False)
    first[...] = rotated(flat[...], factor[...])
    local[...] = product(first[...], first[...])
    entered(dims, False)
    all_reduce(dims, local, total, plane_buf, column_buf, sums_sems)
    gram[...] = total[...] / sites


def project_kernel(
    dims, shape, sites,
    first, factor, onsite, hopping,
    states, gram,
    field, face, edge, corner, face_out, edge_out, corner_out, shifted, halo_sems, image,
    local, total, plane_buf, column_buf, sums_sems,
):
    size_x, size_y, size_z, columns = shape
    refs = (field, face, edge, corner, face_out, edge_out, corner_out)
    zero_border(dims, shape, 1, field, face, edge, corner)
    enter(dims, True)
    states[...] = rotated(first[...], factor[...])

    def rows(x, y):
        return pl.ds(pl.multiple_of((x * size_y + y) * size_z, size_z), size_z)

    @pl.loop(0, size_x)
    def _(x):
        for y in range(size_y):
            value = states[rows(x, y)]
            field[0, x + 1, y + 1] = value
            pack_column(shape, 0, x, y, value, face_out, edge_out)

    pack_corners(shape, 0, field, corner_out)
    entered(dims, True)
    halo_send(dims, shape, 0, refs, halo_sems)
    halo_wait(dims, shape, 0, refs, halo_sems, True)
    shift_columns(shape, 0, field, face, edge, corner, shifted)

    @pl.loop(0, size_x)
    def _(x):
        totals, _ = apply_rows(shape, 0, x, field, shifted, onsite, hopping)
        for y in range(size_y):
            image[rows(x, y)] = totals[y]

    halo_wait(dims, shape, 0, refs, halo_sems, False)
    local[...] = product(states[...], image[...])
    all_reduce(dims, local, total, plane_buf, column_buf, sums_sems)
    gram[...] = total[...] / sites


def call(kernel, inputs, scalars, outputs, scratch, ident):
    vmem = pl.BlockSpec(memory_space=pltpu.VMEM)
    smem = pl.BlockSpec(memory_space=pltpu.SMEM)
    return pl.pallas_call(
        kernel,
        out_shape=[jax.ShapeDtypeStruct(shape, jnp.float32) for shape in outputs],
        in_specs=[vmem] * len(inputs) + [smem] * len(scalars),
        out_specs=[vmem] * len(outputs),
        scratch_shapes=scratch,
        compiler_params=pltpu.CompilerParams(
            collective_id=ident, has_side_effects=True, vmem_limit_bytes=48 << 20
        ),
    )(*inputs, *scalars)


def lower_and_inverse(gram):
    lower = jnp.linalg.cholesky(gram)
    ident = jnp.eye(gram.shape[0], dtype=jnp.float32)
    return (lower, jax.scipy.linalg.solve_triangular(lower, ident, lower=True))


def body(dims, block, onsite, hopping, cut_frac):
    shape = block.shape
    size_x, size_y, size_z, columns = shape
    count = size_x * size_y * size_z
    sites = count * dims[0] * dims[1] * dims[2]
    plane, column = dims[0] * dims[2], dims[1]
    sums = reduce_scratch(dims, columns)
    levels = jnp.broadcast_to(onsite[..., None], onsite.shape + (128,))
    flat, gram_one = call(
        functools.partial(filter_kernel, dims, shape, sites),
        [block, levels],
        [hopping, cut_frac],
        [(count, columns), (columns, columns)],
        halo_scratch(shape, 2)
        + [
            pltpu.VMEM((plane, 8, 128), jnp.float32),
            pltpu.VMEM((column, 8, 128), jnp.float32),
            pltpu.SemaphoreType.DMA((4,)),
            pltpu.VMEM((2 * DEG, 8, 128), jnp.float32),
        ]
        + sums,
        1,
    )
    lower_one, inverse_one = lower_and_inverse(gram_one)
    first, gram_two = call(
        functools.partial(rotate_kernel, dims, sites),
        [flat, inverse_one],
        [],
        [(count, columns), (columns, columns)],
        sums,
        2,
    )
    _, inverse_two = lower_and_inverse(gram_two)
    states, projected = call(
        functools.partial(project_kernel, dims, shape, sites),
        [first, inverse_two, levels],
        [hopping],
        [(count, columns), (columns, columns)],
        halo_scratch(shape, 1) + [pltpu.VMEM((count, columns), jnp.float32)] + sums,
        3,
    )
    return (states.reshape(shape), projected, lower_one)


def solution(mesh):
    dims = (mesh.shape["gx"], mesh.shape["gy"], mesh.shape["gz"])
    return jax.shard_map(
        functools.partial(body, dims),
        mesh=mesh,
        in_specs=(P("gx", "gy", "gz", None), P("gx", "gy", "gz"), P(), P()),
        out_specs=(P("gx", "gy", "gz", None), P(), P()),
        check_vma=False,
    )
```

```python
import functools

import jax
import jax.numpy as jnp
from jax import lax
from jax.experimental import pallas as pl
from jax.experimental.pallas import tpu as pltpu
from jax.sharding import PartitionSpec as P

DEG = 4
MESH = pl.DeviceIdType.MESH
HIGHEST = lax.Precision.HIGHEST
AXES = ("gx", "gy", "gz")
OFFSETS = [
    (dx, dy, dz)
    for dx in (-1, 0, 1)
    for dy in (-1, 0, 1)
    for dz in (-1, 0, 1)
    if (dx, dy, dz) != (0, 0, 0)
]
POSITIVE = [offset for offset in OFFSETS if offset > (0, 0, 0)]


def hop_index(offset):
    return POSITIVE.index(max(offset, tuple(-d for d in offset)))


def plane_peer(dims, offset):
    size_x, _, size_z = dims
    place = lax.axis_index("gx") * size_z + lax.axis_index("gz")
    peer = lax.rem(place + offset, size_x * size_z)
    return peer, {"gx": peer // size_z, "gz": lax.rem(peer, size_z)}


def column_peer(dims, offset):
    peer = lax.rem(lax.axis_index("gy") + offset, dims[1])
    return peer, {"gy": peer}


def has_neighbour(dims, offset):
    valid = None
    for axis, size, step in zip(AXES, dims, offset):
        if step:
            place = lax.axis_index(axis)
            here = place < size - 1 if step > 0 else place > 0
            valid = here if valid is None else jnp.logical_and(valid, here)
    return valid


def neighbour(offset):
    return {axis: lax.axis_index(axis) + step for axis, step in zip(AXES, offset) if step}


def enter(dims, halo):
    barrier = pltpu.get_barrier_semaphore()

    @pl.loop(1, dims[0] * dims[2])
    def _(k):
        pl.semaphore_signal(barrier, inc=1, device_id=plane_peer(dims, k)[1], device_id_type=MESH)

    @pl.loop(1, dims[1])
    def _(k):
        pl.semaphore_signal(barrier, inc=1, device_id=column_peer(dims, k)[1], device_id_type=MESH)

    if halo:
        for offset in OFFSETS:

            @pl.when(has_neighbour(dims, offset))
            def _():
                pl.semaphore_signal(
                    barrier, inc=1, device_id=neighbour(offset), device_id_type=MESH
                )


def entered(dims, halo):
    count = dims[0] * dims[2] + dims[1] - 2
    if halo:
        boxes = 1
        for axis, size in zip(AXES, dims):
            place = lax.axis_index(axis)
            boxes = boxes * (3 - (place == 0).astype(jnp.int32) - (place == size - 1).astype(jnp.int32))
        count = count + boxes - 1
    pl.semaphore_wait(pltpu.get_barrier_semaphore(), count)


def wait_bytes(ref, sem):
    pltpu.make_async_copy(ref, ref, sem).wait()


def send(src, dst, send_sem, recv_sem, device):
    pltpu.make_async_remote_copy(
        src_ref=src,
        dst_ref=dst,
        send_sem=send_sem,
        recv_sem=recv_sem,
        device_id=device,
        device_id_type=MESH,
    ).start()


def all_reduce(dims, local, total, plane_buf, column_buf, sems):
    plane, column = dims[0] * dims[2], dims[1]
    rows = local.shape[0] // plane
    place = lax.axis_index("gx") * dims[2] + lax.axis_index("gz")
    level = lax.axis_index("gy")
    mine = pl.ds(pl.multiple_of(place * rows, rows), rows)

    @pl.loop(1, plane)
    def _(k):
        peer, device = plane_peer(dims, k)
        theirs = pl.ds(pl.multiple_of(peer * rows, rows), rows)
        send(local.at[theirs], plane_buf.at[k - 1], sems.at[0], sems.at[1], device)

    wait_bytes(plane_buf, sems.at[1])
    column_buf[level] = lax.fori_loop(
        0, plane - 1, lambda k, acc: acc + plane_buf[k], local[mine]
    )

    @pl.loop(1, column)
    def _(k):
        _, device = column_peer(dims, k)
        send(column_buf.at[level], column_buf.at[level], sems.at[2], sems.at[3], device)

    wait_bytes(column_buf.at[pl.ds(0, column - 1)], sems.at[3])
    part = column_buf[0]
    for k in range(1, column):
        part = part + column_buf[k]
    total[mine] = part

    @pl.loop(1, plane)
    def _(k):
        _, device = plane_peer(dims, k)
        send(total.at[mine], total.at[mine], sems.at[4], sems.at[5], device)

    wait_bytes(total.at[pl.ds(0, (plane - 1) * rows)], sems.at[5])
    wait_bytes(plane_buf, sems.at[0])
    wait_bytes(column_buf.at[pl.ds(0, column - 1)], sems.at[2])
    wait_bytes(total.at[pl.ds(0, (plane - 1) * rows)], sems.at[4])


def reduce_scratch(dims, size):
    plane, column = dims[0] * dims[2], dims[1]
    rows = size // plane
    return [
        pltpu.VMEM((size, size), jnp.float32),
        pltpu.VMEM((size, size), jnp.float32),
        pltpu.VMEM((plane - 1, rows, size), jnp.float32),
        pltpu.VMEM((column, rows, size), jnp.float32),
        pltpu.SemaphoreType.DMA((6,)),
    ]


def max_start(dims, value, plane_buf, sems):
    plane = dims[0] * dims[2]
    place = lax.axis_index("gx") * dims[2] + lax.axis_index("gz")

    @pl.loop(1, plane)
    def _(k):
        _, device = plane_peer(dims, k)
        send(plane_buf.at[place], plane_buf.at[place], sems.at[0], sems.at[1], device)


def max_middle(dims, plane_buf, column_buf, sems):
    plane, column = dims[0] * dims[2], dims[1]
    level = lax.axis_index("gy")
    wait_bytes(plane_buf.at[pl.ds(0, plane - 1)], sems.at[1])
    column_buf[level] = jnp.max(plane_buf[...], axis=0)

    @pl.loop(1, column)
    def _(k):
        _, device = column_peer(dims, k)
        send(column_buf.at[level], column_buf.at[level], sems.at[2], sems.at[3], device)


def max_end(dims, plane_buf, column_buf, sems):
    plane, column = dims[0] * dims[2], dims[1]
    wait_bytes(column_buf.at[pl.ds(0, column - 1)], sems.at[3])
    wait_bytes(plane_buf.at[pl.ds(0, plane - 1)], sems.at[0])
    wait_bytes(column_buf.at[pl.ds(0, column - 1)], sems.at[2])
    return jnp.max(column_buf[...], axis=0)


def halo_scratch(shape, slots):
    size_x, size_y, size_z, columns = shape
    f32 = jnp.float32
    return [
        pltpu.VMEM((slots, size_x + 2, size_y + 2, size_z, columns), f32),
        pltpu.VMEM((slots, 2, size_x + 2, size_y, columns), f32),
        pltpu.VMEM((slots, 2, 2, size_x, columns), f32),
        pltpu.VMEM((slots, 2, 2, 2, 8, columns), f32),
        pltpu.VMEM((slots, 2, size_x, size_y, columns), f32),
        pltpu.VMEM((slots, 2, 2, size_x, columns), f32),
        pltpu.VMEM((slots, 2, 2, 2, 8, columns), f32),
        pltpu.VMEM((2, size_x + 2, size_y + 2, size_z, columns), f32),
        pltpu.SemaphoreType.DMA((slots, 2, len(OFFSETS))),
    ]


def halo_parts(shape, slot, offset, field, face, edge, corner, face_out, edge_out, corner_out):
    size_x, size_y, _, _ = shape
    sx, sy, sz = offset
    low = {1: 0, -1: 1}

    def ends(step, size):
        if step == 0:
            return pl.ds(1, size), pl.ds(1, size)
        return (size, 0) if step > 0 else (1, size + 1)

    from_x, to_x = ends(sx, size_x)
    from_y, to_y = ends(sy, size_y)
    if sz == 0:
        return field.at[slot, from_x, from_y], field.at[slot, to_x, to_y]
    top = 1 if sz > 0 else 0
    if sy == 0:
        source = pl.ds(0, size_x) if sx == 0 else from_x - 1
        return face_out.at[slot, top, source], face.at[slot, 1 - top, to_x]
    far = 1 if sy > 0 else 0
    if sx == 0:
        return edge_out.at[slot, top, far], edge.at[slot, 1 - top, 1 - far]
    right = 1 if sx > 0 else 0
    return (
        corner_out.at[slot, top, far, right],
        corner.at[slot, 1 - top, 1 - far, 1 - right],
    )


def zero_border(dims, shape, slots, field, face, edge, corner):
    size_x, size_y, size_z, columns = shape
    for slot in range(slots):
        for side in (0, 1):
            step = 1 if side else -1
            row = size_x + 1 if side else 0

            @pl.when(jnp.logical_not(has_neighbour(dims, (step, 0, 0))))
            def _():
                field[slot, row] = jnp.zeros((size_y + 2, size_z, columns), jnp.float32)
                for top in (0, 1):
                    face[slot, top, row] = jnp.zeros((size_y, columns), jnp.float32)
                    for far in (0, 1):
                        corner[slot, top, far, side] = jnp.zeros((8, columns), jnp.float32)

            row_y = size_y + 1 if side else 0

            @pl.when(jnp.logical_not(has_neighbour(dims, (0, step, 0))))
            def _():
                field[slot, :, row_y] = jnp.zeros((size_x + 2, size_z, columns), jnp.float32)
                for top in (0, 1):
                    edge[slot, top, side] = jnp.zeros((size_x, columns), jnp.float32)
                    for right in (0, 1):
                        corner[slot, top, side, right] = jnp.zeros((8, columns), jnp.float32)

            @pl.when(jnp.logical_not(has_neighbour(dims, (0, 0, step))))
            def _():
                face[slot, side] = jnp.zeros((size_x + 2, size_y, columns), jnp.float32)
                edge[slot, side] = jnp.zeros((2, size_x, columns), jnp.float32)
                corner[slot, side] = jnp.zeros((2, 2, 8, columns), jnp.float32)


def pack_column(shape, slot, x, y, value, face_out, edge_out):
    size_y, size_z = shape[1], shape[2]
    for top, z in ((0, 0), (1, size_z - 1)):
        row = value[z : z + 1]
        face_out[slot, top, x, y : y + 1] = row
        if y in (0, size_y - 1):
            edge_out[slot, top, 1 if y else 0, pl.ds(x, 1)] = row


def pack_corners(shape, slot, field, corner_out):
    size_x, size_y, size_z, columns = shape
    for top in (0, 1):
        for far in (0, 1):
            for right in (0, 1):
                z = (size_z - 1) * top
                corner_out[slot, top, far, right] = jnp.broadcast_to(
                    field[slot, size_x if right else 1, size_y if far else 1, z : z + 1],
                    (8, columns),
                )


def halo_send(dims, shape, slot, refs, sems):
    for index, offset in enumerate(OFFSETS):

        @pl.when(has_neighbour(dims, offset))
        def _():
            src, dst = halo_parts(shape, slot, offset, *refs)
            send(src, dst, sems.at[slot, 0, index], sems.at[slot, 1, index], neighbour(offset))


def halo_wait(dims, shape, slot, refs, sems, received):
    for index, offset in enumerate(OFFSETS):
        from_there = tuple(-step for step in offset)

        @pl.when(has_neighbour(dims, from_there if received else offset))
        def _():
            src, dst = halo_parts(shape, slot, offset, *refs)
            if received:
                wait_bytes(dst, sems.at[slot, 1, index])
            else:
                wait_bytes(src, sems.at[slot, 0, index])


def shift_columns(shape, slot, field, face, edge, corner, shifted):
    size_x, size_y, size_z, columns = shape
    place = lax.broadcasted_iota(jnp.int32, (size_z, columns), 0)

    def put(x, y, below, above):
        value = field[slot, x, y]
        shifted[0, x, y] = jnp.where(place == 0, below, pltpu.roll(value, 1, 0))
        shifted[1, x, y] = jnp.where(place == size_z - 1, above, pltpu.roll(value, size_z - 1, 0))

    @pl.loop(0, size_x + 2)
    def _(x):
        for y in range(size_y):
            put(x, y + 1, face[slot, 0, x, y : y + 1], face[slot, 1, x, y : y + 1])

    for far in (0, 1):
        y = size_y + 1 if far else 0

        @pl.loop(0, size_x)
        def _(x):
            put(x + 1, y, edge[slot, 0, far, pl.ds(x, 1)], edge[slot, 1, far, pl.ds(x, 1)])

        for right in (0, 1):
            x = size_x + 1 if right else 0
            put(x, y, corner[slot, 0, far, right], corner[slot, 1, far, right])


def apply_rows(shape, slot, x, field, shifted, onsite, hopping):
    size_y, columns = shape[1], shape[3]
    totals = [None] * size_y
    centres = [None] * size_y
    for dx in (-1, 0, 1):
        for y in range(-1, size_y + 1):
            for dz in (-1, 0, 1):
                if dz == 0:
                    value = field[slot, x + 1 + dx, y + 1]
                else:
                    value = shifted[0 if dz < 0 else 1, x + 1 + dx, y + 1]
                for dy in (-1, 0, 1):
                    target = y - dy
                    if not 0 <= target < size_y:
                        continue
                    if (dx, dy, dz) == (0, 0, 0):
                        centres[target] = value
                        level = onsite[x, target]
                        term = jnp.concatenate([level] * (columns // level.shape[1]), 1) * value
                    else:
                        term = hopping[hop_index((dx, dy, dz))] * value
                    totals[target] = term if totals[target] is None else totals[target] + term
    return totals, centres


def filter_kernel(
    dims, shape, sites,
    block, onsite, hopping, cut_frac,
    flat, gram,
    field, face, edge, corner, face_out, edge_out, corner_out, shifted, halo_sems,
    max_plane, max_column, max_sems, coef,
    local, total, plane_buf, column_buf, sums_sems,
):
    size_x, size_y, size_z, columns = shape
    refs = (field, face, edge, corner, face_out, edge_out, corner_out)
    zero_border(dims, shape, 2, field, face, edge, corner)
    enter(dims, True)
    place = lax.axis_index("gx") * dims[2] + lax.axis_index("gz")
    max_plane[place] = jnp.full((8, 128), jnp.max(jnp.abs(onsite[...])), jnp.float32)

    @pl.loop(0, size_x)
    def _(x):
        for y in range(size_y):
            value = block[x, y]
            field[0, x + 1, y + 1] = value
            pack_column(shape, 0, x, y, value, face_out, edge_out)

    pack_corners(shape, 0, field, corner_out)
    entered(dims, True)
    for step in range(DEG):
        slot, after = step % 2, (step + 1) % 2
        halo_send(dims, shape, slot, refs, halo_sems)
        if step == 0:
            max_start(dims, None, max_plane, max_sems)
            max_middle(dims, max_plane, max_column, max_sems)
        halo_wait(dims, shape, slot, refs, halo_sems, True)
        shift_columns(shape, slot, field, face, edge, corner, shifted)
        if step == 0:
            bound = max_end(dims, max_plane, max_column, max_sems)
            reach = jnp.abs(hopping[0])
            for k in range(1, len(POSITIVE)):
                reach = reach + jnp.abs(hopping[k])
            bound = bound + 2.0 * reach
            cut = cut_frac[0] * bound
            half_width = (bound - cut) / 2.0
            center = (bound + cut) / 2.0
            sigma_one = half_width / (-bound - center)
            sigma = sigma_one
            coef[0] = center
            coef[1] = sigma / half_width
            for k in range(1, DEG):
                sigma_next = 1.0 / (2.0 / sigma_one - sigma)
                coef[2 * k] = 2.0 * sigma_next / half_width
                coef[2 * k + 1] = sigma * sigma_next
                sigma = sigma_next
        if step:
            halo_wait(dims, shape, after, refs, halo_sems, False)

        @pl.loop(0, size_x)
        def _(x):
            wide = lambda k: jnp.concatenate([coef[k]] * (columns // 128), 1)
            totals, centres = apply_rows(shape, slot, x, field, shifted, onsite, hopping)
            for y in range(size_y):
                value = totals[y] - wide(0) * centres[y]
                if step == 0:
                    value = wide(1) * value
                else:
                    older = field[after, x + 1, y + 1]
                    value = wide(2 * step) * value - wide(2 * step + 1) * older
                if step == DEG - 1:
                    flat[pl.ds(pl.multiple_of((x * size_y + y) * size_z, size_z), size_z)] = value
                else:
                    field[after, x + 1, y + 1] = value
                    pack_column(shape, after, x, y, value, face_out, edge_out)

        if step < DEG - 1:
            pack_corners(shape, after, field, corner_out)
    halo_wait(dims, shape, (DEG - 1) % 2, refs, halo_sems, False)
    local[...] = product(flat[...], flat[...])
    all_reduce(dims, local, total, plane_buf, column_buf, sums_sems)
    gram[...] = total[...] / sites


def product(left, right):
    return lax.dot_general(
        left,
        right,
        (((0,), (0,)), ((), ())),
        precision=HIGHEST,
        preferred_element_type=jnp.float32,
    )


def rotated(flat, factor):
    return lax.dot_general(
        flat,
        factor,
        (((1,), (1,)), ((), ())),
        precision=HIGHEST,
        preferred_element_type=jnp.float32,
    )


def rotate_kernel(
    dims, sites, flat, factor, first, gram, local, total, plane_buf, column_buf, sums_sems
):
    enter(dims, False)
    first[...] = rotated(flat[...], factor[...])
    local[...] = product(first[...], first[...])
    entered(dims, False)
    all_reduce(dims, local, total, plane_buf, column_buf, sums_sems)
    gram[...] = total[...] / sites


def project_kernel(
    dims, shape, sites,
    first, factor, onsite, hopping,
    states, gram,
    field, face, edge, corner, face_out, edge_out, corner_out, shifted, halo_sems, image,
    local, total, plane_buf, column_buf, sums_sems,
):
    size_x, size_y, size_z, columns = shape
    refs = (field, face, edge, corner, face_out, edge_out, corner_out)
    zero_border(dims, shape, 1, field, face, edge, corner)
    enter(dims, True)
    states[...] = rotated(first[...], factor[...])

    def rows(x, y):
        return pl.ds(pl.multiple_of((x * size_y + y) * size_z, size_z), size_z)

    @pl.loop(0, size_x)
    def _(x):
        for y in range(size_y):
            value = states[rows(x, y)]
            field[0, x + 1, y + 1] = value
            pack_column(shape, 0, x, y, value, face_out, edge_out)

    pack_corners(shape, 0, field, corner_out)
    entered(dims, True)
    halo_send(dims, shape, 0, refs, halo_sems)
    halo_wait(dims, shape, 0, refs, halo_sems, True)
    shift_columns(shape, 0, field, face, edge, corner, shifted)

    @pl.loop(0, size_x)
    def _(x):
        totals, _ = apply_rows(shape, 0, x, field, shifted, onsite, hopping)
        for y in range(size_y):
            image[rows(x, y)] = totals[y]

    halo_wait(dims, shape, 0, refs, halo_sems, False)
    local[...] = product(states[...], image[...])
    all_reduce(dims, local, total, plane_buf, column_buf, sums_sems)
    gram[...] = total[...] / sites


def call(kernel, inputs, scalars, outputs, scratch, ident):
    vmem = pl.BlockSpec(memory_space=pltpu.VMEM)
    smem = pl.BlockSpec(memory_space=pltpu.SMEM)
    return pl.pallas_call(
        kernel,
        out_shape=[jax.ShapeDtypeStruct(shape, jnp.float32) for shape in outputs],
        in_specs=[vmem] * len(inputs) + [smem] * len(scalars),
        out_specs=[vmem] * len(outputs),
        scratch_shapes=scratch,
        compiler_params=pltpu.CompilerParams(
            collective_id=ident, has_side_effects=True, vmem_limit_bytes=48 << 20
        ),
    )(*inputs, *scalars)


def factor_kernel(nb, gram, lower, inverse, work):
    size = gram.shape[0]
    tiles = size // 128
    groups = nb // 8
    lane = lax.broadcasted_iota(jnp.int32, (8, 128), 1)
    sub = lax.broadcasted_iota(jnp.int32, (8, 128), 0)
    for t in range(tiles):
        work[t] = gram[:, 128 * t : 128 * (t + 1)]
    for t in range(tiles):
        r = lax.broadcasted_iota(jnp.int32, (size, 128), 0)
        c = lax.broadcasted_iota(jnp.int32, (size, 128), 1) + 128 * t
        work[tiles + t] = jnp.where(r == c, 1.0, 0.0)

    def row(v, j):
        return jnp.broadcast_to(v[j % 8 : j % 8 + 1], (8, 128))

    for start in range(0, size, nb):
        stop = start + nb
        active = [t for t in range(tiles) if 128 * (t + 1) > start]
        active += [tiles + t for t in range(tiles) if 128 * t < stop]
        home = start // 128
        panel = {
            t: [work[t, start + 8 * g : start + 8 * g + 8] for g in range(groups)] for t in active
        }
        cols = [
            [
                jnp.broadcast_to(
                    panel[home][g][:, start % 128 + k : start % 128 + k + 1], (8, 128)
                )
                for g in range(groups)
            ]
            for k in range(nb)
        ]
        recip = [jnp.ones((8, 128), jnp.float32)] * groups
        pivots = [jnp.ones((8, 128), jnp.float32)] * groups
        for j in range(nb):
            home_group = j // 8
            pivot = row(cols[j][home_group], j)
            inv = 1.0 / pivot
            at = sub == j % 8
            recip[home_group] = jnp.where(at, inv, recip[home_group])
            pivots[home_group] = jnp.where(at, pivot, pivots[home_group])
            mult = [None] * groups
            for g in range(home_group, groups):
                mult[g] = cols[j][g] * inv
                if g == home_group:
                    mult[g] = jnp.where(sub > j % 8, mult[g], 0.0)
            for k in range(j + 1, nb):
                top = row(cols[k][home_group], j)
                for g in range(home_group, groups):
                    cols[k][g] = cols[k][g] - mult[g] * top
            for t in active:
                top = row(panel[t][home_group], j)
                for g in range(home_group, groups):
                    panel[t][g] = panel[t][g] - mult[g] * top
        if stop < size:
            full = {t: jnp.concatenate(panel[t], 0) if groups > 1 else panel[t][0] for t in active}
            recips = jnp.concatenate(recip, 0) if groups > 1 else recip[0]
            for u in range(tiles):
                low = max(128 * u, stop)
                if low >= 128 * (u + 1):
                    continue
                left = (full[u] * recips)[:, low - 128 * u :]
                for t in active:
                    if t < u:
                        continue
                    work[t, low : 128 * (u + 1)] -= lax.dot_general(
                        left, full[t], (((0,), (0,)), ((), ())),
                        precision=HIGHEST, preferred_element_type=jnp.float32)
        for g in range(groups):
            scale = 1.0 / jnp.sqrt(pivots[g])
            at = slice(start + 8 * g, start + 8 * g + 8)
            for t in range(tiles):
                if t in active:
                    keep = lane + 128 * t >= sub + (start + 8 * g)
                    work[t, at] = jnp.where(keep, panel[t][g] * scale, 0.0)
                else:
                    work[t, at] = jnp.zeros((8, 128), jnp.float32)
                if tiles + t in active:
                    inverse[at, 128 * t : 128 * t + 128] = panel[tiles + t][g] * scale
                else:
                    inverse[at, 128 * t : 128 * t + 128] = jnp.zeros((8, 128), jnp.float32)
    for t in range(tiles):
        lower[128 * t : 128 * t + 128, :] = work[t].T

def lower_and_inverse(gram, nb=16):
    size = gram.shape[0]
    vmem = pl.BlockSpec(memory_space=pltpu.VMEM)
    return pl.pallas_call(
        functools.partial(factor_kernel, nb),
        out_shape=[jax.ShapeDtypeStruct((size, size), jnp.float32)] * 2,
        in_specs=[vmem], out_specs=[vmem] * 2,
        scratch_shapes=[pltpu.VMEM((2 * (size // 128), size, 128), jnp.float32)],
        compiler_params=pltpu.CompilerParams(vmem_limit_bytes=32 << 20),
    )(gram)


def body(dims, block, onsite, hopping, cut_frac):
    shape = block.shape
    size_x, size_y, size_z, columns = shape
    count = size_x * size_y * size_z
    sites = count * dims[0] * dims[1] * dims[2]
    plane, column = dims[0] * dims[2], dims[1]
    sums = reduce_scratch(dims, columns)
    levels = jnp.broadcast_to(onsite[..., None], onsite.shape + (128,))
    flat, gram_one = call(
        functools.partial(filter_kernel, dims, shape, sites),
        [block, levels],
        [hopping, cut_frac],
        [(count, columns), (columns, columns)],
        halo_scratch(shape, 2)
        + [
            pltpu.VMEM((plane, 8, 128), jnp.float32),
            pltpu.VMEM((column, 8, 128), jnp.float32),
            pltpu.SemaphoreType.DMA((4,)),
            pltpu.VMEM((2 * DEG, 8, 128), jnp.float32),
        ]
        + sums,
        1,
    )
    lower_one, inverse_one = lower_and_inverse(gram_one)
    first, gram_two = call(
        functools.partial(rotate_kernel, dims, sites),
        [flat, inverse_one],
        [],
        [(count, columns), (columns, columns)],
        sums,
        2,
    )
    _, inverse_two = lower_and_inverse(gram_two)
    states, projected = call(
        functools.partial(project_kernel, dims, shape, sites),
        [first, inverse_two, levels],
        [hopping],
        [(count, columns), (columns, columns)],
        halo_scratch(shape, 1) + [pltpu.VMEM((count, columns), jnp.float32)] + sums,
        3,
    )
    return (states.reshape(shape), projected, lower_one)


def solution(mesh):
    dims = (mesh.shape["gx"], mesh.shape["gy"], mesh.shape["gz"])
    return jax.shard_map(
        functools.partial(body, dims),
        mesh=mesh,
        in_specs=(P("gx", "gy", "gz", None), P("gx", "gy", "gz"), P(), P()),
        out_specs=(P("gx", "gy", "gz", None), P(), P()),
        check_vma=False,
    )
```

```python
import functools

import jax
import jax.numpy as jnp
from jax import lax
from jax.experimental import pallas as pl
from jax.experimental.pallas import tpu as pltpu
from jax.sharding import PartitionSpec as P

DEG = 4
PANEL = 16
MESH = pl.DeviceIdType.MESH
HIGHEST = lax.Precision.HIGHEST
AXES = ("gx", "gy", "gz")
OFFSETS = [
    (dx, dy, dz)
    for dx in (-1, 0, 1)
    for dy in (-1, 0, 1)
    for dz in (-1, 0, 1)
    if (dx, dy, dz) != (0, 0, 0)
]
POSITIVE = [offset for offset in OFFSETS if offset > (0, 0, 0)]


def hop_index(offset):
    return POSITIVE.index(max(offset, tuple(-d for d in offset)))


def plane_peer(dims, offset):
    size_x, _, size_z = dims
    place = lax.axis_index("gx") * size_z + lax.axis_index("gz")
    peer = lax.rem(place + offset, size_x * size_z)
    return peer, {"gx": peer // size_z, "gz": lax.rem(peer, size_z)}


def column_peer(dims, offset):
    peer = lax.rem(lax.axis_index("gy") + offset, dims[1])
    return peer, {"gy": peer}


def has_neighbour(dims, offset):
    valid = None
    for axis, size, step in zip(AXES, dims, offset):
        if step:
            place = lax.axis_index(axis)
            here = place < size - 1 if step > 0 else place > 0
            valid = here if valid is None else jnp.logical_and(valid, here)
    return valid


def neighbour(offset):
    return {axis: lax.axis_index(axis) + step for axis, step in zip(AXES, offset) if step}


def enter(dims, halo):
    barrier = pltpu.get_barrier_semaphore()

    @pl.loop(1, dims[0] * dims[2])
    def _(k):
        pl.semaphore_signal(barrier, inc=1, device_id=plane_peer(dims, k)[1], device_id_type=MESH)

    @pl.loop(1, dims[1])
    def _(k):
        pl.semaphore_signal(barrier, inc=1, device_id=column_peer(dims, k)[1], device_id_type=MESH)

    if halo:
        for offset in OFFSETS:

            @pl.when(has_neighbour(dims, offset))
            def _():
                pl.semaphore_signal(
                    barrier, inc=1, device_id=neighbour(offset), device_id_type=MESH
                )


def entered(dims, halo):
    count = dims[0] * dims[2] + dims[1] - 2
    if halo:
        boxes = 1
        for axis, size in zip(AXES, dims):
            place = lax.axis_index(axis)
            boxes = boxes * (3 - (place == 0).astype(jnp.int32) - (place == size - 1).astype(jnp.int32))
        count = count + boxes - 1
    pl.semaphore_wait(pltpu.get_barrier_semaphore(), count)


def wait_bytes(ref, sem):
    pltpu.make_async_copy(ref, ref, sem).wait()


def send(src, dst, send_sem, recv_sem, device):
    pltpu.make_async_remote_copy(
        src_ref=src,
        dst_ref=dst,
        send_sem=send_sem,
        recv_sem=recv_sem,
        device_id=device,
        device_id_type=MESH,
    ).start()


def place_of(dims):
    return lax.axis_index("gx") * dims[2] + lax.axis_index("gz")


class AllReduce:
    def __init__(self, dims, local, total, plane_buf, column_buf, sems):
        self.dims, self.local, self.total = dims, local, total
        self.plane_buf, self.column_buf, self.sems = plane_buf, column_buf, sems
        self.plane, self.column = dims[0] * dims[2], dims[1]
        self.rows = local.shape[0] // self.plane
        self.mine = pl.ds(pl.multiple_of(place_of(dims) * self.rows, self.rows), self.rows)

    def scatter(self):
        @pl.loop(1, self.plane)
        def _(k):
            peer, device = plane_peer(self.dims, k)
            theirs = pl.ds(pl.multiple_of(peer * self.rows, self.rows), self.rows)
            send(
                self.local.at[theirs], self.plane_buf.at[k - 1],
                self.sems.at[0], self.sems.at[1], device,
            )

    def across(self):
        level = lax.axis_index("gy")
        wait_bytes(self.plane_buf, self.sems.at[1])
        self.column_buf[level] = lax.fori_loop(
            0, self.plane - 1, lambda k, acc: acc + self.plane_buf[k], self.local[self.mine]
        )
        mine = self.column_buf.at[level]

        @pl.loop(1, self.column)
        def _(k):
            _, device = column_peer(self.dims, k)
            send(mine, mine, self.sems.at[2], self.sems.at[3], device)

    def gather(self):
        wait_bytes(self.column_buf.at[pl.ds(0, self.column - 1)], self.sems.at[3])
        part = self.column_buf[0]
        for k in range(1, self.column):
            part = part + self.column_buf[k]
        self.total[self.mine] = part
        mine = self.total.at[self.mine]

        @pl.loop(1, self.plane)
        def _(k):
            _, device = plane_peer(self.dims, k)
            send(mine, mine, self.sems.at[4], self.sems.at[5], device)

    def finish(self):
        others = self.total.at[pl.ds(0, (self.plane - 1) * self.rows)]
        wait_bytes(others, self.sems.at[5])
        wait_bytes(self.plane_buf, self.sems.at[0])
        wait_bytes(self.column_buf.at[pl.ds(0, self.column - 1)], self.sems.at[2])
        wait_bytes(others, self.sems.at[4])


def reduce_scratch(dims, size):
    plane, column = dims[0] * dims[2], dims[1]
    rows = size // plane
    return [
        pltpu.VMEM((size, size), jnp.float32),
        pltpu.VMEM((size, size), jnp.float32),
        pltpu.VMEM((plane - 1, rows, size), jnp.float32),
        pltpu.VMEM((column, rows, size), jnp.float32),
        pltpu.SemaphoreType.DMA((6,)),
    ]


def max_start(dims, value, plane_buf, sems):
    plane = dims[0] * dims[2]
    place = lax.axis_index("gx") * dims[2] + lax.axis_index("gz")

    @pl.loop(1, plane)
    def _(k):
        _, device = plane_peer(dims, k)
        send(plane_buf.at[place], plane_buf.at[place], sems.at[0], sems.at[1], device)


def max_middle(dims, plane_buf, column_buf, sems):
    plane, column = dims[0] * dims[2], dims[1]
    level = lax.axis_index("gy")
    wait_bytes(plane_buf.at[pl.ds(0, plane - 1)], sems.at[1])
    column_buf[level] = jnp.max(plane_buf[...], axis=0)

    @pl.loop(1, column)
    def _(k):
        _, device = column_peer(dims, k)
        send(column_buf.at[level], column_buf.at[level], sems.at[2], sems.at[3], device)


def max_end(dims, plane_buf, column_buf, sems):
    plane, column = dims[0] * dims[2], dims[1]
    wait_bytes(column_buf.at[pl.ds(0, column - 1)], sems.at[3])
    wait_bytes(plane_buf.at[pl.ds(0, plane - 1)], sems.at[0])
    wait_bytes(column_buf.at[pl.ds(0, column - 1)], sems.at[2])
    return jnp.max(column_buf[...], axis=0)


def halo_scratch(shape, slots):
    size_x, size_y, size_z, columns = shape
    f32 = jnp.float32
    return [
        pltpu.VMEM((slots, size_x + 2, size_y + 2, size_z, columns), f32),
        pltpu.VMEM((slots, 2, size_x + 2, size_y, columns), f32),
        pltpu.VMEM((slots, 2, 2, size_x, columns), f32),
        pltpu.VMEM((slots, 2, 2, 2, 8, columns), f32),
        pltpu.VMEM((slots, 2, size_x, size_y, columns), f32),
        pltpu.VMEM((slots, 2, 2, size_x, columns), f32),
        pltpu.VMEM((slots, 2, 2, 2, 8, columns), f32),
        pltpu.VMEM((2, size_x + 2, size_y + 2, size_z, columns), f32),
        pltpu.SemaphoreType.DMA((slots, 2, len(OFFSETS))),
    ]


def halo_parts(shape, slot, offset, field, face, edge, corner, face_out, edge_out, corner_out):
    size_x, size_y, _, _ = shape
    sx, sy, sz = offset
    low = {1: 0, -1: 1}

    def ends(step, size):
        if step == 0:
            return pl.ds(1, size), pl.ds(1, size)
        return (size, 0) if step > 0 else (1, size + 1)

    from_x, to_x = ends(sx, size_x)
    from_y, to_y = ends(sy, size_y)
    if sz == 0:
        return field.at[slot, from_x, from_y], field.at[slot, to_x, to_y]
    top = 1 if sz > 0 else 0
    if sy == 0:
        source = pl.ds(0, size_x) if sx == 0 else from_x - 1
        return face_out.at[slot, top, source], face.at[slot, 1 - top, to_x]
    far = 1 if sy > 0 else 0
    if sx == 0:
        return edge_out.at[slot, top, far], edge.at[slot, 1 - top, 1 - far]
    right = 1 if sx > 0 else 0
    return (
        corner_out.at[slot, top, far, right],
        corner.at[slot, 1 - top, 1 - far, 1 - right],
    )


def zero_border(dims, shape, slots, field, face, edge, corner):
    size_x, size_y, size_z, columns = shape
    for slot in range(slots):
        for side in (0, 1):
            step = 1 if side else -1
            row = size_x + 1 if side else 0

            @pl.when(jnp.logical_not(has_neighbour(dims, (step, 0, 0))))
            def _():
                field[slot, row] = jnp.zeros((size_y + 2, size_z, columns), jnp.float32)
                for top in (0, 1):
                    face[slot, top, row] = jnp.zeros((size_y, columns), jnp.float32)
                    for far in (0, 1):
                        corner[slot, top, far, side] = jnp.zeros((8, columns), jnp.float32)

            row_y = size_y + 1 if side else 0

            @pl.when(jnp.logical_not(has_neighbour(dims, (0, step, 0))))
            def _():
                field[slot, :, row_y] = jnp.zeros((size_x + 2, size_z, columns), jnp.float32)
                for top in (0, 1):
                    edge[slot, top, side] = jnp.zeros((size_x, columns), jnp.float32)
                    for right in (0, 1):
                        corner[slot, top, side, right] = jnp.zeros((8, columns), jnp.float32)

            @pl.when(jnp.logical_not(has_neighbour(dims, (0, 0, step))))
            def _():
                face[slot, side] = jnp.zeros((size_x + 2, size_y, columns), jnp.float32)
                edge[slot, side] = jnp.zeros((2, size_x, columns), jnp.float32)
                corner[slot, side] = jnp.zeros((2, 2, 8, columns), jnp.float32)


def pack_column(shape, slot, x, y, value, face_out, edge_out):
    size_y, size_z = shape[1], shape[2]
    for top, z in ((0, 0), (1, size_z - 1)):
        row = value[z : z + 1]
        face_out[slot, top, x, y : y + 1] = row
        if y in (0, size_y - 1):
            edge_out[slot, top, 1 if y else 0, pl.ds(x, 1)] = row


def pack_corners(shape, slot, field, corner_out):
    size_x, size_y, size_z, columns = shape
    for top in (0, 1):
        for far in (0, 1):
            for right in (0, 1):
                z = (size_z - 1) * top
                corner_out[slot, top, far, right] = jnp.broadcast_to(
                    field[slot, size_x if right else 1, size_y if far else 1, z : z + 1],
                    (8, columns),
                )


def halo_send(dims, shape, slot, refs, sems):
    for index, offset in enumerate(OFFSETS):

        @pl.when(has_neighbour(dims, offset))
        def _():
            src, dst = halo_parts(shape, slot, offset, *refs)
            send(src, dst, sems.at[slot, 0, index], sems.at[slot, 1, index], neighbour(offset))


def halo_wait(dims, shape, slot, refs, sems, received):
    for index, offset in enumerate(OFFSETS):
        from_there = tuple(-step for step in offset)

        @pl.when(has_neighbour(dims, from_there if received else offset))
        def _():
            src, dst = halo_parts(shape, slot, offset, *refs)
            if received:
                wait_bytes(dst, sems.at[slot, 1, index])
            else:
                wait_bytes(src, sems.at[slot, 0, index])


def shift_columns(shape, slot, field, face, edge, corner, shifted):
    size_x, size_y, size_z, columns = shape
    place = lax.broadcasted_iota(jnp.int32, (size_z, columns), 0)

    def put(x, y, below, above):
        value = field[slot, x, y]
        shifted[0, x, y] = jnp.where(place == 0, below, pltpu.roll(value, 1, 0))
        shifted[1, x, y] = jnp.where(place == size_z - 1, above, pltpu.roll(value, size_z - 1, 0))

    @pl.loop(0, size_x + 2)
    def _(x):
        for y in range(size_y):
            put(x, y + 1, face[slot, 0, x, y : y + 1], face[slot, 1, x, y : y + 1])

    for far in (0, 1):
        y = size_y + 1 if far else 0

        @pl.loop(0, size_x)
        def _(x):
            put(x + 1, y, edge[slot, 0, far, pl.ds(x, 1)], edge[slot, 1, far, pl.ds(x, 1)])

        for right in (0, 1):
            x = size_x + 1 if right else 0
            put(x, y, corner[slot, 0, far, right], corner[slot, 1, far, right])


def apply_rows(shape, slot, x, field, shifted, onsite, hopping):
    size_y, columns = shape[1], shape[3]
    totals = [None] * size_y
    centres = [None] * size_y
    for dx in (-1, 0, 1):
        for y in range(-1, size_y + 1):
            for dz in (-1, 0, 1):
                if dz == 0:
                    value = field[slot, x + 1 + dx, y + 1]
                else:
                    value = shifted[0 if dz < 0 else 1, x + 1 + dx, y + 1]
                for dy in (-1, 0, 1):
                    target = y - dy
                    if not 0 <= target < size_y:
                        continue
                    if (dx, dy, dz) == (0, 0, 0):
                        centres[target] = value
                        level = onsite[x, target]
                        term = jnp.concatenate([level] * (columns // level.shape[1]), 1) * value
                    else:
                        term = hopping[hop_index((dx, dy, dz))] * value
                    totals[target] = term if totals[target] is None else totals[target] + term
    return totals, centres


def filter_kernel(
    dims, shape, sites,
    block, onsite, hopping, cut_frac,
    flat, image, gram,
    field, face, edge, corner, face_out, edge_out, corner_out, shifted, halo_sems,
    max_plane, max_column, max_sems, coef,
    local, total, plane_buf, column_buf, sums_sems,
):
    size_x, size_y, size_z, columns = shape
    refs = (field, face, edge, corner, face_out, edge_out, corner_out)
    zero_border(dims, shape, 2, field, face, edge, corner)
    enter(dims, True)
    place = lax.axis_index("gx") * dims[2] + lax.axis_index("gz")
    max_plane[place] = jnp.full((8, 128), jnp.max(jnp.abs(onsite[...])), jnp.float32)

    @pl.loop(0, size_x)
    def _(x):
        for y in range(size_y):
            value = block[x, y]
            field[0, x + 1, y + 1] = value
            pack_column(shape, 0, x, y, value, face_out, edge_out)

    pack_corners(shape, 0, field, corner_out)
    entered(dims, True)
    for step in range(DEG):
        slot, after = step % 2, (step + 1) % 2
        halo_send(dims, shape, slot, refs, halo_sems)
        if step == 0:
            max_start(dims, None, max_plane, max_sems)
            max_middle(dims, max_plane, max_column, max_sems)
        halo_wait(dims, shape, slot, refs, halo_sems, True)
        shift_columns(shape, slot, field, face, edge, corner, shifted)
        if step == 0:
            bound = max_end(dims, max_plane, max_column, max_sems)
            reach = jnp.abs(hopping[0])
            for k in range(1, len(POSITIVE)):
                reach = reach + jnp.abs(hopping[k])
            bound = bound + 2.0 * reach
            cut = cut_frac[0] * bound
            half_width = (bound - cut) / 2.0
            center = (bound + cut) / 2.0
            sigma_one = half_width / (-bound - center)
            sigma = sigma_one
            coef[0] = center
            coef[1] = sigma / half_width
            for k in range(1, DEG):
                sigma_next = 1.0 / (2.0 / sigma_one - sigma)
                coef[2 * k] = 2.0 * sigma_next / half_width
                coef[2 * k + 1] = sigma * sigma_next
                sigma = sigma_next
        if step:
            halo_wait(dims, shape, after, refs, halo_sems, False)

        @pl.loop(0, size_x)
        def _(x):
            wide = lambda k: jnp.concatenate([coef[k]] * (columns // 128), 1)
            totals, centres = apply_rows(shape, slot, x, field, shifted, onsite, hopping)
            for y in range(size_y):
                value = totals[y] - wide(0) * centres[y]
                if step == 0:
                    value = wide(1) * value
                else:
                    older = field[after, x + 1, y + 1]
                    value = wide(2 * step) * value - wide(2 * step + 1) * older
                if step == DEG - 1:
                    flat[site_rows(shape, x, y)] = value
                field[after, x + 1, y + 1] = value
                pack_column(shape, after, x, y, value, face_out, edge_out)

        pack_corners(shape, after, field, corner_out)
    slot = DEG % 2
    sums = AllReduce(dims, local, total, plane_buf, column_buf, sums_sems)
    halo_send(dims, shape, slot, refs, halo_sems)
    local[...] = product(flat[...], flat[...])
    sums.scatter()
    halo_wait(dims, shape, slot, refs, halo_sems, True)
    shift_columns(shape, slot, field, face, edge, corner, shifted)
    sums.across()

    @pl.loop(0, size_x)
    def _(x):
        totals, _ = apply_rows(shape, slot, x, field, shifted, onsite, hopping)
        for y in range(size_y):
            image[site_rows(shape, x, y)] = totals[y]

    sums.gather()
    halo_wait(dims, shape, 1 - slot, refs, halo_sems, False)
    halo_wait(dims, shape, slot, refs, halo_sems, False)
    sums.finish()
    gram[...] = total[...] / sites


def site_rows(shape, x, y):
    _, size_y, size_z, _ = shape
    return pl.ds(pl.multiple_of((x * size_y + y) * size_z, size_z), size_z)


def product(left, right):
    return lax.dot_general(
        left,
        right,
        (((0,), (0,)), ((), ())),
        precision=HIGHEST,
        preferred_element_type=jnp.float32,
    )


def rotated(flat, factor):
    return lax.dot_general(
        flat,
        factor,
        (((1,), (1,)), ((), ())),
        precision=HIGHEST,
        preferred_element_type=jnp.float32,
    )


def rotate_kernel(
    dims, sites,
    flat, image, factor,
    first, gram, between,
    moved,
    local, total, plane_buf, column_buf, sums_sems,
    local_b, total_b, plane_buf_b, column_buf_b, sums_sems_b,
):
    enter(dims, False)
    sums = AllReduce(dims, local, total, plane_buf, column_buf, sums_sems)
    sums_b = AllReduce(dims, local_b, total_b, plane_buf_b, column_buf_b, sums_sems_b)
    first[...] = rotated(flat[...], factor[...])
    local[...] = product(first[...], first[...])
    entered(dims, False)
    sums.scatter()
    moved[...] = rotated(image[...], factor[...])
    local_b[...] = product(first[...], moved[...])
    sums_b.scatter()
    sums.across()
    sums_b.across()
    sums.gather()
    sums_b.gather()
    sums.finish()
    gram[...] = total[...] / sites
    sums_b.finish()
    between[...] = total_b[...] / sites


def call(kernel, inputs, scalars, outputs, scratch, ident):
    vmem = pl.BlockSpec(memory_space=pltpu.VMEM)
    smem = pl.BlockSpec(memory_space=pltpu.SMEM)
    return pl.pallas_call(
        kernel,
        out_shape=[jax.ShapeDtypeStruct(shape, jnp.float32) for shape in outputs],
        in_specs=[vmem] * len(inputs) + [smem] * len(scalars),
        out_specs=[vmem] * len(outputs),
        scratch_shapes=scratch,
        compiler_params=pltpu.CompilerParams(
            collective_id=ident, has_side_effects=True, vmem_limit_bytes=48 << 20
        ),
    )(*inputs, *scalars)


def factor_kernel(nb, gram, lower, inverse, work):
    size = gram.shape[0]
    tiles = size // 128
    groups = nb // 8
    lane = lax.broadcasted_iota(jnp.int32, (8, 128), 1)
    sub = lax.broadcasted_iota(jnp.int32, (8, 128), 0)
    for t in range(tiles):
        work[t] = gram[:, 128 * t : 128 * (t + 1)]
    for t in range(tiles):
        r = lax.broadcasted_iota(jnp.int32, (size, 128), 0)
        c = lax.broadcasted_iota(jnp.int32, (size, 128), 1) + 128 * t
        work[tiles + t] = jnp.where(r == c, 1.0, 0.0)

    def row(v, j):
        return jnp.broadcast_to(v[j % 8 : j % 8 + 1], (8, 128))

    for start in range(0, size, nb):
        stop = start + nb
        active = [t for t in range(tiles) if 128 * (t + 1) > start]
        active += [tiles + t for t in range(tiles) if 128 * t < stop]
        home = start // 128
        panel = {
            t: [work[t, start + 8 * g : start + 8 * g + 8] for g in range(groups)] for t in active
        }
        cols = [
            [
                jnp.broadcast_to(
                    panel[home][g][:, start % 128 + k : start % 128 + k + 1], (8, 128)
                )
                for g in range(groups)
            ]
            for k in range(nb)
        ]
        recip = [jnp.ones((8, 128), jnp.float32)] * groups
        pivots = [jnp.ones((8, 128), jnp.float32)] * groups
        for j in range(nb):
            home_group = j // 8
            pivot = row(cols[j][home_group], j)
            inv = 1.0 / pivot
            at = sub == j % 8
            recip[home_group] = jnp.where(at, inv, recip[home_group])
            pivots[home_group] = jnp.where(at, pivot, pivots[home_group])
            mult = [None] * groups
            for g in range(home_group, groups):
                mult[g] = cols[j][g] * inv
                if g == home_group:
                    mult[g] = jnp.where(sub > j % 8, mult[g], 0.0)
            for k in range(j + 1, nb):
                top = row(cols[k][home_group], j)
                for g in range(home_group, groups):
                    cols[k][g] = cols[k][g] - mult[g] * top
            for t in active:
                top = row(panel[t][home_group], j)
                for g in range(home_group, groups):
                    panel[t][g] = panel[t][g] - mult[g] * top
        if stop < size:
            full = {t: jnp.concatenate(panel[t], 0) if groups > 1 else panel[t][0] for t in active}
            recips = jnp.concatenate(recip, 0) if groups > 1 else recip[0]
            for u in range(tiles):
                low = max(128 * u, stop)
                if low >= 128 * (u + 1):
                    continue
                left = (full[u] * recips)[:, low - 128 * u :]
                for t in active:
                    if t < u:
                        continue
                    work[t, low : 128 * (u + 1)] -= lax.dot_general(
                        left, full[t], (((0,), (0,)), ((), ())),
                        precision=HIGHEST, preferred_element_type=jnp.float32)
        for g in range(groups):
            scale = 1.0 / jnp.sqrt(pivots[g])
            at = slice(start + 8 * g, start + 8 * g + 8)
            for t in range(tiles):
                if t in active:
                    keep = lane + 128 * t >= sub + (start + 8 * g)
                    work[t, at] = jnp.where(keep, panel[t][g] * scale, 0.0)
                else:
                    work[t, at] = jnp.zeros((8, 128), jnp.float32)
                if tiles + t in active:
                    inverse[at, 128 * t : 128 * t + 128] = panel[tiles + t][g] * scale
                else:
                    inverse[at, 128 * t : 128 * t + 128] = jnp.zeros((8, 128), jnp.float32)
    for t in range(tiles):
        lower[128 * t : 128 * t + 128, :] = work[t].T

def finish_kernel(nb, gram, first, between, states, projected, lower, inverse, work):
    factor_kernel(nb, gram, lower, inverse, work)
    states[...] = rotated(first[...], inverse[...])
    half = rotated(between[...], inverse[...])
    projected[...] = jnp.dot(
        inverse[...], half, precision=HIGHEST, preferred_element_type=jnp.float32
    )


def local_call(kernel, inputs, outputs, scratch):
    vmem = pl.BlockSpec(memory_space=pltpu.VMEM)
    return pl.pallas_call(
        kernel,
        out_shape=[jax.ShapeDtypeStruct(shape, jnp.float32) for shape in outputs],
        in_specs=[vmem] * len(inputs),
        out_specs=[vmem] * len(outputs),
        scratch_shapes=scratch,
        compiler_params=pltpu.CompilerParams(vmem_limit_bytes=32 << 20),
    )(*inputs)


def body(dims, block, onsite, hopping, cut_frac):
    shape = block.shape
    size_x, size_y, size_z, columns = shape
    count = size_x * size_y * size_z
    sites = count * dims[0] * dims[1] * dims[2]
    plane, column = dims[0] * dims[2], dims[1]
    sums = reduce_scratch(dims, columns)
    levels = jnp.broadcast_to(onsite[..., None], onsite.shape + (128,))
    square = (columns, columns)
    work = pltpu.VMEM((2 * (columns // 128), columns, 128), jnp.float32)
    flat, image, gram_one = call(
        functools.partial(filter_kernel, dims, shape, sites),
        [block, levels],
        [hopping, cut_frac],
        [(count, columns), (count, columns), square],
        halo_scratch(shape, 2)
        + [
            pltpu.VMEM((plane, 8, 128), jnp.float32),
            pltpu.VMEM((column, 8, 128), jnp.float32),
            pltpu.SemaphoreType.DMA((4,)),
            pltpu.VMEM((2 * DEG, 8, 128), jnp.float32),
        ]
        + sums,
        1,
    )
    lower_one, inverse_one = local_call(
        functools.partial(factor_kernel, PANEL), [gram_one], [square, square], [work]
    )
    first, gram_two, between = call(
        functools.partial(rotate_kernel, dims, sites),
        [flat, image, inverse_one],
        [],
        [(count, columns), square, square],
        [pltpu.VMEM((count, columns), jnp.float32)] + sums + sums,
        2,
    )
    states, projected = local_call(
        functools.partial(finish_kernel, PANEL),
        [gram_two, first, between],
        [(count, columns), square],
        [pltpu.VMEM(square, jnp.float32), pltpu.VMEM(square, jnp.float32), work],
    )
    return (states.reshape(shape), projected, lower_one)


def solution(mesh):
    dims = (mesh.shape["gx"], mesh.shape["gy"], mesh.shape["gz"])
    return jax.shard_map(
        functools.partial(body, dims),
        mesh=mesh,
        in_specs=(P("gx", "gy", "gz", None), P("gx", "gy", "gz"), P(), P()),
        out_specs=(P("gx", "gy", "gz", None), P(), P()),
        check_vma=False,
    )
```

```python
import functools

import jax
import jax.numpy as jnp
from jax import lax
from jax.experimental import pallas as pl
from jax.experimental.pallas import tpu as pltpu
from jax.sharding import PartitionSpec as P

DEG = 4
PANEL = 16
HALVES = 2
HALO_REFS = 9
MESH = pl.DeviceIdType.MESH
HIGHEST = lax.Precision.HIGHEST
AXES = ("gx", "gy", "gz")
OFFSETS = [
    (dx, dy, dz)
    for dx in (-1, 0, 1)
    for dy in (-1, 0, 1)
    for dz in (-1, 0, 1)
    if (dx, dy, dz) != (0, 0, 0)
]
POSITIVE = [offset for offset in OFFSETS if offset > (0, 0, 0)]


def hop_index(offset):
    return POSITIVE.index(max(offset, tuple(-d for d in offset)))


def plane_peer(dims, offset):
    size_x, _, size_z = dims
    place = lax.axis_index("gx") * size_z + lax.axis_index("gz")
    peer = lax.rem(place + offset, size_x * size_z)
    return peer, {"gx": peer // size_z, "gz": lax.rem(peer, size_z)}


def column_peer(dims, offset):
    peer = lax.rem(lax.axis_index("gy") + offset, dims[1])
    return peer, {"gy": peer}


def has_neighbour(dims, offset):
    valid = None
    for axis, size, step in zip(AXES, dims, offset):
        if step:
            place = lax.axis_index(axis)
            here = place < size - 1 if step > 0 else place > 0
            valid = here if valid is None else jnp.logical_and(valid, here)
    return valid


def neighbour(offset):
    return {axis: lax.axis_index(axis) + step for axis, step in zip(AXES, offset) if step}


def enter(dims, halo):
    barrier = pltpu.get_barrier_semaphore()

    @pl.loop(1, dims[0] * dims[2])
    def _(k):
        pl.semaphore_signal(barrier, inc=1, device_id=plane_peer(dims, k)[1], device_id_type=MESH)

    @pl.loop(1, dims[1])
    def _(k):
        pl.semaphore_signal(barrier, inc=1, device_id=column_peer(dims, k)[1], device_id_type=MESH)

    if halo:
        for offset in OFFSETS:

            @pl.when(has_neighbour(dims, offset))
            def _():
                pl.semaphore_signal(
                    barrier, inc=1, device_id=neighbour(offset), device_id_type=MESH
                )


def entered(dims, halo):
    count = dims[0] * dims[2] + dims[1] - 2
    if halo:
        boxes = 1
        for axis, size in zip(AXES, dims):
            place = lax.axis_index(axis)
            boxes = boxes * (3 - (place == 0).astype(jnp.int32) - (place == size - 1).astype(jnp.int32))
        count = count + boxes - 1
    pl.semaphore_wait(pltpu.get_barrier_semaphore(), count)


def wait_bytes(ref, sem):
    pltpu.make_async_copy(ref, ref, sem).wait()


def send(src, dst, send_sem, recv_sem, device):
    pltpu.make_async_remote_copy(
        src_ref=src,
        dst_ref=dst,
        send_sem=send_sem,
        recv_sem=recv_sem,
        device_id=device,
        device_id_type=MESH,
    ).start()


def place_of(dims):
    return lax.axis_index("gx") * dims[2] + lax.axis_index("gz")


class AllReduce:
    def __init__(self, dims, local, total, plane_buf, column_buf, sems):
        self.dims, self.local, self.total = dims, local, total
        self.plane_buf, self.column_buf, self.sems = plane_buf, column_buf, sems
        self.plane, self.column = dims[0] * dims[2], dims[1]
        self.rows = local.shape[0] // self.plane
        self.mine = pl.ds(pl.multiple_of(place_of(dims) * self.rows, self.rows), self.rows)

    def scatter(self):
        @pl.loop(1, self.plane)
        def _(k):
            peer, device = plane_peer(self.dims, k)
            theirs = pl.ds(pl.multiple_of(peer * self.rows, self.rows), self.rows)
            send(
                self.local.at[theirs], self.plane_buf.at[k - 1],
                self.sems.at[0], self.sems.at[1], device,
            )

    def across(self):
        level = lax.axis_index("gy")
        wait_bytes(self.plane_buf, self.sems.at[1])
        self.column_buf[level] = lax.fori_loop(
            0, self.plane - 1, lambda k, acc: acc + self.plane_buf[k], self.local[self.mine]
        )
        mine = self.column_buf.at[level]

        @pl.loop(1, self.column)
        def _(k):
            _, device = column_peer(self.dims, k)
            send(mine, mine, self.sems.at[2], self.sems.at[3], device)

    def gather(self):
        wait_bytes(self.column_buf.at[pl.ds(0, self.column - 1)], self.sems.at[3])
        part = self.column_buf[0]
        for k in range(1, self.column):
            part = part + self.column_buf[k]
        self.total[self.mine] = part
        mine = self.total.at[self.mine]

        @pl.loop(1, self.plane)
        def _(k):
            _, device = plane_peer(self.dims, k)
            send(mine, mine, self.sems.at[4], self.sems.at[5], device)

    def finish(self):
        others = self.total.at[pl.ds(0, (self.plane - 1) * self.rows)]
        wait_bytes(others, self.sems.at[5])
        wait_bytes(self.plane_buf, self.sems.at[0])
        wait_bytes(self.column_buf.at[pl.ds(0, self.column - 1)], self.sems.at[2])
        wait_bytes(others, self.sems.at[4])


def reduce_scratch(dims, size):
    plane, column = dims[0] * dims[2], dims[1]
    rows = size // plane
    return [
        pltpu.VMEM((size, size), jnp.float32),
        pltpu.VMEM((size, size), jnp.float32),
        pltpu.VMEM((plane - 1, rows, size), jnp.float32),
        pltpu.VMEM((column, rows, size), jnp.float32),
        pltpu.SemaphoreType.DMA((6,)),
    ]


def max_start(dims, value, plane_buf, sems):
    plane = dims[0] * dims[2]
    place = lax.axis_index("gx") * dims[2] + lax.axis_index("gz")

    @pl.loop(1, plane)
    def _(k):
        _, device = plane_peer(dims, k)
        send(plane_buf.at[place], plane_buf.at[place], sems.at[0], sems.at[1], device)


def max_middle(dims, plane_buf, column_buf, sems):
    plane, column = dims[0] * dims[2], dims[1]
    level = lax.axis_index("gy")
    wait_bytes(plane_buf.at[pl.ds(0, plane - 1)], sems.at[1])
    column_buf[level] = jnp.max(plane_buf[...], axis=0)

    @pl.loop(1, column)
    def _(k):
        _, device = column_peer(dims, k)
        send(column_buf.at[level], column_buf.at[level], sems.at[2], sems.at[3], device)


def max_end(dims, plane_buf, column_buf, sems):
    plane, column = dims[0] * dims[2], dims[1]
    wait_bytes(column_buf.at[pl.ds(0, column - 1)], sems.at[3])
    wait_bytes(plane_buf.at[pl.ds(0, plane - 1)], sems.at[0])
    wait_bytes(column_buf.at[pl.ds(0, column - 1)], sems.at[2])
    return jnp.max(column_buf[...], axis=0)


def halo_scratch(shape, slots):
    size_x, size_y, size_z, columns = shape
    f32 = jnp.float32
    return [
        pltpu.VMEM((slots, size_x + 2, size_y + 2, size_z, columns), f32),
        pltpu.VMEM((slots, 2, size_x + 2, size_y, columns), f32),
        pltpu.VMEM((slots, 2, 2, size_x, columns), f32),
        pltpu.VMEM((slots, 2, 2, 2, 8, columns), f32),
        pltpu.VMEM((slots, 2, size_x, size_y, columns), f32),
        pltpu.VMEM((slots, 2, 2, size_x, columns), f32),
        pltpu.VMEM((slots, 2, 2, 2, 8, columns), f32),
        pltpu.VMEM((2, size_x + 2, size_y + 2, size_z, columns), f32),
        pltpu.SemaphoreType.DMA((slots, 2, len(OFFSETS))),
    ]


def halo_parts(shape, slot, offset, field, face, edge, corner, face_out, edge_out, corner_out):
    size_x, size_y, _, _ = shape
    sx, sy, sz = offset
    low = {1: 0, -1: 1}

    def ends(step, size):
        if step == 0:
            return pl.ds(1, size), pl.ds(1, size)
        return (size, 0) if step > 0 else (1, size + 1)

    from_x, to_x = ends(sx, size_x)
    from_y, to_y = ends(sy, size_y)
    if sz == 0:
        return field.at[slot, from_x, from_y], field.at[slot, to_x, to_y]
    top = 1 if sz > 0 else 0
    if sy == 0:
        source = pl.ds(0, size_x) if sx == 0 else from_x - 1
        return face_out.at[slot, top, source], face.at[slot, 1 - top, to_x]
    far = 1 if sy > 0 else 0
    if sx == 0:
        return edge_out.at[slot, top, far], edge.at[slot, 1 - top, 1 - far]
    right = 1 if sx > 0 else 0
    return (
        corner_out.at[slot, top, far, right],
        corner.at[slot, 1 - top, 1 - far, 1 - right],
    )


def zero_border(dims, shape, slots, field, face, edge, corner):
    size_x, size_y, size_z, columns = shape
    for slot in range(slots):
        for side in (0, 1):
            step = 1 if side else -1
            row = size_x + 1 if side else 0

            @pl.when(jnp.logical_not(has_neighbour(dims, (step, 0, 0))))
            def _():
                field[slot, row] = jnp.zeros((size_y + 2, size_z, columns), jnp.float32)
                for top in (0, 1):
                    face[slot, top, row] = jnp.zeros((size_y, columns), jnp.float32)
                    for far in (0, 1):
                        corner[slot, top, far, side] = jnp.zeros((8, columns), jnp.float32)

            row_y = size_y + 1 if side else 0

            @pl.when(jnp.logical_not(has_neighbour(dims, (0, step, 0))))
            def _():
                field[slot, :, row_y] = jnp.zeros((size_x + 2, size_z, columns), jnp.float32)
                for top in (0, 1):
                    edge[slot, top, side] = jnp.zeros((size_x, columns), jnp.float32)
                    for right in (0, 1):
                        corner[slot, top, side, right] = jnp.zeros((8, columns), jnp.float32)

            @pl.when(jnp.logical_not(has_neighbour(dims, (0, 0, step))))
            def _():
                face[slot, side] = jnp.zeros((size_x + 2, size_y, columns), jnp.float32)
                edge[slot, side] = jnp.zeros((2, size_x, columns), jnp.float32)
                corner[slot, side] = jnp.zeros((2, 2, 8, columns), jnp.float32)


def pack_column(shape, slot, x, y, value, face_out, edge_out):
    size_y, size_z = shape[1], shape[2]
    for top, z in ((0, 0), (1, size_z - 1)):
        row = value[z : z + 1]
        face_out[slot, top, x, y : y + 1] = row
        if y in (0, size_y - 1):
            edge_out[slot, top, 1 if y else 0, pl.ds(x, 1)] = row


def pack_corners(shape, slot, field, corner_out):
    size_x, size_y, size_z, columns = shape
    for top in (0, 1):
        for far in (0, 1):
            for right in (0, 1):
                z = (size_z - 1) * top
                corner_out[slot, top, far, right] = jnp.broadcast_to(
                    field[slot, size_x if right else 1, size_y if far else 1, z : z + 1],
                    (8, columns),
                )


def halo_send(dims, shape, slot, refs, sems):
    for index, offset in enumerate(OFFSETS):

        @pl.when(has_neighbour(dims, offset))
        def _():
            src, dst = halo_parts(shape, slot, offset, *refs)
            send(src, dst, sems.at[slot, 0, index], sems.at[slot, 1, index], neighbour(offset))


def halo_wait(dims, shape, slot, refs, sems, received):
    for index, offset in enumerate(OFFSETS):
        from_there = tuple(-step for step in offset)

        @pl.when(has_neighbour(dims, from_there if received else offset))
        def _():
            src, dst = halo_parts(shape, slot, offset, *refs)
            if received:
                wait_bytes(dst, sems.at[slot, 1, index])
            else:
                wait_bytes(src, sems.at[slot, 0, index])


def shift_columns(shape, slot, field, face, edge, corner, shifted):
    size_x, size_y, size_z, columns = shape
    place = lax.broadcasted_iota(jnp.int32, (size_z, columns), 0)

    def put(x, y, below, above):
        value = field[slot, x, y]
        shifted[0, x, y] = jnp.where(place == 0, below, pltpu.roll(value, 1, 0))
        shifted[1, x, y] = jnp.where(place == size_z - 1, above, pltpu.roll(value, size_z - 1, 0))

    @pl.loop(0, size_x + 2)
    def _(x):
        for y in range(size_y):
            put(x, y + 1, face[slot, 0, x, y : y + 1], face[slot, 1, x, y : y + 1])

    for far in (0, 1):
        y = size_y + 1 if far else 0

        @pl.loop(0, size_x)
        def _(x):
            put(x + 1, y, edge[slot, 0, far, pl.ds(x, 1)], edge[slot, 1, far, pl.ds(x, 1)])

        for right in (0, 1):
            x = size_x + 1 if right else 0
            put(x, y, corner[slot, 0, far, right], corner[slot, 1, far, right])


def apply_rows(shape, slot, x, field, shifted, onsite, hopping):
    size_y = shape[1]
    totals = [None] * size_y
    centres = [None] * size_y
    for dx in (-1, 0, 1):
        for y in range(-1, size_y + 1):
            for dz in (-1, 0, 1):
                if dz == 0:
                    value = field[slot, x + 1 + dx, y + 1]
                else:
                    value = shifted[0 if dz < 0 else 1, x + 1 + dx, y + 1]
                for dy in (-1, 0, 1):
                    target = y - dy
                    if not 0 <= target < size_y:
                        continue
                    if (dx, dy, dz) == (0, 0, 0):
                        centres[target] = value
                        level = onsite[x, target]
                        term = level * value
                    else:
                        term = hopping[hop_index((dx, dy, dz))] * value
                    totals[target] = term if totals[target] is None else totals[target] + term
    return totals, centres


def spread(onsite, levels):
    size_x, size_y, size_z, lanes = levels.shape
    diagonal = lax.broadcasted_iota(jnp.int32, (size_z, size_z), 0) == lax.broadcasted_iota(
        jnp.int32, (size_z, size_z), 1
    )

    @pl.loop(0, size_x)
    def _(x):
        for y in range(size_y):
            row = jnp.broadcast_to(onsite[x, y : y + 1], (size_z, size_z))
            column = jnp.sum(jnp.where(diagonal, row, 0.0), axis=1, keepdims=True)
            levels[x, y] = jnp.broadcast_to(column, (size_z, lanes))


def filter_coefficients(bound, cut_frac, coef):
    cut = cut_frac * bound
    half_width = (bound - cut) / 2.0
    center = (bound + cut) / 2.0
    sigma_one = half_width / (-bound - center)
    sigma = sigma_one
    coef[0] = center
    coef[1] = sigma / half_width
    for k in range(1, DEG):
        sigma_next = 1.0 / (2.0 / sigma_one - sigma)
        coef[2 * k] = 2.0 * sigma_next / half_width
        coef[2 * k + 1] = sigma * sigma_next
        sigma = sigma_next


def filter_kernel(dims, shape, sites, block, onsite, hopping, cut_frac, flat, image, gram, *scratch):
    size_x, size_y, size_z, lanes = shape
    per_half = HALO_REFS
    halves = []
    for half in range(HALVES):
        *refs, shifted, sems = scratch[half * per_half : (half + 1) * per_half]
        halves.append((tuple(refs), shifted, sems))
    (
        onsite_here, levels, input_sems,
        max_plane, max_column, max_sems, coef,
        local, total, plane_buf, column_buf, sums_sems,
    ) = scratch[HALVES * per_half :]
    enter(dims, True)
    copies = [pltpu.make_async_copy(onsite, onsite_here, input_sems.at[HALVES])]
    for half, (refs, _, _) in enumerate(halves):
        inside = refs[0].at[0, pl.ds(1, size_x), pl.ds(1, size_y)]
        source = block.at[:, :, :, pl.ds(lanes * half, lanes)]
        copies.append(pltpu.make_async_copy(source, inside, input_sems.at[half]))
    for copy in copies:
        copy.start()
    for refs, _, _ in halves:
        zero_border(dims, shape, 2, *refs[:4])
    copies[0].wait()
    place = place_of(dims)
    max_plane[place] = jnp.full((8, 128), jnp.max(jnp.abs(onsite_here[...])), jnp.float32)
    for copy, (refs, _, _) in zip(copies[1:], halves):
        copy.wait()
        field, face_out, edge_out, corner_out = refs[0], *refs[4:]

        @pl.loop(0, size_x)
        def _(x):
            for y in range(size_y):
                pack_column(shape, 0, x, y, field[0, x + 1, y + 1], face_out, edge_out)

        pack_corners(shape, 0, field, corner_out)
    spread(onsite_here, levels)
    entered(dims, True)
    for index, (refs, _, sems) in enumerate(halves):
        halo_send(dims, shape, 0, refs, sems)
        if index == 0:
            max_start(dims, None, max_plane, max_sems)
    max_middle(dims, max_plane, max_column, max_sems)
    for step in range(DEG):
        slot, after = step % 2, (step + 1) % 2
        for half, (refs, shifted, sems) in enumerate(halves):
            field, face, edge, corner, face_out, edge_out, corner_out = refs
            halo_wait(dims, shape, slot, refs, sems, True)
            shift_columns(shape, slot, field, face, edge, corner, shifted)
            if step == 0 and half == 0:
                reach = jnp.abs(hopping[0])
                for k in range(1, len(POSITIVE)):
                    reach = reach + jnp.abs(hopping[k])
                bound = max_end(dims, max_plane, max_column, max_sems) + 2.0 * reach
                filter_coefficients(bound, cut_frac[0], coef)
            if step:
                halo_wait(dims, shape, after, refs, sems, False)

            @pl.loop(0, size_x)
            def _(x):
                totals, centres = apply_rows(shape, slot, x, field, shifted, levels, hopping)
                for y in range(size_y):
                    value = totals[y] - coef[0] * centres[y]
                    if step == 0:
                        value = coef[1] * value
                    else:
                        older = field[after, x + 1, y + 1]
                        value = coef[2 * step] * value - coef[2 * step + 1] * older
                    if step == DEG - 1:
                        flat[site_rows(shape, x, y), lanes * half : lanes * (half + 1)] = value
                    field[after, x + 1, y + 1] = value
                    pack_column(shape, after, x, y, value, face_out, edge_out)

            pack_corners(shape, after, field, corner_out)
            halo_send(dims, shape, after, refs, sems)
    slot = DEG % 2
    sums = AllReduce(dims, local, total, plane_buf, column_buf, sums_sems)
    local[...] = product(flat[...], flat[...])
    sums.scatter()
    for refs, shifted, sems in halves:
        halo_wait(dims, shape, slot, refs, sems, True)
        shift_columns(shape, slot, *refs[:4], shifted)
    sums.across()
    for half, (refs, shifted, sems) in enumerate(halves):

        @pl.loop(0, size_x)
        def _(x):
            totals, _ = apply_rows(shape, slot, x, refs[0], shifted, levels, hopping)
            for y in range(size_y):
                image[site_rows(shape, x, y), lanes * half : lanes * (half + 1)] = totals[y]

    sums.gather()
    for refs, _, sems in halves:
        halo_wait(dims, shape, 1 - slot, refs, sems, False)
        halo_wait(dims, shape, slot, refs, sems, False)
    sums.finish()
    gram[...] = total[...] / sites


def site_rows(shape, x, y):
    _, size_y, size_z, _ = shape
    return pl.ds(pl.multiple_of((x * size_y + y) * size_z, size_z), size_z)


def product(left, right):
    return lax.dot_general(
        left,
        right,
        (((0,), (0,)), ((), ())),
        precision=HIGHEST,
        preferred_element_type=jnp.float32,
    )


def rotated(flat, factor):
    return lax.dot_general(
        flat,
        factor,
        (((1,), (1,)), ((), ())),
        precision=HIGHEST,
        preferred_element_type=jnp.float32,
    )


def rotate_kernel(
    dims, sites,
    flat, image, factor,
    first, gram, between,
    moved,
    local, total, plane_buf, column_buf, sums_sems,
    local_b, total_b, plane_buf_b, column_buf_b, sums_sems_b,
):
    enter(dims, False)
    sums = AllReduce(dims, local, total, plane_buf, column_buf, sums_sems)
    sums_b = AllReduce(dims, local_b, total_b, plane_buf_b, column_buf_b, sums_sems_b)
    first[...] = rotated(flat[...], factor[...])
    local[...] = product(first[...], first[...])
    entered(dims, False)
    sums.scatter()
    moved[...] = rotated(image[...], factor[...])
    local_b[...] = product(first[...], moved[...])
    sums_b.scatter()
    sums.across()
    sums_b.across()
    sums.gather()
    sums_b.gather()
    sums.finish()
    gram[...] = total[...] / sites
    sums_b.finish()
    between[...] = total_b[...] / sites


def call(kernel, inputs, scalars, outputs, scratch, ident, space=pltpu.VMEM):
    vmem = pl.BlockSpec(memory_space=pltpu.VMEM)
    smem = pl.BlockSpec(memory_space=pltpu.SMEM)
    return pl.pallas_call(
        kernel,
        out_shape=[jax.ShapeDtypeStruct(shape, jnp.float32) for shape in outputs],
        in_specs=[pl.BlockSpec(memory_space=space)] * len(inputs) + [smem] * len(scalars),
        out_specs=[vmem] * len(outputs),
        scratch_shapes=scratch,
        compiler_params=pltpu.CompilerParams(
            collective_id=ident, has_side_effects=True, vmem_limit_bytes=48 << 20
        ),
    )(*inputs, *scalars)


def factor_kernel(nb, gram, lower, inverse, work):
    size = gram.shape[0]
    tiles = size // 128
    groups = nb // 8
    lane = lax.broadcasted_iota(jnp.int32, (8, 128), 1)
    sub = lax.broadcasted_iota(jnp.int32, (8, 128), 0)
    for t in range(tiles):
        work[t] = gram[:, 128 * t : 128 * (t + 1)]
    for t in range(tiles):
        r = lax.broadcasted_iota(jnp.int32, (size, 128), 0)
        c = lax.broadcasted_iota(jnp.int32, (size, 128), 1) + 128 * t
        work[tiles + t] = jnp.where(r == c, 1.0, 0.0)

    def row(v, j):
        return jnp.broadcast_to(v[j % 8 : j % 8 + 1], (8, 128))

    for start in range(0, size, nb):
        stop = start + nb
        active = [t for t in range(tiles) if 128 * (t + 1) > start]
        active += [tiles + t for t in range(tiles) if 128 * t < stop]
        home = start // 128
        panel = {
            t: [work[t, start + 8 * g : start + 8 * g + 8] for g in range(groups)] for t in active
        }
        cols = [
            [
                jnp.broadcast_to(
                    panel[home][g][:, start % 128 + k : start % 128 + k + 1], (8, 128)
                )
                for g in range(groups)
            ]
            for k in range(nb)
        ]
        recip = [jnp.ones((8, 128), jnp.float32)] * groups
        pivots = [jnp.ones((8, 128), jnp.float32)] * groups
        for j in range(nb):
            home_group = j // 8
            pivot = row(cols[j][home_group], j)
            inv = 1.0 / pivot
            at = sub == j % 8
            recip[home_group] = jnp.where(at, inv, recip[home_group])
            pivots[home_group] = jnp.where(at, pivot, pivots[home_group])
            mult = [None] * groups
            for g in range(home_group, groups):
                mult[g] = cols[j][g] * inv
                if g == home_group:
                    mult[g] = jnp.where(sub > j % 8, mult[g], 0.0)
            for k in range(j + 1, nb):
                top = row(cols[k][home_group], j)
                for g in range(home_group, groups):
                    cols[k][g] = cols[k][g] - mult[g] * top
            for t in active:
                top = row(panel[t][home_group], j)
                for g in range(home_group, groups):
                    panel[t][g] = panel[t][g] - mult[g] * top
        if stop < size:
            full = {t: jnp.concatenate(panel[t], 0) if groups > 1 else panel[t][0] for t in active}
            recips = jnp.concatenate(recip, 0) if groups > 1 else recip[0]
            for u in range(tiles):
                low = max(128 * u, stop)
                if low >= 128 * (u + 1):
                    continue
                left = (full[u] * recips)[:, low - 128 * u :]
                for t in active:
                    if t < u:
                        continue
                    work[t, low : 128 * (u + 1)] -= lax.dot_general(
                        left, full[t], (((0,), (0,)), ((), ())),
                        precision=HIGHEST, preferred_element_type=jnp.float32)
        for g in range(groups):
            scale = 1.0 / jnp.sqrt(pivots[g])
            at = slice(start + 8 * g, start + 8 * g + 8)
            for t in range(tiles):
                if t in active:
                    keep = lane + 128 * t >= sub + (start + 8 * g)
                    work[t, at] = jnp.where(keep, panel[t][g] * scale, 0.0)
                else:
                    work[t, at] = jnp.zeros((8, 128), jnp.float32)
                if tiles + t in active:
                    inverse[at, 128 * t : 128 * t + 128] = panel[tiles + t][g] * scale
                else:
                    inverse[at, 128 * t : 128 * t + 128] = jnp.zeros((8, 128), jnp.float32)
    for t in range(tiles):
        lower[128 * t : 128 * t + 128, :] = work[t].T

def finish_kernel(nb, gram, first, between, states, projected, lower, inverse, work):
    factor_kernel(nb, gram, lower, inverse, work)
    states[...] = rotated(first[...], inverse[...])
    half = rotated(between[...], inverse[...])
    projected[...] = jnp.dot(
        inverse[...], half, precision=HIGHEST, preferred_element_type=jnp.float32
    )


def local_call(kernel, inputs, outputs, scratch):
    vmem = pl.BlockSpec(memory_space=pltpu.VMEM)
    return pl.pallas_call(
        kernel,
        out_shape=[jax.ShapeDtypeStruct(shape, jnp.float32) for shape in outputs],
        in_specs=[vmem] * len(inputs),
        out_specs=[vmem] * len(outputs),
        scratch_shapes=scratch,
        compiler_params=pltpu.CompilerParams(vmem_limit_bytes=32 << 20),
    )(*inputs)


def body(dims, block, onsite, hopping, cut_frac):
    shape = block.shape
    size_x, size_y, size_z, columns = shape
    count = size_x * size_y * size_z
    sites = count * dims[0] * dims[1] * dims[2]
    plane, column = dims[0] * dims[2], dims[1]
    sums = reduce_scratch(dims, columns)
    square = (columns, columns)
    work = pltpu.VMEM((2 * (columns // 128), columns, 128), jnp.float32)
    lanes = columns // HALVES
    part = (size_x, size_y, size_z, lanes)
    flat, image, gram_one = call(
        functools.partial(filter_kernel, dims, part, sites),
        [block, onsite],
        [hopping, cut_frac],
        [(count, columns), (count, columns), square],
        halo_scratch(part, 2) * HALVES
        + [
            pltpu.VMEM((size_x, size_y, size_z), jnp.float32),
            pltpu.VMEM(part, jnp.float32),
            pltpu.SemaphoreType.DMA((HALVES + 1,)),
            pltpu.VMEM((plane, 8, 128), jnp.float32),
            pltpu.VMEM((column, 8, 128), jnp.float32),
            pltpu.SemaphoreType.DMA((4,)),
            pltpu.VMEM((2 * DEG, 8, 128), jnp.float32),
        ]
        + sums,
        1,
        pltpu.HBM,
    )
    lower_one, inverse_one = local_call(
        functools.partial(factor_kernel, PANEL), [gram_one], [square, square], [work]
    )
    first, gram_two, between = call(
        functools.partial(rotate_kernel, dims, sites),
        [flat, image, inverse_one],
        [],
        [(count, columns), square, square],
        [pltpu.VMEM((count, columns), jnp.float32)] + sums + sums,
        2,
    )
    states, projected = local_call(
        functools.partial(finish_kernel, PANEL),
        [gram_two, first, between],
        [(count, columns), square],
        [pltpu.VMEM(square, jnp.float32), pltpu.VMEM(square, jnp.float32), work],
    )
    return (states.reshape(shape), projected, lower_one)


def solution(mesh):
    dims = (mesh.shape["gx"], mesh.shape["gy"], mesh.shape["gz"])
    return jax.shard_map(
        functools.partial(body, dims),
        mesh=mesh,
        in_specs=(P("gx", "gy", "gz", None), P("gx", "gy", "gz"), P(), P()),
        out_specs=(P("gx", "gy", "gz", None), P(), P()),
        check_vma=False,
    )
```

```python
import functools

import jax
import jax.numpy as jnp
from jax import lax
from jax.experimental import pallas as pl
from jax.experimental.pallas import tpu as pltpu
from jax.sharding import PartitionSpec as P

DEG = 4
PANEL = 16
NEAR_STEPS = 4
NEAR_LEFT = 1e-3
HALVES = 2
HALO_REFS = 9
MESH = pl.DeviceIdType.MESH
HIGHEST = lax.Precision.HIGHEST
AXES = ("gx", "gy", "gz")
OFFSETS = [
    (dx, dy, dz)
    for dx in (-1, 0, 1)
    for dy in (-1, 0, 1)
    for dz in (-1, 0, 1)
    if (dx, dy, dz) != (0, 0, 0)
]
POSITIVE = [offset for offset in OFFSETS if offset > (0, 0, 0)]


def hop_index(offset):
    return POSITIVE.index(max(offset, tuple(-d for d in offset)))


def plane_peer(dims, offset):
    size_x, _, size_z = dims
    place = lax.axis_index("gx") * size_z + lax.axis_index("gz")
    peer = lax.rem(place + offset, size_x * size_z)
    return peer, {"gx": peer // size_z, "gz": lax.rem(peer, size_z)}


def column_peer(dims, offset):
    peer = lax.rem(lax.axis_index("gy") + offset, dims[1])
    return peer, {"gy": peer}


def has_neighbour(dims, offset):
    valid = None
    for axis, size, step in zip(AXES, dims, offset):
        if step:
            place = lax.axis_index(axis)
            here = place < size - 1 if step > 0 else place > 0
            valid = here if valid is None else jnp.logical_and(valid, here)
    return valid


def neighbour(offset):
    return {axis: lax.axis_index(axis) + step for axis, step in zip(AXES, offset) if step}


def enter(dims, halo):
    barrier = pltpu.get_barrier_semaphore()

    @pl.loop(1, dims[0] * dims[2])
    def _(k):
        pl.semaphore_signal(barrier, inc=1, device_id=plane_peer(dims, k)[1], device_id_type=MESH)

    @pl.loop(1, dims[1])
    def _(k):
        pl.semaphore_signal(barrier, inc=1, device_id=column_peer(dims, k)[1], device_id_type=MESH)

    if halo:
        for offset in OFFSETS:

            @pl.when(has_neighbour(dims, offset))
            def _():
                pl.semaphore_signal(
                    barrier, inc=1, device_id=neighbour(offset), device_id_type=MESH
                )


def entered(dims, halo):
    count = dims[0] * dims[2] + dims[1] - 2
    if halo:
        boxes = 1
        for axis, size in zip(AXES, dims):
            place = lax.axis_index(axis)
            boxes = boxes * (3 - (place == 0).astype(jnp.int32) - (place == size - 1).astype(jnp.int32))
        count = count + boxes - 1
    pl.semaphore_wait(pltpu.get_barrier_semaphore(), count)


def wait_bytes(ref, sem):
    pltpu.make_async_copy(ref, ref, sem).wait()


def send(src, dst, send_sem, recv_sem, device):
    pltpu.make_async_remote_copy(
        src_ref=src,
        dst_ref=dst,
        send_sem=send_sem,
        recv_sem=recv_sem,
        device_id=device,
        device_id_type=MESH,
    ).start()


def place_of(dims):
    return lax.axis_index("gx") * dims[2] + lax.axis_index("gz")


class AllReduce:
    def __init__(self, dims, local, total, plane_buf, column_buf, sems):
        self.dims, self.local, self.total = dims, local, total
        self.plane_buf, self.column_buf, self.sems = plane_buf, column_buf, sems
        self.plane, self.column = dims[0] * dims[2], dims[1]
        self.rows = local.shape[0] // self.plane
        self.mine = pl.ds(pl.multiple_of(place_of(dims) * self.rows, self.rows), self.rows)

    def scatter(self):
        @pl.loop(1, self.plane)
        def _(k):
            peer, device = plane_peer(self.dims, k)
            theirs = pl.ds(pl.multiple_of(peer * self.rows, self.rows), self.rows)
            send(
                self.local.at[theirs], self.plane_buf.at[k - 1],
                self.sems.at[0], self.sems.at[1], device,
            )

    def across(self):
        level = lax.axis_index("gy")
        wait_bytes(self.plane_buf, self.sems.at[1])
        self.column_buf[level] = lax.fori_loop(
            0, self.plane - 1, lambda k, acc: acc + self.plane_buf[k], self.local[self.mine]
        )
        mine = self.column_buf.at[level]

        @pl.loop(1, self.column)
        def _(k):
            _, device = column_peer(self.dims, k)
            send(mine, mine, self.sems.at[2], self.sems.at[3], device)

    def gather(self):
        wait_bytes(self.column_buf.at[pl.ds(0, self.column - 1)], self.sems.at[3])
        part = self.column_buf[0]
        for k in range(1, self.column):
            part = part + self.column_buf[k]
        self.total[self.mine] = part
        mine = self.total.at[self.mine]

        @pl.loop(1, self.plane)
        def _(k):
            _, device = plane_peer(self.dims, k)
            send(mine, mine, self.sems.at[4], self.sems.at[5], device)

    def finish(self):
        others = self.total.at[pl.ds(0, (self.plane - 1) * self.rows)]
        wait_bytes(others, self.sems.at[5])
        wait_bytes(self.plane_buf, self.sems.at[0])
        wait_bytes(self.column_buf.at[pl.ds(0, self.column - 1)], self.sems.at[2])
        wait_bytes(others, self.sems.at[4])


def reduce_scratch(dims, size):
    plane, column = dims[0] * dims[2], dims[1]
    rows = size // plane
    return [
        pltpu.VMEM((size, size), jnp.float32),
        pltpu.VMEM((size, size), jnp.float32),
        pltpu.VMEM((plane - 1, rows, size), jnp.float32),
        pltpu.VMEM((column, rows, size), jnp.float32),
        pltpu.SemaphoreType.DMA((6,)),
    ]


def max_start(dims, value, plane_buf, sems):
    plane = dims[0] * dims[2]
    place = lax.axis_index("gx") * dims[2] + lax.axis_index("gz")

    @pl.loop(1, plane)
    def _(k):
        _, device = plane_peer(dims, k)
        send(plane_buf.at[place], plane_buf.at[place], sems.at[0], sems.at[1], device)


def max_middle(dims, plane_buf, column_buf, sems):
    plane, column = dims[0] * dims[2], dims[1]
    level = lax.axis_index("gy")
    wait_bytes(plane_buf.at[pl.ds(0, plane - 1)], sems.at[1])
    column_buf[level] = jnp.max(plane_buf[...], axis=0)

    @pl.loop(1, column)
    def _(k):
        _, device = column_peer(dims, k)
        send(column_buf.at[level], column_buf.at[level], sems.at[2], sems.at[3], device)


def max_end(dims, plane_buf, column_buf, sems):
    plane, column = dims[0] * dims[2], dims[1]
    wait_bytes(column_buf.at[pl.ds(0, column - 1)], sems.at[3])
    wait_bytes(plane_buf.at[pl.ds(0, plane - 1)], sems.at[0])
    wait_bytes(column_buf.at[pl.ds(0, column - 1)], sems.at[2])
    return jnp.max(column_buf[...], axis=0)


def halo_scratch(shape, slots):
    size_x, size_y, size_z, columns = shape
    f32 = jnp.float32
    return [
        pltpu.VMEM((slots, size_x + 2, size_y + 2, size_z, columns), f32),
        pltpu.VMEM((slots, 2, size_x + 2, size_y, columns), f32),
        pltpu.VMEM((slots, 2, 2, size_x, columns), f32),
        pltpu.VMEM((slots, 2, 2, 2, 8, columns), f32),
        pltpu.VMEM((slots, 2, size_x, size_y, columns), f32),
        pltpu.VMEM((slots, 2, 2, size_x, columns), f32),
        pltpu.VMEM((slots, 2, 2, 2, 8, columns), f32),
        pltpu.VMEM((2, size_x + 2, size_y + 2, size_z, columns), f32),
        pltpu.SemaphoreType.DMA((slots, 2, len(OFFSETS))),
    ]


def halo_parts(shape, slot, offset, field, face, edge, corner, face_out, edge_out, corner_out):
    size_x, size_y, _, _ = shape
    sx, sy, sz = offset
    low = {1: 0, -1: 1}

    def ends(step, size):
        if step == 0:
            return pl.ds(1, size), pl.ds(1, size)
        return (size, 0) if step > 0 else (1, size + 1)

    from_x, to_x = ends(sx, size_x)
    from_y, to_y = ends(sy, size_y)
    if sz == 0:
        return field.at[slot, from_x, from_y], field.at[slot, to_x, to_y]
    top = 1 if sz > 0 else 0
    if sy == 0:
        source = pl.ds(0, size_x) if sx == 0 else from_x - 1
        return face_out.at[slot, top, source], face.at[slot, 1 - top, to_x]
    far = 1 if sy > 0 else 0
    if sx == 0:
        return edge_out.at[slot, top, far], edge.at[slot, 1 - top, 1 - far]
    right = 1 if sx > 0 else 0
    return (
        corner_out.at[slot, top, far, right],
        corner.at[slot, 1 - top, 1 - far, 1 - right],
    )


def zero_border(dims, shape, slots, field, face, edge, corner):
    size_x, size_y, size_z, columns = shape
    for slot in range(slots):
        for side in (0, 1):
            step = 1 if side else -1
            row = size_x + 1 if side else 0

            @pl.when(jnp.logical_not(has_neighbour(dims, (step, 0, 0))))
            def _():
                field[slot, row] = jnp.zeros((size_y + 2, size_z, columns), jnp.float32)
                for top in (0, 1):
                    face[slot, top, row] = jnp.zeros((size_y, columns), jnp.float32)
                    for far in (0, 1):
                        corner[slot, top, far, side] = jnp.zeros((8, columns), jnp.float32)

            row_y = size_y + 1 if side else 0

            @pl.when(jnp.logical_not(has_neighbour(dims, (0, step, 0))))
            def _():
                field[slot, :, row_y] = jnp.zeros((size_x + 2, size_z, columns), jnp.float32)
                for top in (0, 1):
                    edge[slot, top, side] = jnp.zeros((size_x, columns), jnp.float32)
                    for right in (0, 1):
                        corner[slot, top, side, right] = jnp.zeros((8, columns), jnp.float32)

            @pl.when(jnp.logical_not(has_neighbour(dims, (0, 0, step))))
            def _():
                face[slot, side] = jnp.zeros((size_x + 2, size_y, columns), jnp.float32)
                edge[slot, side] = jnp.zeros((2, size_x, columns), jnp.float32)
                corner[slot, side] = jnp.zeros((2, 2, 8, columns), jnp.float32)


def pack_column(shape, slot, x, y, value, face_out, edge_out):
    size_y, size_z = shape[1], shape[2]
    for top, z in ((0, 0), (1, size_z - 1)):
        row = value[z : z + 1]
        face_out[slot, top, x, y : y + 1] = row
        if y in (0, size_y - 1):
            edge_out[slot, top, 1 if y else 0, pl.ds(x, 1)] = row


def pack_corners(shape, slot, field, corner_out):
    size_x, size_y, size_z, columns = shape
    for top in (0, 1):
        for far in (0, 1):
            for right in (0, 1):
                z = (size_z - 1) * top
                corner_out[slot, top, far, right] = jnp.broadcast_to(
                    field[slot, size_x if right else 1, size_y if far else 1, z : z + 1],
                    (8, columns),
                )


def halo_send(dims, shape, slot, refs, sems):
    for index, offset in enumerate(OFFSETS):

        @pl.when(has_neighbour(dims, offset))
        def _():
            src, dst = halo_parts(shape, slot, offset, *refs)
            send(src, dst, sems.at[slot, 0, index], sems.at[slot, 1, index], neighbour(offset))


def halo_wait(dims, shape, slot, refs, sems, received):
    for index, offset in enumerate(OFFSETS):
        from_there = tuple(-step for step in offset)

        @pl.when(has_neighbour(dims, from_there if received else offset))
        def _():
            src, dst = halo_parts(shape, slot, offset, *refs)
            if received:
                wait_bytes(dst, sems.at[slot, 1, index])
            else:
                wait_bytes(src, sems.at[slot, 0, index])


def shift_columns(shape, slot, field, face, edge, corner, shifted):
    size_x, size_y, size_z, columns = shape
    place = lax.broadcasted_iota(jnp.int32, (size_z, columns), 0)

    def put(x, y, below, above):
        value = field[slot, x, y]
        shifted[0, x, y] = jnp.where(place == 0, below, pltpu.roll(value, 1, 0))
        shifted[1, x, y] = jnp.where(place == size_z - 1, above, pltpu.roll(value, size_z - 1, 0))

    @pl.loop(0, size_x + 2)
    def _(x):
        for y in range(size_y):
            put(x, y + 1, face[slot, 0, x, y : y + 1], face[slot, 1, x, y : y + 1])

    for far in (0, 1):
        y = size_y + 1 if far else 0

        @pl.loop(0, size_x)
        def _(x):
            put(x + 1, y, edge[slot, 0, far, pl.ds(x, 1)], edge[slot, 1, far, pl.ds(x, 1)])

        for right in (0, 1):
            x = size_x + 1 if right else 0
            put(x, y, corner[slot, 0, far, right], corner[slot, 1, far, right])


def apply_rows(shape, slot, x, field, shifted, onsite, hopping):
    size_y = shape[1]
    totals = [None] * size_y
    centres = [None] * size_y
    for dx in (-1, 0, 1):
        for y in range(-1, size_y + 1):
            for dz in (-1, 0, 1):
                if dz == 0:
                    value = field[slot, x + 1 + dx, y + 1]
                else:
                    value = shifted[0 if dz < 0 else 1, x + 1 + dx, y + 1]
                for dy in (-1, 0, 1):
                    target = y - dy
                    if not 0 <= target < size_y:
                        continue
                    if (dx, dy, dz) == (0, 0, 0):
                        centres[target] = value
                        level = onsite[x, target]
                        term = level * value
                    else:
                        term = hopping[hop_index((dx, dy, dz))] * value
                    totals[target] = term if totals[target] is None else totals[target] + term
    return totals, centres


def spread(onsite, levels):
    size_x, size_y, size_z, lanes = levels.shape
    diagonal = lax.broadcasted_iota(jnp.int32, (size_z, size_z), 0) == lax.broadcasted_iota(
        jnp.int32, (size_z, size_z), 1
    )

    @pl.loop(0, size_x)
    def _(x):
        for y in range(size_y):
            row = jnp.broadcast_to(onsite[x, y : y + 1], (size_z, size_z))
            column = jnp.sum(jnp.where(diagonal, row, 0.0), axis=1, keepdims=True)
            levels[x, y] = jnp.broadcast_to(column, (size_z, lanes))


def filter_coefficients(bound, cut_frac, coef):
    cut = cut_frac * bound
    half_width = (bound - cut) / 2.0
    center = (bound + cut) / 2.0
    sigma_one = half_width / (-bound - center)
    sigma = sigma_one
    coef[0] = center
    coef[1] = sigma / half_width
    for k in range(1, DEG):
        sigma_next = 1.0 / (2.0 / sigma_one - sigma)
        coef[2 * k] = 2.0 * sigma_next / half_width
        coef[2 * k + 1] = sigma * sigma_next
        sigma = sigma_next


def filter_kernel(dims, shape, sites, block, onsite, hopping, cut_frac, flat, image, gram, *scratch):
    size_x, size_y, size_z, lanes = shape
    per_half = HALO_REFS
    halves = []
    for half in range(HALVES):
        *refs, shifted, sems = scratch[half * per_half : (half + 1) * per_half]
        halves.append((tuple(refs), shifted, sems))
    (
        onsite_here, levels, input_sems,
        max_plane, max_column, max_sems, coef,
        local, total, plane_buf, column_buf, sums_sems,
    ) = scratch[HALVES * per_half :]
    enter(dims, True)
    copies = [pltpu.make_async_copy(onsite, onsite_here, input_sems.at[HALVES])]
    for half, (refs, _, _) in enumerate(halves):
        inside = refs[0].at[0, pl.ds(1, size_x), pl.ds(1, size_y)]
        source = block.at[:, :, :, pl.ds(lanes * half, lanes)]
        copies.append(pltpu.make_async_copy(source, inside, input_sems.at[half]))
    for copy in copies:
        copy.start()
    for refs, _, _ in halves:
        zero_border(dims, shape, 2, *refs[:4])
    copies[0].wait()
    place = place_of(dims)
    max_plane[place] = jnp.full((8, 128), jnp.max(jnp.abs(onsite_here[...])), jnp.float32)
    for copy, (refs, _, _) in zip(copies[1:], halves):
        copy.wait()
        field, face_out, edge_out, corner_out = refs[0], *refs[4:]

        @pl.loop(0, size_x)
        def _(x):
            for y in range(size_y):
                pack_column(shape, 0, x, y, field[0, x + 1, y + 1], face_out, edge_out)

        pack_corners(shape, 0, field, corner_out)
    spread(onsite_here, levels)
    entered(dims, True)
    for index, (refs, _, sems) in enumerate(halves):
        halo_send(dims, shape, 0, refs, sems)
        if index == 0:
            max_start(dims, None, max_plane, max_sems)
    max_middle(dims, max_plane, max_column, max_sems)
    for step in range(DEG):
        slot, after = step % 2, (step + 1) % 2
        for half, (refs, shifted, sems) in enumerate(halves):
            field, face, edge, corner, face_out, edge_out, corner_out = refs
            halo_wait(dims, shape, slot, refs, sems, True)
            shift_columns(shape, slot, field, face, edge, corner, shifted)
            if step == 0 and half == 0:
                reach = jnp.abs(hopping[0])
                for k in range(1, len(POSITIVE)):
                    reach = reach + jnp.abs(hopping[k])
                bound = max_end(dims, max_plane, max_column, max_sems) + 2.0 * reach
                filter_coefficients(bound, cut_frac[0], coef)
            if step:
                halo_wait(dims, shape, after, refs, sems, False)

            @pl.loop(0, size_x)
            def _(x):
                totals, centres = apply_rows(shape, slot, x, field, shifted, levels, hopping)
                for y in range(size_y):
                    value = totals[y] - coef[0] * centres[y]
                    if step == 0:
                        value = coef[1] * value
                    else:
                        older = field[after, x + 1, y + 1]
                        value = coef[2 * step] * value - coef[2 * step + 1] * older
                    if step == DEG - 1:
                        flat[site_rows(shape, x, y), lanes * half : lanes * (half + 1)] = value
                    field[after, x + 1, y + 1] = value
                    pack_column(shape, after, x, y, value, face_out, edge_out)

            pack_corners(shape, after, field, corner_out)
            halo_send(dims, shape, after, refs, sems)
    slot = DEG % 2
    sums = AllReduce(dims, local, total, plane_buf, column_buf, sums_sems)
    local[...] = product(flat[...], flat[...])
    sums.scatter()
    for refs, shifted, sems in halves:
        halo_wait(dims, shape, slot, refs, sems, True)
        shift_columns(shape, slot, *refs[:4], shifted)
    sums.across()
    for half, (refs, shifted, sems) in enumerate(halves):

        @pl.loop(0, size_x)
        def _(x):
            totals, _ = apply_rows(shape, slot, x, refs[0], shifted, levels, hopping)
            for y in range(size_y):
                image[site_rows(shape, x, y), lanes * half : lanes * (half + 1)] = totals[y]

    sums.gather()
    for refs, _, sems in halves:
        halo_wait(dims, shape, 1 - slot, refs, sems, False)
        halo_wait(dims, shape, slot, refs, sems, False)
    sums.finish()
    gram[...] = total[...] / sites


def site_rows(shape, x, y):
    _, size_y, size_z, _ = shape
    return pl.ds(pl.multiple_of((x * size_y + y) * size_z, size_z), size_z)


def product(left, right):
    return lax.dot_general(
        left,
        right,
        (((0,), (0,)), ((), ())),
        precision=HIGHEST,
        preferred_element_type=jnp.float32,
    )


def rotated(flat, factor):
    return lax.dot_general(
        flat,
        factor,
        (((1,), (1,)), ((), ())),
        precision=HIGHEST,
        preferred_element_type=jnp.float32,
    )


def rotate_kernel(
    dims, sites,
    flat, image, gram_one,
    first, gram, between, lower,
    factor, work, moved,
    local, total, plane_buf, column_buf, sums_sems,
    local_b, total_b, plane_buf_b, column_buf_b, sums_sems_b,
):
    enter(dims, False)
    sums = AllReduce(dims, local, total, plane_buf, column_buf, sums_sems)
    sums_b = AllReduce(dims, local_b, total_b, plane_buf_b, column_buf_b, sums_sems_b)
    factor_kernel(PANEL, gram_one, lower, factor, work)
    first[...] = rotated(flat[...], factor[...])
    local[...] = product(first[...], first[...])
    entered(dims, False)
    sums.scatter()
    moved[...] = rotated(image[...], factor[...])
    local_b[...] = product(first[...], moved[...])
    sums_b.scatter()
    sums.across()
    sums_b.across()
    sums.gather()
    sums_b.gather()
    sums.finish()
    gram[...] = total[...] / sites
    sums_b.finish()
    between[...] = total_b[...] / sites


def call(kernel, inputs, scalars, outputs, scratch, ident, space=pltpu.VMEM):
    vmem = pl.BlockSpec(memory_space=pltpu.VMEM)
    smem = pl.BlockSpec(memory_space=pltpu.SMEM)
    return pl.pallas_call(
        kernel,
        out_shape=[jax.ShapeDtypeStruct(shape, jnp.float32) for shape in outputs],
        in_specs=[pl.BlockSpec(memory_space=space)] * len(inputs) + [smem] * len(scalars),
        out_specs=[vmem] * len(outputs),
        scratch_shapes=scratch,
        compiler_params=pltpu.CompilerParams(
            collective_id=ident, has_side_effects=True, vmem_limit_bytes=48 << 20
        ),
    )(*inputs, *scalars)


def factor_kernel(nb, gram, lower, inverse, work):
    size = gram.shape[0]
    tiles = size // 128
    groups = nb // 8
    lane = lax.broadcasted_iota(jnp.int32, (8, 128), 1)
    sub = lax.broadcasted_iota(jnp.int32, (8, 128), 0)
    for t in range(tiles):
        work[t] = gram[:, 128 * t : 128 * (t + 1)]
    for t in range(tiles):
        r = lax.broadcasted_iota(jnp.int32, (size, 128), 0)
        c = lax.broadcasted_iota(jnp.int32, (size, 128), 1) + 128 * t
        work[tiles + t] = jnp.where(r == c, 1.0, 0.0)

    def row(v, j):
        return jnp.broadcast_to(v[j % 8 : j % 8 + 1], (8, 128))

    for start in range(0, size, nb):
        stop = start + nb
        active = [t for t in range(tiles) if 128 * (t + 1) > start]
        active += [tiles + t for t in range(tiles) if 128 * t < stop]
        home = start // 128
        panel = {
            t: [work[t, start + 8 * g : start + 8 * g + 8] for g in range(groups)] for t in active
        }
        cols = [
            [
                jnp.broadcast_to(
                    panel[home][g][:, start % 128 + k : start % 128 + k + 1], (8, 128)
                )
                for g in range(groups)
            ]
            for k in range(nb)
        ]
        recip = [jnp.ones((8, 128), jnp.float32)] * groups
        pivots = [jnp.ones((8, 128), jnp.float32)] * groups
        for j in range(nb):
            home_group = j // 8
            pivot = row(cols[j][home_group], j)
            inv = 1.0 / pivot
            at = sub == j % 8
            recip[home_group] = jnp.where(at, inv, recip[home_group])
            pivots[home_group] = jnp.where(at, pivot, pivots[home_group])
            mult = [None] * groups
            for g in range(home_group, groups):
                mult[g] = cols[j][g] * inv
                if g == home_group:
                    mult[g] = jnp.where(sub > j % 8, mult[g], 0.0)
            for k in range(j + 1, nb):
                top = row(cols[k][home_group], j)
                for g in range(home_group, groups):
                    cols[k][g] = cols[k][g] - mult[g] * top
            for t in active:
                top = row(panel[t][home_group], j)
                for g in range(home_group, groups):
                    panel[t][g] = panel[t][g] - mult[g] * top
        if stop < size:
            full = {t: jnp.concatenate(panel[t], 0) if groups > 1 else panel[t][0] for t in active}
            recips = jnp.concatenate(recip, 0) if groups > 1 else recip[0]
            for u in range(tiles):
                low = max(128 * u, stop)
                if low >= 128 * (u + 1):
                    continue
                left = (full[u] * recips)[:, low - 128 * u :]
                for t in active:
                    if t < u:
                        continue
                    work[t, low : 128 * (u + 1)] -= lax.dot_general(
                        left, full[t], (((0,), (0,)), ((), ())),
                        precision=HIGHEST, preferred_element_type=jnp.float32)
        for g in range(groups):
            scale = 1.0 / jnp.sqrt(pivots[g])
            at = slice(start + 8 * g, start + 8 * g + 8)
            for t in range(tiles):
                if t in active:
                    keep = lane + 128 * t >= sub + (start + 8 * g)
                    work[t, at] = jnp.where(keep, panel[t][g] * scale, 0.0)
                else:
                    work[t, at] = jnp.zeros((8, 128), jnp.float32)
                if tiles + t in active:
                    inverse[at, 128 * t : 128 * t + 128] = panel[tiles + t][g] * scale
                else:
                    inverse[at, 128 * t : 128 * t + 128] = jnp.zeros((8, 128), jnp.float32)
    for t in range(tiles):
        lower[128 * t : 128 * t + 128, :] = work[t].T

def near_identity_kernel(gram, inverse):
    size = gram.shape[0]
    row = lax.broadcasted_iota(jnp.int32, (size, size), 0)
    col = lax.broadcasted_iota(jnp.int32, (size, size), 1)
    ident = jnp.where(row == col, 1.0, 0.0)
    weight = jnp.where(row > col, 1.0, 0.5 * ident)

    def times(left, right, across):
        return lax.dot_general(
            left, right, (((1,), (across,)), ((), ())),
            precision=HIGHEST, preferred_element_type=jnp.float32,
        )

    error = gram[...] - ident
    shift = None
    for step in range(NEAR_STEPS):
        low = weight * error
        shift = low if shift is None else shift + low - times(low, shift, 0)
        if step < NEAR_STEPS - 1:
            cross = times(low, error, 0)
            error = times(low + cross, low, 1) - cross - cross.T
    inverse[...] = ident - shift
    return jnp.sum(error * error)


def finish_kernel(
    nb, gram, first, between, lower_one, states, projected, factor, lower, inverse, work
):
    factor[...] = lower_one[...]
    left = near_identity_kernel(gram, inverse)

    @pl.when(jnp.logical_not(left < NEAR_LEFT * NEAR_LEFT))
    def _():
        factor_kernel(nb, gram, lower, inverse, work)

    states[...] = rotated(first[...], inverse[...])
    half = rotated(between[...], inverse[...])
    projected[...] = jnp.dot(
        inverse[...], half, precision=HIGHEST, preferred_element_type=jnp.float32
    )


def local_call(kernel, inputs, outputs, scratch):
    vmem = pl.BlockSpec(memory_space=pltpu.VMEM)
    return pl.pallas_call(
        kernel,
        out_shape=[jax.ShapeDtypeStruct(shape, jnp.float32) for shape in outputs],
        in_specs=[vmem] * len(inputs),
        out_specs=[vmem] * len(outputs),
        scratch_shapes=scratch,
        compiler_params=pltpu.CompilerParams(vmem_limit_bytes=32 << 20),
    )(*inputs)


def body(dims, block, onsite, hopping, cut_frac):
    shape = block.shape
    size_x, size_y, size_z, columns = shape
    count = size_x * size_y * size_z
    sites = count * dims[0] * dims[1] * dims[2]
    plane, column = dims[0] * dims[2], dims[1]
    sums = reduce_scratch(dims, columns)
    square = (columns, columns)
    work = pltpu.VMEM((2 * (columns // 128), columns, 128), jnp.float32)
    lanes = columns // HALVES
    part = (size_x, size_y, size_z, lanes)
    flat, image, gram_one = call(
        functools.partial(filter_kernel, dims, part, sites),
        [block, onsite],
        [hopping, cut_frac],
        [(count, columns), (count, columns), square],
        halo_scratch(part, 2) * HALVES
        + [
            pltpu.VMEM((size_x, size_y, size_z), jnp.float32),
            pltpu.VMEM(part, jnp.float32),
            pltpu.SemaphoreType.DMA((HALVES + 1,)),
            pltpu.VMEM((plane, 8, 128), jnp.float32),
            pltpu.VMEM((column, 8, 128), jnp.float32),
            pltpu.SemaphoreType.DMA((4,)),
            pltpu.VMEM((2 * DEG, 8, 128), jnp.float32),
        ]
        + sums,
        1,
        pltpu.HBM,
    )
    first, gram_two, between, lower_one = call(
        functools.partial(rotate_kernel, dims, sites),
        [flat, image, gram_one],
        [],
        [(count, columns), square, square, square],
        [pltpu.VMEM(square, jnp.float32), work, pltpu.VMEM((count, columns), jnp.float32)]
        + sums
        + sums,
        2,
    )
    states, projected, factor = local_call(
        functools.partial(finish_kernel, PANEL),
        [gram_two, first, between, lower_one],
        [(count, columns), square, square],
        [pltpu.VMEM(square, jnp.float32), pltpu.VMEM(square, jnp.float32), work],
    )
    return (states.reshape(shape), projected, factor)


def solution(mesh):
    dims = (mesh.shape["gx"], mesh.shape["gy"], mesh.shape["gz"])
    return jax.shard_map(
        functools.partial(body, dims),
        mesh=mesh,
        in_specs=(P("gx", "gy", "gz", None), P("gx", "gy", "gz"), P(), P()),
        out_specs=(P("gx", "gy", "gz", None), P(), P()),
        check_vma=False,
    )
```

```python
import functools

import jax
import jax.numpy as jnp
from jax import lax
from jax.experimental import pallas as pl
from jax.experimental.pallas import tpu as pltpu
from jax.sharding import PartitionSpec as P

DEG = 4
PANEL = 16
NEAR_STEPS = 4
NEAR_LEFT = 1e-3
HALVES = 2
HALO_REFS = 9
MESH = pl.DeviceIdType.MESH
HIGHEST = lax.Precision.HIGHEST
AXES = ("gx", "gy", "gz")
OFFSETS = [
    (dx, dy, dz)
    for dx in (-1, 0, 1)
    for dy in (-1, 0, 1)
    for dz in (-1, 0, 1)
    if (dx, dy, dz) != (0, 0, 0)
]
POSITIVE = [offset for offset in OFFSETS if offset > (0, 0, 0)]


def hop_index(offset):
    return POSITIVE.index(max(offset, tuple(-d for d in offset)))


def plane_peer(dims, offset):
    size_x, _, size_z = dims
    place = lax.axis_index("gx") * size_z + lax.axis_index("gz")
    peer = lax.rem(place + offset, size_x * size_z)
    return peer, {"gx": peer // size_z, "gz": lax.rem(peer, size_z)}


def column_peer(dims, offset):
    peer = lax.rem(lax.axis_index("gy") + offset, dims[1])
    return peer, {"gy": peer}


def has_neighbour(dims, offset):
    valid = None
    for axis, size, step in zip(AXES, dims, offset):
        if step:
            place = lax.axis_index(axis)
            here = place < size - 1 if step > 0 else place > 0
            valid = here if valid is None else jnp.logical_and(valid, here)
    return valid


def neighbour(offset):
    return {axis: lax.axis_index(axis) + step for axis, step in zip(AXES, offset) if step}


def enter(dims, halo):
    barrier = pltpu.get_barrier_semaphore()

    @pl.loop(1, dims[0] * dims[2])
    def _(k):
        pl.semaphore_signal(barrier, inc=1, device_id=plane_peer(dims, k)[1], device_id_type=MESH)

    @pl.loop(1, dims[1])
    def _(k):
        pl.semaphore_signal(barrier, inc=1, device_id=column_peer(dims, k)[1], device_id_type=MESH)

    if halo:
        for offset in OFFSETS:

            @pl.when(has_neighbour(dims, offset))
            def _():
                pl.semaphore_signal(
                    barrier, inc=1, device_id=neighbour(offset), device_id_type=MESH
                )


def entered(dims, halo):
    count = dims[0] * dims[2] + dims[1] - 2
    if halo:
        boxes = 1
        for axis, size in zip(AXES, dims):
            place = lax.axis_index(axis)
            boxes = boxes * (3 - (place == 0).astype(jnp.int32) - (place == size - 1).astype(jnp.int32))
        count = count + boxes - 1
    pl.semaphore_wait(pltpu.get_barrier_semaphore(), count)


def wait_bytes(ref, sem):
    pltpu.make_async_copy(ref, ref, sem).wait()


def send(src, dst, send_sem, recv_sem, device):
    pltpu.make_async_remote_copy(
        src_ref=src,
        dst_ref=dst,
        send_sem=send_sem,
        recv_sem=recv_sem,
        device_id=device,
        device_id_type=MESH,
    ).start()


def place_of(dims):
    return lax.axis_index("gx") * dims[2] + lax.axis_index("gz")


class AllReduce:
    def __init__(self, dims, local, total, plane_buf, column_buf, sems):
        self.dims, self.local, self.total = dims, local, total
        self.plane_buf, self.column_buf, self.sems = plane_buf, column_buf, sems
        self.plane, self.column = dims[0] * dims[2], dims[1]
        self.rows = local.shape[0] // self.plane
        self.mine = pl.ds(pl.multiple_of(place_of(dims) * self.rows, self.rows), self.rows)

    def scatter(self):
        @pl.loop(1, self.plane)
        def _(k):
            peer, device = plane_peer(self.dims, k)
            theirs = pl.ds(pl.multiple_of(peer * self.rows, self.rows), self.rows)
            send(
                self.local.at[theirs], self.plane_buf.at[k - 1],
                self.sems.at[0], self.sems.at[1], device,
            )

    def across(self):
        level = lax.axis_index("gy")
        wait_bytes(self.plane_buf, self.sems.at[1])
        self.column_buf[level] = lax.fori_loop(
            0, self.plane - 1, lambda k, acc: acc + self.plane_buf[k], self.local[self.mine]
        )
        mine = self.column_buf.at[level]

        @pl.loop(1, self.column)
        def _(k):
            _, device = column_peer(self.dims, k)
            send(mine, mine, self.sems.at[2], self.sems.at[3], device)

    def gather(self):
        wait_bytes(self.column_buf.at[pl.ds(0, self.column - 1)], self.sems.at[3])
        part = self.column_buf[0]
        for k in range(1, self.column):
            part = part + self.column_buf[k]
        self.total[self.mine] = part
        mine = self.total.at[self.mine]

        @pl.loop(1, self.plane)
        def _(k):
            _, device = plane_peer(self.dims, k)
            send(mine, mine, self.sems.at[4], self.sems.at[5], device)

    def finish(self):
        others = self.total.at[pl.ds(0, (self.plane - 1) * self.rows)]
        wait_bytes(others, self.sems.at[5])
        wait_bytes(self.plane_buf, self.sems.at[0])
        wait_bytes(self.column_buf.at[pl.ds(0, self.column - 1)], self.sems.at[2])
        wait_bytes(others, self.sems.at[4])


def reduce_scratch(dims, size):
    plane, column = dims[0] * dims[2], dims[1]
    rows = size // plane
    return [
        pltpu.VMEM((size, size), jnp.float32),
        pltpu.VMEM((size, size), jnp.float32),
        pltpu.VMEM((plane - 1, rows, size), jnp.float32),
        pltpu.VMEM((column, rows, size), jnp.float32),
        pltpu.SemaphoreType.DMA((6,)),
    ]


def max_start(dims, value, plane_buf, sems):
    plane = dims[0] * dims[2]
    place = lax.axis_index("gx") * dims[2] + lax.axis_index("gz")

    @pl.loop(1, plane)
    def _(k):
        _, device = plane_peer(dims, k)
        send(plane_buf.at[place], plane_buf.at[place], sems.at[0], sems.at[1], device)


def max_middle(dims, plane_buf, column_buf, sems):
    plane, column = dims[0] * dims[2], dims[1]
    level = lax.axis_index("gy")
    wait_bytes(plane_buf.at[pl.ds(0, plane - 1)], sems.at[1])
    column_buf[level] = jnp.max(plane_buf[...], axis=0)

    @pl.loop(1, column)
    def _(k):
        _, device = column_peer(dims, k)
        send(column_buf.at[level], column_buf.at[level], sems.at[2], sems.at[3], device)


def max_end(dims, plane_buf, column_buf, sems):
    plane, column = dims[0] * dims[2], dims[1]
    wait_bytes(column_buf.at[pl.ds(0, column - 1)], sems.at[3])
    wait_bytes(plane_buf.at[pl.ds(0, plane - 1)], sems.at[0])
    wait_bytes(column_buf.at[pl.ds(0, column - 1)], sems.at[2])
    return jnp.max(column_buf[...], axis=0)


def halo_scratch(shape, slots):
    size_x, size_y, size_z, columns = shape
    f32 = jnp.float32
    return [
        pltpu.VMEM((slots, size_x + 2, size_y + 2, size_z, columns), f32),
        pltpu.VMEM((slots, 2, size_x + 2, size_y, columns), f32),
        pltpu.VMEM((slots, 2, 2, size_x, columns), f32),
        pltpu.VMEM((slots, 2, 2, 2, 8, columns), f32),
        pltpu.VMEM((slots, 2, size_x, size_y, columns), f32),
        pltpu.VMEM((slots, 2, 2, size_x, columns), f32),
        pltpu.VMEM((slots, 2, 2, 2, 8, columns), f32),
        pltpu.VMEM((2, size_x + 2, size_y + 2, size_z, columns), f32),
        pltpu.SemaphoreType.DMA((slots, 2, len(OFFSETS))),
    ]


def halo_parts(shape, slot, offset, field, face, edge, corner, face_out, edge_out, corner_out):
    size_x, size_y, _, _ = shape
    sx, sy, sz = offset
    low = {1: 0, -1: 1}

    def ends(step, size):
        if step == 0:
            return pl.ds(1, size), pl.ds(1, size)
        return (size, 0) if step > 0 else (1, size + 1)

    from_x, to_x = ends(sx, size_x)
    from_y, to_y = ends(sy, size_y)
    if sz == 0:
        return field.at[slot, from_x, from_y], field.at[slot, to_x, to_y]
    top = 1 if sz > 0 else 0
    if sy == 0:
        source = pl.ds(0, size_x) if sx == 0 else from_x - 1
        return face_out.at[slot, top, source], face.at[slot, 1 - top, to_x]
    far = 1 if sy > 0 else 0
    if sx == 0:
        return edge_out.at[slot, top, far], edge.at[slot, 1 - top, 1 - far]
    right = 1 if sx > 0 else 0
    return (
        corner_out.at[slot, top, far, right],
        corner.at[slot, 1 - top, 1 - far, 1 - right],
    )


def zero_border(dims, shape, slots, field, face, edge, corner):
    size_x, size_y, size_z, columns = shape
    for slot in range(slots):
        for side in (0, 1):
            step = 1 if side else -1
            row = size_x + 1 if side else 0

            @pl.when(jnp.logical_not(has_neighbour(dims, (step, 0, 0))))
            def _():
                field[slot, row] = jnp.zeros((size_y + 2, size_z, columns), jnp.float32)
                for top in (0, 1):
                    face[slot, top, row] = jnp.zeros((size_y, columns), jnp.float32)
                    for far in (0, 1):
                        corner[slot, top, far, side] = jnp.zeros((8, columns), jnp.float32)

            row_y = size_y + 1 if side else 0

            @pl.when(jnp.logical_not(has_neighbour(dims, (0, step, 0))))
            def _():
                field[slot, :, row_y] = jnp.zeros((size_x + 2, size_z, columns), jnp.float32)
                for top in (0, 1):
                    edge[slot, top, side] = jnp.zeros((size_x, columns), jnp.float32)
                    for right in (0, 1):
                        corner[slot, top, side, right] = jnp.zeros((8, columns), jnp.float32)

            @pl.when(jnp.logical_not(has_neighbour(dims, (0, 0, step))))
            def _():
                face[slot, side] = jnp.zeros((size_x + 2, size_y, columns), jnp.float32)
                edge[slot, side] = jnp.zeros((2, size_x, columns), jnp.float32)
                corner[slot, side] = jnp.zeros((2, 2, 8, columns), jnp.float32)


def pack_column(shape, slot, x, y, value, face_out, edge_out):
    size_y, size_z = shape[1], shape[2]
    for top, z in ((0, 0), (1, size_z - 1)):
        row = value[z : z + 1]
        face_out[slot, top, x, y : y + 1] = row
        if y in (0, size_y - 1):
            edge_out[slot, top, 1 if y else 0, pl.ds(x, 1)] = row


def pack_corners(shape, slot, field, corner_out):
    size_x, size_y, size_z, columns = shape
    for top in (0, 1):
        for far in (0, 1):
            for right in (0, 1):
                z = (size_z - 1) * top
                corner_out[slot, top, far, right] = jnp.broadcast_to(
                    field[slot, size_x if right else 1, size_y if far else 1, z : z + 1],
                    (8, columns),
                )


def halo_send(dims, shape, slot, refs, sems):
    for index, offset in enumerate(OFFSETS):

        @pl.when(has_neighbour(dims, offset))
        def _():
            src, dst = halo_parts(shape, slot, offset, *refs)
            send(src, dst, sems.at[slot, 0, index], sems.at[slot, 1, index], neighbour(offset))


def halo_wait(dims, shape, slot, refs, sems, received):
    for index, offset in enumerate(OFFSETS):
        from_there = tuple(-step for step in offset)

        @pl.when(has_neighbour(dims, from_there if received else offset))
        def _():
            src, dst = halo_parts(shape, slot, offset, *refs)
            if received:
                wait_bytes(dst, sems.at[slot, 1, index])
            else:
                wait_bytes(src, sems.at[slot, 0, index])


def shift_columns(shape, slot, field, face, edge, corner, shifted):
    size_x, size_y, size_z, columns = shape
    place = lax.broadcasted_iota(jnp.int32, (size_z, columns), 0)

    def put(x, y, below, above):
        value = field[slot, x, y]
        shifted[0, x, y] = jnp.where(place == 0, below, pltpu.roll(value, 1, 0))
        shifted[1, x, y] = jnp.where(place == size_z - 1, above, pltpu.roll(value, size_z - 1, 0))

    @pl.loop(0, size_x + 2)
    def _(x):
        for y in range(size_y):
            put(x, y + 1, face[slot, 0, x, y : y + 1], face[slot, 1, x, y : y + 1])

    for far in (0, 1):
        y = size_y + 1 if far else 0

        @pl.loop(0, size_x)
        def _(x):
            put(x + 1, y, edge[slot, 0, far, pl.ds(x, 1)], edge[slot, 1, far, pl.ds(x, 1)])

        for right in (0, 1):
            x = size_x + 1 if right else 0
            put(x, y, corner[slot, 0, far, right], corner[slot, 1, far, right])


def apply_rows(shape, slot, x, field, shifted, onsite, hopping):
    size_y = shape[1]
    totals = [None] * size_y
    centres = [None] * size_y
    for dx in (-1, 0, 1):
        for y in range(-1, size_y + 1):
            for dz in (-1, 0, 1):
                if dz == 0:
                    value = field[slot, x + 1 + dx, y + 1]
                else:
                    value = shifted[0 if dz < 0 else 1, x + 1 + dx, y + 1]
                for dy in (-1, 0, 1):
                    target = y - dy
                    if not 0 <= target < size_y:
                        continue
                    if (dx, dy, dz) == (0, 0, 0):
                        centres[target] = value
                        level = onsite[x, target]
                        term = level * value
                    else:
                        term = hopping[hop_index((dx, dy, dz))] * value
                    totals[target] = term if totals[target] is None else totals[target] + term
    return totals, centres


def spread(onsite, levels):
    size_x, size_y, size_z, lanes = levels.shape
    diagonal = lax.broadcasted_iota(jnp.int32, (size_z, size_z), 0) == lax.broadcasted_iota(
        jnp.int32, (size_z, size_z), 1
    )

    @pl.loop(0, size_x)
    def _(x):
        for y in range(size_y):
            row = jnp.broadcast_to(onsite[x, y : y + 1], (size_z, size_z))
            column = jnp.sum(jnp.where(diagonal, row, 0.0), axis=1, keepdims=True)
            levels[x, y] = jnp.broadcast_to(column, (size_z, lanes))


def filter_coefficients(bound, cut_frac, coef):
    cut = cut_frac * bound
    half_width = (bound - cut) / 2.0
    center = (bound + cut) / 2.0
    sigma_one = half_width / (-bound - center)
    sigma = sigma_one
    coef[0] = center
    coef[1] = sigma / half_width
    for k in range(1, DEG):
        sigma_next = 1.0 / (2.0 / sigma_one - sigma)
        coef[2 * k] = 2.0 * sigma_next / half_width
        coef[2 * k + 1] = sigma * sigma_next
        sigma = sigma_next


def filter_kernel(
    dims, shape, sites,
    block, onsite, hopping, cut_frac,
    first, gram_two, between, lower,
    *scratch,
):
    size_x, size_y, size_z, lanes = shape
    per_half = HALO_REFS
    halves = []
    for half in range(HALVES):
        *refs, shifted, sems = scratch[half * per_half : (half + 1) * per_half]
        halves.append((tuple(refs), shifted, sems))
    (
        onsite_here, levels, input_sems,
        max_plane, max_column, max_sems, coef,
        flat, image, moved, gram, inverse, work,
        *sum_refs,
    ) = scratch[HALVES * per_half :]
    enter(dims, True)
    copies = [pltpu.make_async_copy(onsite, onsite_here, input_sems.at[HALVES])]
    for half, (refs, _, _) in enumerate(halves):
        inside = refs[0].at[0, pl.ds(1, size_x), pl.ds(1, size_y)]
        source = block.at[:, :, :, pl.ds(lanes * half, lanes)]
        copies.append(pltpu.make_async_copy(source, inside, input_sems.at[half]))
    for copy in copies:
        copy.start()
    for refs, _, _ in halves:
        zero_border(dims, shape, 2, *refs[:4])
    copies[0].wait()
    place = place_of(dims)
    max_plane[place] = jnp.full((8, 128), jnp.max(jnp.abs(onsite_here[...])), jnp.float32)
    for copy, (refs, _, _) in zip(copies[1:], halves):
        copy.wait()
        field, face_out, edge_out, corner_out = refs[0], *refs[4:]

        @pl.loop(0, size_x)
        def _(x):
            for y in range(size_y):
                pack_column(shape, 0, x, y, field[0, x + 1, y + 1], face_out, edge_out)

        pack_corners(shape, 0, field, corner_out)
    spread(onsite_here, levels)
    entered(dims, True)
    for index, (refs, _, sems) in enumerate(halves):
        halo_send(dims, shape, 0, refs, sems)
        if index == 0:
            max_start(dims, None, max_plane, max_sems)
    max_middle(dims, max_plane, max_column, max_sems)
    for step in range(DEG):
        slot, after = step % 2, (step + 1) % 2
        for half, (refs, shifted, sems) in enumerate(halves):
            field, face, edge, corner, face_out, edge_out, corner_out = refs
            halo_wait(dims, shape, slot, refs, sems, True)
            shift_columns(shape, slot, field, face, edge, corner, shifted)
            if step == 0 and half == 0:
                reach = jnp.abs(hopping[0])
                for k in range(1, len(POSITIVE)):
                    reach = reach + jnp.abs(hopping[k])
                bound = max_end(dims, max_plane, max_column, max_sems) + 2.0 * reach
                filter_coefficients(bound, cut_frac[0], coef)
            if step:
                halo_wait(dims, shape, after, refs, sems, False)

            @pl.loop(0, size_x)
            def _(x):
                totals, centres = apply_rows(shape, slot, x, field, shifted, levels, hopping)
                for y in range(size_y):
                    value = totals[y] - coef[0] * centres[y]
                    if step == 0:
                        value = coef[1] * value
                    else:
                        older = field[after, x + 1, y + 1]
                        value = coef[2 * step] * value - coef[2 * step + 1] * older
                    if step == DEG - 1:
                        flat[site_rows(shape, x, y), lanes * half : lanes * (half + 1)] = value
                    field[after, x + 1, y + 1] = value
                    pack_column(shape, after, x, y, value, face_out, edge_out)

            pack_corners(shape, after, field, corner_out)
            halo_send(dims, shape, after, refs, sems)
    slot = DEG % 2
    per_sum = len(sum_refs) // 3
    sums, sums_two, sums_between = [
        AllReduce(dims, *sum_refs[k * per_sum : (k + 1) * per_sum]) for k in range(3)
    ]
    sums.local[...] = product(flat[...], flat[...])
    sums.scatter()
    for refs, shifted, sems in halves:
        halo_wait(dims, shape, slot, refs, sems, True)
        shift_columns(shape, slot, *refs[:4], shifted)
    sums.across()
    for half, (refs, shifted, sems) in enumerate(halves):

        @pl.loop(0, size_x)
        def _(x):
            totals, _ = apply_rows(shape, slot, x, refs[0], shifted, levels, hopping)
            for y in range(size_y):
                image[site_rows(shape, x, y), lanes * half : lanes * (half + 1)] = totals[y]

    sums.gather()
    for refs, _, sems in halves:
        halo_wait(dims, shape, 1 - slot, refs, sems, False)
        halo_wait(dims, shape, slot, refs, sems, False)
    sums.finish()
    gram[...] = sums.total[...] / sites
    factor_kernel(PANEL, gram, lower, inverse, work)
    rotate_and_sum(
        dims, sites, flat, image, inverse, first, gram_two, between, moved, sums_two, sums_between
    )


def site_rows(shape, x, y):
    _, size_y, size_z, _ = shape
    return pl.ds(pl.multiple_of((x * size_y + y) * size_z, size_z), size_z)


def product(left, right):
    return lax.dot_general(
        left,
        right,
        (((0,), (0,)), ((), ())),
        precision=HIGHEST,
        preferred_element_type=jnp.float32,
    )


def rotated(flat, factor):
    return lax.dot_general(
        flat,
        factor,
        (((1,), (1,)), ((), ())),
        precision=HIGHEST,
        preferred_element_type=jnp.float32,
    )


def rotate_and_sum(dims, sites, flat, image, inverse, first, gram, between, moved, sums, sums_b):
    first[...] = rotated(flat[...], inverse[...])
    sums.local[...] = product(first[...], first[...])
    sums.scatter()
    moved[...] = rotated(image[...], inverse[...])
    sums_b.local[...] = product(first[...], moved[...])
    sums_b.scatter()
    sums.across()
    sums_b.across()
    sums.gather()
    sums_b.gather()
    sums.finish()
    gram[...] = sums.total[...] / sites
    sums_b.finish()
    between[...] = sums_b.total[...] / sites


def call(kernel, inputs, scalars, outputs, scratch, ident, space=pltpu.VMEM):
    vmem = pl.BlockSpec(memory_space=pltpu.VMEM)
    smem = pl.BlockSpec(memory_space=pltpu.SMEM)
    return pl.pallas_call(
        kernel,
        out_shape=[jax.ShapeDtypeStruct(shape, jnp.float32) for shape in outputs],
        in_specs=[pl.BlockSpec(memory_space=space)] * len(inputs) + [smem] * len(scalars),
        out_specs=[vmem] * len(outputs),
        scratch_shapes=scratch,
        compiler_params=pltpu.CompilerParams(
            collective_id=ident, has_side_effects=True, vmem_limit_bytes=48 << 20
        ),
    )(*inputs, *scalars)


def factor_kernel(nb, gram, lower, inverse, work):
    size = gram.shape[0]
    tiles = size // 128
    groups = nb // 8
    lane = lax.broadcasted_iota(jnp.int32, (8, 128), 1)
    sub = lax.broadcasted_iota(jnp.int32, (8, 128), 0)
    for t in range(tiles):
        work[t] = gram[:, 128 * t : 128 * (t + 1)]
    for t in range(tiles):
        r = lax.broadcasted_iota(jnp.int32, (size, 128), 0)
        c = lax.broadcasted_iota(jnp.int32, (size, 128), 1) + 128 * t
        work[tiles + t] = jnp.where(r == c, 1.0, 0.0)

    def row(v, j):
        return jnp.broadcast_to(v[j % 8 : j % 8 + 1], (8, 128))

    for start in range(0, size, nb):
        stop = start + nb
        active = [t for t in range(tiles) if 128 * (t + 1) > start]
        active += [tiles + t for t in range(tiles) if 128 * t < stop]
        home = start // 128
        panel = {
            t: [work[t, start + 8 * g : start + 8 * g + 8] for g in range(groups)] for t in active
        }
        cols = [
            [
                jnp.broadcast_to(
                    panel[home][g][:, start % 128 + k : start % 128 + k + 1], (8, 128)
                )
                for g in range(groups)
            ]
            for k in range(nb)
        ]
        recip = [jnp.ones((8, 128), jnp.float32)] * groups
        pivots = [jnp.ones((8, 128), jnp.float32)] * groups
        for j in range(nb):
            home_group = j // 8
            pivot = row(cols[j][home_group], j)
            inv = 1.0 / pivot
            at = sub == j % 8
            recip[home_group] = jnp.where(at, inv, recip[home_group])
            pivots[home_group] = jnp.where(at, pivot, pivots[home_group])
            mult = [None] * groups
            for g in range(home_group, groups):
                mult[g] = cols[j][g] * inv
                if g == home_group:
                    mult[g] = jnp.where(sub > j % 8, mult[g], 0.0)
            for k in range(j + 1, nb):
                top = row(cols[k][home_group], j)
                for g in range(home_group, groups):
                    cols[k][g] = cols[k][g] - mult[g] * top
            for t in active:
                top = row(panel[t][home_group], j)
                for g in range(home_group, groups):
                    panel[t][g] = panel[t][g] - mult[g] * top
        if stop < size:
            full = {t: jnp.concatenate(panel[t], 0) if groups > 1 else panel[t][0] for t in active}
            recips = jnp.concatenate(recip, 0) if groups > 1 else recip[0]
            for u in range(tiles):
                low = max(128 * u, stop)
                if low >= 128 * (u + 1):
                    continue
                left = (full[u] * recips)[:, low - 128 * u :]
                for t in active:
                    if t < u:
                        continue
                    work[t, low : 128 * (u + 1)] -= lax.dot_general(
                        left, full[t], (((0,), (0,)), ((), ())),
                        precision=HIGHEST, preferred_element_type=jnp.float32)
        for g in range(groups):
            scale = 1.0 / jnp.sqrt(pivots[g])
            at = slice(start + 8 * g, start + 8 * g + 8)
            for t in range(tiles):
                if t in active:
                    keep = lane + 128 * t >= sub + (start + 8 * g)
                    work[t, at] = jnp.where(keep, panel[t][g] * scale, 0.0)
                else:
                    work[t, at] = jnp.zeros((8, 128), jnp.float32)
                if tiles + t in active:
                    inverse[at, 128 * t : 128 * t + 128] = panel[tiles + t][g] * scale
                else:
                    inverse[at, 128 * t : 128 * t + 128] = jnp.zeros((8, 128), jnp.float32)
    for t in range(tiles):
        lower[128 * t : 128 * t + 128, :] = work[t].T

def near_identity_kernel(gram, inverse):
    size = gram.shape[0]
    row = lax.broadcasted_iota(jnp.int32, (size, size), 0)
    col = lax.broadcasted_iota(jnp.int32, (size, size), 1)
    ident = jnp.where(row == col, 1.0, 0.0)
    weight = jnp.where(row > col, 1.0, 0.5 * ident)

    def times(left, right, across):
        return lax.dot_general(
            left, right, (((1,), (across,)), ((), ())),
            precision=HIGHEST, preferred_element_type=jnp.float32,
        )

    error = gram[...] - ident
    shift = None
    for step in range(NEAR_STEPS):
        low = weight * error
        shift = low if shift is None else shift + low - times(low, shift, 0)
        if step < NEAR_STEPS - 1:
            cross = times(low, error, 0)
            error = times(low + cross, low, 1) - cross - cross.T
    inverse[...] = ident - shift
    return jnp.sum(error * error)


def finish_kernel(
    nb, gram, first, between, lower_one, states, projected, factor, lower, inverse, work
):
    factor[...] = lower_one[...]
    left = near_identity_kernel(gram, inverse)

    @pl.when(jnp.logical_not(left < NEAR_LEFT * NEAR_LEFT))
    def _():
        factor_kernel(nb, gram, lower, inverse, work)

    states[...] = rotated(first[...], inverse[...])
    half = rotated(between[...], inverse[...])
    projected[...] = jnp.dot(
        inverse[...], half, precision=HIGHEST, preferred_element_type=jnp.float32
    )


def local_call(kernel, inputs, outputs, scratch):
    vmem = pl.BlockSpec(memory_space=pltpu.VMEM)
    return pl.pallas_call(
        kernel,
        out_shape=[jax.ShapeDtypeStruct(shape, jnp.float32) for shape in outputs],
        in_specs=[vmem] * len(inputs),
        out_specs=[vmem] * len(outputs),
        scratch_shapes=scratch,
        compiler_params=pltpu.CompilerParams(vmem_limit_bytes=32 << 20),
    )(*inputs)


def body(dims, block, onsite, hopping, cut_frac):
    shape = block.shape
    size_x, size_y, size_z, columns = shape
    count = size_x * size_y * size_z
    sites = count * dims[0] * dims[1] * dims[2]
    plane, column = dims[0] * dims[2], dims[1]
    sums = reduce_scratch(dims, columns)
    square = (columns, columns)
    work = pltpu.VMEM((2 * (columns // 128), columns, 128), jnp.float32)
    lanes = columns // HALVES
    part = (size_x, size_y, size_z, lanes)
    first, gram_two, between, lower_one = call(
        functools.partial(filter_kernel, dims, part, sites),
        [pltpu.with_memory_space_constraint(v, pltpu.HBM) for v in (block, onsite)],
        [hopping, cut_frac],
        [(count, columns), square, square, square],
        halo_scratch(part, 2) * HALVES
        + [
            pltpu.VMEM((size_x, size_y, size_z), jnp.float32),
            pltpu.VMEM(part, jnp.float32),
            pltpu.SemaphoreType.DMA((HALVES + 1,)),
            pltpu.VMEM((plane, 8, 128), jnp.float32),
            pltpu.VMEM((column, 8, 128), jnp.float32),
            pltpu.SemaphoreType.DMA((4,)),
            pltpu.VMEM((2 * DEG, 8, 128), jnp.float32),
        ]
        + [pltpu.VMEM((count, columns), jnp.float32)] * 3
        + [pltpu.VMEM(square, jnp.float32)] * 2
        + [work]
        + sums * 3,
        1,
        pltpu.HBM,
    )
    states, projected, factor = local_call(
        functools.partial(finish_kernel, PANEL),
        [gram_two, first, between, lower_one],
        [(count, columns), square, square],
        [pltpu.VMEM(square, jnp.float32), pltpu.VMEM(square, jnp.float32), work],
    )
    return (states.reshape(shape), projected, factor)


def solution(mesh):
    dims = (mesh.shape["gx"], mesh.shape["gy"], mesh.shape["gz"])
    return jax.shard_map(
        functools.partial(body, dims),
        mesh=mesh,
        in_specs=(P("gx", "gy", "gz", None), P("gx", "gy", "gz"), P(), P()),
        out_specs=(P("gx", "gy", "gz", None), P(), P()),
        check_vma=False,
    )
```

```python
import functools

import jax
import jax.numpy as jnp
from jax import lax
from jax.experimental import pallas as pl
from jax.experimental.pallas import tpu as pltpu
from jax.sharding import PartitionSpec as P

DEG = 4
PANEL = 16
NEAR_STEPS = 4
NEAR_LEFT = 1e-3
HALVES = 2
HALO_REFS = 9
MESH = pl.DeviceIdType.MESH
HIGHEST = lax.Precision.HIGHEST
AXES = ("gx", "gy", "gz")
OFFSETS = [
    (dx, dy, dz)
    for dx in (-1, 0, 1)
    for dy in (-1, 0, 1)
    for dz in (-1, 0, 1)
    if (dx, dy, dz) != (0, 0, 0)
]
POSITIVE = [offset for offset in OFFSETS if offset > (0, 0, 0)]


def hop_index(offset):
    return POSITIVE.index(max(offset, tuple(-d for d in offset)))


def plane_peer(dims, offset):
    size_x, _, size_z = dims
    place = lax.axis_index("gx") * size_z + lax.axis_index("gz")
    peer = lax.rem(place + offset, size_x * size_z)
    return peer, {"gx": peer // size_z, "gz": lax.rem(peer, size_z)}


def column_peer(dims, offset):
    peer = lax.rem(lax.axis_index("gy") + offset, dims[1])
    return peer, {"gy": peer}


def has_neighbour(dims, offset):
    valid = None
    for axis, size, step in zip(AXES, dims, offset):
        if step:
            place = lax.axis_index(axis)
            here = place < size - 1 if step > 0 else place > 0
            valid = here if valid is None else jnp.logical_and(valid, here)
    return valid


def neighbour(offset):
    return {axis: lax.axis_index(axis) + step for axis, step in zip(AXES, offset) if step}


def enter(dims, halo):
    barrier = pltpu.get_barrier_semaphore()

    @pl.loop(1, dims[0] * dims[2])
    def _(k):
        pl.semaphore_signal(barrier, inc=1, device_id=plane_peer(dims, k)[1], device_id_type=MESH)

    @pl.loop(1, dims[1])
    def _(k):
        pl.semaphore_signal(barrier, inc=1, device_id=column_peer(dims, k)[1], device_id_type=MESH)

    if halo:
        for offset in OFFSETS:

            @pl.when(has_neighbour(dims, offset))
            def _():
                pl.semaphore_signal(
                    barrier, inc=1, device_id=neighbour(offset), device_id_type=MESH
                )


def entered(dims, halo):
    count = dims[0] * dims[2] + dims[1] - 2
    if halo:
        boxes = 1
        for axis, size in zip(AXES, dims):
            place = lax.axis_index(axis)
            boxes = boxes * (3 - (place == 0).astype(jnp.int32) - (place == size - 1).astype(jnp.int32))
        count = count + boxes - 1
    pl.semaphore_wait(pltpu.get_barrier_semaphore(), count)


def wait_bytes(ref, sem):
    pltpu.make_async_copy(ref, ref, sem).wait()


def send(src, dst, send_sem, recv_sem, device):
    pltpu.make_async_remote_copy(
        src_ref=src,
        dst_ref=dst,
        send_sem=send_sem,
        recv_sem=recv_sem,
        device_id=device,
        device_id_type=MESH,
    ).start()


def place_of(dims):
    return lax.axis_index("gx") * dims[2] + lax.axis_index("gz")


class AllReduce:
    def __init__(self, dims, local, total, plane_buf, column_buf, sems):
        self.dims, self.local, self.total = dims, local, total
        self.plane_buf, self.column_buf, self.sems = plane_buf, column_buf, sems
        self.plane, self.column = dims[0] * dims[2], dims[1]
        self.rows = local.shape[0] // self.plane
        self.mine = pl.ds(pl.multiple_of(place_of(dims) * self.rows, self.rows), self.rows)

    def scatter(self):
        @pl.loop(1, self.plane)
        def _(k):
            peer, device = plane_peer(self.dims, k)
            theirs = pl.ds(pl.multiple_of(peer * self.rows, self.rows), self.rows)
            send(
                self.local.at[theirs], self.plane_buf.at[k - 1],
                self.sems.at[0], self.sems.at[1], device,
            )

    def across(self):
        level = lax.axis_index("gy")
        wait_bytes(self.plane_buf, self.sems.at[1])
        self.column_buf[level] = lax.fori_loop(
            0, self.plane - 1, lambda k, acc: acc + self.plane_buf[k], self.local[self.mine]
        )
        mine = self.column_buf.at[level]

        @pl.loop(1, self.column)
        def _(k):
            _, device = column_peer(self.dims, k)
            send(mine, mine, self.sems.at[2], self.sems.at[3], device)

    def gather(self):
        wait_bytes(self.column_buf.at[pl.ds(0, self.column - 1)], self.sems.at[3])
        part = self.column_buf[0]
        for k in range(1, self.column):
            part = part + self.column_buf[k]
        self.total[self.mine] = part
        mine = self.total.at[self.mine]

        @pl.loop(1, self.plane)
        def _(k):
            _, device = plane_peer(self.dims, k)
            send(mine, mine, self.sems.at[4], self.sems.at[5], device)

    def finish(self):
        others = self.total.at[pl.ds(0, (self.plane - 1) * self.rows)]
        wait_bytes(others, self.sems.at[5])
        wait_bytes(self.plane_buf, self.sems.at[0])
        wait_bytes(self.column_buf.at[pl.ds(0, self.column - 1)], self.sems.at[2])
        wait_bytes(others, self.sems.at[4])


def reduce_scratch(dims, size):
    plane, column = dims[0] * dims[2], dims[1]
    rows = size // plane
    return [
        pltpu.VMEM((size, size), jnp.float32),
        pltpu.VMEM((size, size), jnp.float32),
        pltpu.VMEM((plane - 1, rows, size), jnp.float32),
        pltpu.VMEM((column, rows, size), jnp.float32),
        pltpu.SemaphoreType.DMA((6,)),
    ]


def max_start(dims, value, plane_buf, sems):
    plane = dims[0] * dims[2]
    place = lax.axis_index("gx") * dims[2] + lax.axis_index("gz")

    @pl.loop(1, plane)
    def _(k):
        _, device = plane_peer(dims, k)
        send(plane_buf.at[place], plane_buf.at[place], sems.at[0], sems.at[1], device)


def max_middle(dims, plane_buf, column_buf, sems):
    plane, column = dims[0] * dims[2], dims[1]
    level = lax.axis_index("gy")
    wait_bytes(plane_buf.at[pl.ds(0, plane - 1)], sems.at[1])
    column_buf[level] = jnp.max(plane_buf[...], axis=0)

    @pl.loop(1, column)
    def _(k):
        _, device = column_peer(dims, k)
        send(column_buf.at[level], column_buf.at[level], sems.at[2], sems.at[3], device)


def max_end(dims, plane_buf, column_buf, sems):
    plane, column = dims[0] * dims[2], dims[1]
    wait_bytes(column_buf.at[pl.ds(0, column - 1)], sems.at[3])
    wait_bytes(plane_buf.at[pl.ds(0, plane - 1)], sems.at[0])
    wait_bytes(column_buf.at[pl.ds(0, column - 1)], sems.at[2])
    return jnp.max(column_buf[...], axis=0)


def halo_scratch(shape, slots):
    size_x, size_y, size_z, columns = shape
    f32 = jnp.float32
    return [
        pltpu.VMEM((slots, size_x + 2, size_y + 2, size_z, columns), f32),
        pltpu.VMEM((slots, 2, size_x + 2, size_y, columns), f32),
        pltpu.VMEM((slots, 2, 2, size_x, columns), f32),
        pltpu.VMEM((slots, 2, 2, 2, 8, columns), f32),
        pltpu.VMEM((slots, 2, size_x, size_y, columns), f32),
        pltpu.VMEM((slots, 2, 2, size_x, columns), f32),
        pltpu.VMEM((slots, 2, 2, 2, 8, columns), f32),
        pltpu.VMEM((2, size_x + 2, size_y + 2, size_z, columns), f32),
        pltpu.SemaphoreType.DMA((slots, 2, len(OFFSETS))),
    ]


def halo_parts(shape, slot, offset, field, face, edge, corner, face_out, edge_out, corner_out):
    size_x, size_y, _, _ = shape
    sx, sy, sz = offset
    low = {1: 0, -1: 1}

    def ends(step, size):
        if step == 0:
            return pl.ds(1, size), pl.ds(1, size)
        return (size, 0) if step > 0 else (1, size + 1)

    from_x, to_x = ends(sx, size_x)
    from_y, to_y = ends(sy, size_y)
    if sz == 0:
        return field.at[slot, from_x, from_y], field.at[slot, to_x, to_y]
    top = 1 if sz > 0 else 0
    if sy == 0:
        source = pl.ds(0, size_x) if sx == 0 else from_x - 1
        return face_out.at[slot, top, source], face.at[slot, 1 - top, to_x]
    far = 1 if sy > 0 else 0
    if sx == 0:
        return edge_out.at[slot, top, far], edge.at[slot, 1 - top, 1 - far]
    right = 1 if sx > 0 else 0
    return (
        corner_out.at[slot, top, far, right],
        corner.at[slot, 1 - top, 1 - far, 1 - right],
    )


def zero_border(dims, shape, slots, field, face, edge, corner):
    size_x, size_y, size_z, columns = shape
    for slot in range(slots):
        for side in (0, 1):
            step = 1 if side else -1
            row = size_x + 1 if side else 0

            @pl.when(jnp.logical_not(has_neighbour(dims, (step, 0, 0))))
            def _():
                field[slot, row] = jnp.zeros((size_y + 2, size_z, columns), jnp.float32)
                for top in (0, 1):
                    face[slot, top, row] = jnp.zeros((size_y, columns), jnp.float32)
                    for far in (0, 1):
                        corner[slot, top, far, side] = jnp.zeros((8, columns), jnp.float32)

            row_y = size_y + 1 if side else 0

            @pl.when(jnp.logical_not(has_neighbour(dims, (0, step, 0))))
            def _():
                field[slot, :, row_y] = jnp.zeros((size_x + 2, size_z, columns), jnp.float32)
                for top in (0, 1):
                    edge[slot, top, side] = jnp.zeros((size_x, columns), jnp.float32)
                    for right in (0, 1):
                        corner[slot, top, side, right] = jnp.zeros((8, columns), jnp.float32)

            @pl.when(jnp.logical_not(has_neighbour(dims, (0, 0, step))))
            def _():
                face[slot, side] = jnp.zeros((size_x + 2, size_y, columns), jnp.float32)
                edge[slot, side] = jnp.zeros((2, size_x, columns), jnp.float32)
                corner[slot, side] = jnp.zeros((2, 2, 8, columns), jnp.float32)


def pack_column(shape, slot, x, y, value, face_out, edge_out):
    size_y, size_z = shape[1], shape[2]
    for top, z in ((0, 0), (1, size_z - 1)):
        row = value[z : z + 1]
        face_out[slot, top, x, y : y + 1] = row
        if y in (0, size_y - 1):
            edge_out[slot, top, 1 if y else 0, pl.ds(x, 1)] = row


def pack_corners(shape, slot, field, corner_out):
    size_x, size_y, size_z, columns = shape
    for top in (0, 1):
        for far in (0, 1):
            for right in (0, 1):
                z = (size_z - 1) * top
                corner_out[slot, top, far, right] = jnp.broadcast_to(
                    field[slot, size_x if right else 1, size_y if far else 1, z : z + 1],
                    (8, columns),
                )


def halo_send(dims, shape, slot, refs, sems):
    for index, offset in enumerate(OFFSETS):

        @pl.when(has_neighbour(dims, offset))
        def _():
            src, dst = halo_parts(shape, slot, offset, *refs)
            send(src, dst, sems.at[slot, 0, index], sems.at[slot, 1, index], neighbour(offset))


def halo_wait(dims, shape, slot, refs, sems, received):
    for index, offset in enumerate(OFFSETS):
        from_there = tuple(-step for step in offset)

        @pl.when(has_neighbour(dims, from_there if received else offset))
        def _():
            src, dst = halo_parts(shape, slot, offset, *refs)
            if received:
                wait_bytes(dst, sems.at[slot, 1, index])
            else:
                wait_bytes(src, sems.at[slot, 0, index])


def shift_columns(shape, slot, field, face, edge, corner, shifted):
    size_x, size_y, size_z, columns = shape
    place = lax.broadcasted_iota(jnp.int32, (size_z, columns), 0)

    def put(x, y, below, above):
        value = field[slot, x, y]
        shifted[0, x, y] = jnp.where(place == 0, below, pltpu.roll(value, 1, 0))
        shifted[1, x, y] = jnp.where(place == size_z - 1, above, pltpu.roll(value, size_z - 1, 0))

    @pl.loop(0, size_x + 2)
    def _(x):
        for y in range(size_y):
            put(x, y + 1, face[slot, 0, x, y : y + 1], face[slot, 1, x, y : y + 1])

    for far in (0, 1):
        y = size_y + 1 if far else 0

        @pl.loop(0, size_x)
        def _(x):
            put(x + 1, y, edge[slot, 0, far, pl.ds(x, 1)], edge[slot, 1, far, pl.ds(x, 1)])

        for right in (0, 1):
            x = size_x + 1 if right else 0
            put(x, y, corner[slot, 0, far, right], corner[slot, 1, far, right])


def apply_rows(shape, slot, x, field, shifted, onsite, hopping):
    size_y = shape[1]
    totals = [None] * size_y
    centres = [None] * size_y
    for dx in (-1, 0, 1):
        for y in range(-1, size_y + 1):
            for dz in (-1, 0, 1):
                if dz == 0:
                    value = field[slot, x + 1 + dx, y + 1]
                else:
                    value = shifted[0 if dz < 0 else 1, x + 1 + dx, y + 1]
                for dy in (-1, 0, 1):
                    target = y - dy
                    if not 0 <= target < size_y:
                        continue
                    if (dx, dy, dz) == (0, 0, 0):
                        centres[target] = value
                        level = onsite[x, target]
                        term = level * value
                    else:
                        term = hopping[hop_index((dx, dy, dz))] * value
                    totals[target] = term if totals[target] is None else totals[target] + term
    return totals, centres


def spread(onsite, levels):
    size_x, size_y, size_z, lanes = levels.shape
    diagonal = lax.broadcasted_iota(jnp.int32, (size_z, size_z), 0) == lax.broadcasted_iota(
        jnp.int32, (size_z, size_z), 1
    )

    @pl.loop(0, size_x)
    def _(x):
        for y in range(size_y):
            row = jnp.broadcast_to(onsite[x, y : y + 1], (size_z, size_z))
            column = jnp.sum(jnp.where(diagonal, row, 0.0), axis=1, keepdims=True)
            levels[x, y] = jnp.broadcast_to(column, (size_z, lanes))


def filter_coefficients(bound, cut_frac, coef):
    cut = cut_frac * bound
    half_width = (bound - cut) / 2.0
    center = (bound + cut) / 2.0
    sigma_one = half_width / (-bound - center)
    sigma = sigma_one
    coef[0] = center
    coef[1] = sigma / half_width
    for k in range(1, DEG):
        sigma_next = 1.0 / (2.0 / sigma_one - sigma)
        coef[2 * k] = 2.0 * sigma_next / half_width
        coef[2 * k + 1] = sigma * sigma_next
        sigma = sigma_next


def filter_kernel(
    dims, shape, sites,
    block, onsite, hopping, cut_frac,
    first, gram_two, between, lower,
    *scratch,
):
    size_x, size_y, size_z, lanes = shape
    per_half = HALO_REFS
    halves = []
    for half in range(HALVES):
        *refs, shifted, sems = scratch[half * per_half : (half + 1) * per_half]
        halves.append((tuple(refs), shifted, sems))
    (
        onsite_here, levels, input_sems,
        max_plane, max_column, max_sems, coef,
        flat, image, moved, gram, inverse, work,
        *sum_refs,
    ) = scratch[HALVES * per_half :]
    enter(dims, True)
    early = moved
    copies = [pltpu.make_async_copy(onsite, onsite_here, input_sems.at[HALVES])]
    for half, (refs, _, _) in enumerate(halves):
        inside = refs[0].at[0, pl.ds(1, size_x), pl.ds(1, size_y)]
        source = block.at[:, :, :, pl.ds(lanes * half, lanes)]
        copies.append(pltpu.make_async_copy(source, inside, input_sems.at[half]))
    for copy in copies:
        copy.start()
    for refs, _, _ in halves:
        zero_border(dims, shape, 2, *refs[:4])
    copies[0].wait()
    place = place_of(dims)
    max_plane[place] = jnp.full((8, 128), jnp.max(jnp.abs(onsite_here[...])), jnp.float32)
    for copy, (refs, _, _) in zip(copies[1:], halves):
        copy.wait()
        field, face_out, edge_out, corner_out = refs[0], *refs[4:]

        @pl.loop(0, size_x)
        def _(x):
            for y in range(size_y):
                pack_column(shape, 0, x, y, field[0, x + 1, y + 1], face_out, edge_out)

        pack_corners(shape, 0, field, corner_out)
    spread(onsite_here, levels)
    entered(dims, True)
    for index, (refs, _, sems) in enumerate(halves):
        halo_send(dims, shape, 0, refs, sems)
        if index == 0:
            max_start(dims, None, max_plane, max_sems)
    for step in range(DEG):
        slot, after = step % 2, (step + 1) % 2
        for half, (refs, shifted, sems) in enumerate(halves):
            field, face, edge, corner, face_out, edge_out, corner_out = refs
            halo_wait(dims, shape, slot, refs, sems, True)
            shift_columns(shape, slot, field, face, edge, corner, shifted)
            if step == 1 and half == 0:
                reach = jnp.abs(hopping[0])
                for k in range(1, len(POSITIVE)):
                    reach = reach + jnp.abs(hopping[k])
                bound = max_end(dims, max_plane, max_column, max_sems) + 2.0 * reach
                filter_coefficients(bound, cut_frac[0], coef)
            if step:
                halo_wait(dims, shape, after, refs, sems, False)

            @pl.loop(0, size_x)
            def _(x):
                totals, centres = apply_rows(shape, slot, x, field, shifted, levels, hopping)
                for y in range(size_y):
                    mine = (site_rows(shape, x, y), slice(lanes * half, lanes * (half + 1)))
                    value = totals[y]
                    if step == 1:
                        older = field[after, x + 1, y + 1]
                        newer = coef[1] * (centres[y] - coef[0] * older)
                        early[mine] = newer
                        value = coef[1] * (value - coef[0] * centres[y])
                    elif step > 1:
                        newer = centres[y]
                        older = early[mine] if step == 2 else field[after, x + 1, y + 1]
                    if step:
                        value = coef[2 * step] * (value - coef[0] * newer)
                        value = value - coef[2 * step + 1] * older
                    if step == DEG - 1:
                        flat[mine] = value
                    field[after, x + 1, y + 1] = value
                    pack_column(shape, after, x, y, value, face_out, edge_out)

            pack_corners(shape, after, field, corner_out)
            halo_send(dims, shape, after, refs, sems)
            if step == 0 and half == 0:
                max_middle(dims, max_plane, max_column, max_sems)
    slot = DEG % 2
    per_sum = len(sum_refs) // 3
    sums, sums_two, sums_between = [
        AllReduce(dims, *sum_refs[k * per_sum : (k + 1) * per_sum]) for k in range(3)
    ]
    sums.local[...] = product(flat[...], flat[...])
    sums.scatter()
    for refs, shifted, sems in halves:
        halo_wait(dims, shape, slot, refs, sems, True)
        shift_columns(shape, slot, *refs[:4], shifted)
    sums.across()
    for half, (refs, shifted, sems) in enumerate(halves):

        @pl.loop(0, size_x)
        def _(x):
            totals, _ = apply_rows(shape, slot, x, refs[0], shifted, levels, hopping)
            for y in range(size_y):
                image[site_rows(shape, x, y), lanes * half : lanes * (half + 1)] = totals[y]

    sums.gather()
    for refs, _, sems in halves:
        halo_wait(dims, shape, 1 - slot, refs, sems, False)
        halo_wait(dims, shape, slot, refs, sems, False)
    sums.finish()
    gram[...] = sums.total[...] / sites
    factor_kernel(PANEL, gram, lower, inverse, work)
    rotate_and_sum(
        dims, sites, flat, image, inverse, first, gram_two, between, moved, sums_two, sums_between
    )


def site_rows(shape, x, y):
    _, size_y, size_z, _ = shape
    return pl.ds(pl.multiple_of((x * size_y + y) * size_z, size_z), size_z)


def product(left, right):
    return lax.dot_general(
        left,
        right,
        (((0,), (0,)), ((), ())),
        precision=HIGHEST,
        preferred_element_type=jnp.float32,
    )


def rotated(flat, factor):
    return lax.dot_general(
        flat,
        factor,
        (((1,), (1,)), ((), ())),
        precision=HIGHEST,
        preferred_element_type=jnp.float32,
    )


def rotate_and_sum(dims, sites, flat, image, inverse, first, gram, between, moved, sums, sums_b):
    first[...] = rotated(flat[...], inverse[...])
    sums.local[...] = product(first[...], first[...])
    sums.scatter()
    moved[...] = rotated(image[...], inverse[...])
    sums_b.local[...] = product(first[...], moved[...])
    sums_b.scatter()
    sums.across()
    sums_b.across()
    sums.gather()
    sums_b.gather()
    sums.finish()
    gram[...] = sums.total[...] / sites
    sums_b.finish()
    between[...] = sums_b.total[...] / sites


def call(kernel, inputs, scalars, outputs, scratch, ident, space=pltpu.VMEM):
    vmem = pl.BlockSpec(memory_space=pltpu.VMEM)
    smem = pl.BlockSpec(memory_space=pltpu.SMEM)
    return pl.pallas_call(
        kernel,
        out_shape=[jax.ShapeDtypeStruct(shape, jnp.float32) for shape in outputs],
        in_specs=[pl.BlockSpec(memory_space=space)] * len(inputs) + [smem] * len(scalars),
        out_specs=[vmem] * len(outputs),
        scratch_shapes=scratch,
        compiler_params=pltpu.CompilerParams(
            collective_id=ident, has_side_effects=True, vmem_limit_bytes=48 << 20
        ),
    )(*inputs, *scalars)


def factor_kernel(nb, gram, lower, inverse, work):
    size = gram.shape[0]
    tiles = size // 128
    groups = nb // 8
    lane = lax.broadcasted_iota(jnp.int32, (8, 128), 1)
    sub = lax.broadcasted_iota(jnp.int32, (8, 128), 0)
    for t in range(tiles):
        work[t] = gram[:, 128 * t : 128 * (t + 1)]
    for t in range(tiles):
        r = lax.broadcasted_iota(jnp.int32, (size, 128), 0)
        c = lax.broadcasted_iota(jnp.int32, (size, 128), 1) + 128 * t
        work[tiles + t] = jnp.where(r == c, 1.0, 0.0)

    def row(v, j):
        return jnp.broadcast_to(v[j % 8 : j % 8 + 1], (8, 128))

    for start in range(0, size, nb):
        stop = start + nb
        active = [t for t in range(tiles) if 128 * (t + 1) > start]
        active += [tiles + t for t in range(tiles) if 128 * t < stop]
        home = start // 128
        panel = {
            t: [work[t, start + 8 * g : start + 8 * g + 8] for g in range(groups)] for t in active
        }
        cols = [
            [
                jnp.broadcast_to(
                    panel[home][g][:, start % 128 + k : start % 128 + k + 1], (8, 128)
                )
                for g in range(groups)
            ]
            for k in range(nb)
        ]
        recip = [jnp.ones((8, 128), jnp.float32)] * groups
        pivots = [jnp.ones((8, 128), jnp.float32)] * groups
        for j in range(nb):
            home_group = j // 8
            pivot = row(cols[j][home_group], j)
            inv = 1.0 / pivot
            at = sub == j % 8
            recip[home_group] = jnp.where(at, inv, recip[home_group])
            pivots[home_group] = jnp.where(at, pivot, pivots[home_group])
            mult = [None] * groups
            for g in range(home_group, groups):
                mult[g] = cols[j][g] * inv
                if g == home_group:
                    mult[g] = jnp.where(sub > j % 8, mult[g], 0.0)
            for k in range(j + 1, nb):
                top = row(cols[k][home_group], j)
                for g in range(home_group, groups):
                    cols[k][g] = cols[k][g] - mult[g] * top
            for t in active:
                top = row(panel[t][home_group], j)
                for g in range(home_group, groups):
                    panel[t][g] = panel[t][g] - mult[g] * top
        if stop < size:
            full = {t: jnp.concatenate(panel[t], 0) if groups > 1 else panel[t][0] for t in active}
            recips = jnp.concatenate(recip, 0) if groups > 1 else recip[0]
            chunks = [(stop, stop + nb)] + [
                (max(128 * u, stop + nb), 128 * (u + 1)) for u in range(tiles)
            ]
            for low, high in chunks:
                if low >= high:
                    continue
                u = low // 128
                left = (full[u] * recips)[:, low - 128 * u : high - 128 * u]
                for t in active:
                    if t < u:
                        continue
                    work[t, low:high] -= lax.dot_general(
                        left, full[t], (((0,), (0,)), ((), ())),
                        precision=HIGHEST, preferred_element_type=jnp.float32)
        for g in range(groups):
            scale = 1.0 / jnp.sqrt(pivots[g])
            at = slice(start + 8 * g, start + 8 * g + 8)
            for t in range(tiles):
                if t in active:
                    keep = lane + 128 * t >= sub + (start + 8 * g)
                    work[t, at] = jnp.where(keep, panel[t][g] * scale, 0.0)
                else:
                    work[t, at] = jnp.zeros((8, 128), jnp.float32)
                if tiles + t in active:
                    inverse[at, 128 * t : 128 * t + 128] = panel[tiles + t][g] * scale
                else:
                    inverse[at, 128 * t : 128 * t + 128] = jnp.zeros((8, 128), jnp.float32)
    for t in range(tiles):
        lower[128 * t : 128 * t + 128, :] = work[t].T

def near_identity_kernel(gram, inverse):
    size = gram.shape[0]
    row = lax.broadcasted_iota(jnp.int32, (size, size), 0)
    col = lax.broadcasted_iota(jnp.int32, (size, size), 1)
    ident = jnp.where(row == col, 1.0, 0.0)
    weight = jnp.where(row > col, 1.0, 0.5 * ident)

    def times(left, right, across):
        return lax.dot_general(
            left, right, (((1,), (across,)), ((), ())),
            precision=HIGHEST, preferred_element_type=jnp.float32,
        )

    error = gram[...] - ident
    shift = None
    for step in range(NEAR_STEPS):
        low = weight * error
        shift = low if shift is None else shift + low - times(low, shift, 0)
        if step < NEAR_STEPS - 1:
            cross = times(low, error, 0)
            error = times(low + cross, low, 1) - cross - cross.T
    inverse[...] = ident - shift
    return jnp.sum(error * error)


def finish_kernel(
    nb, gram, first, between, lower_one, states, projected, factor, lower, inverse, work
):
    factor[...] = lower_one[...]
    left = near_identity_kernel(gram, inverse)

    @pl.when(jnp.logical_not(left < NEAR_LEFT * NEAR_LEFT))
    def _():
        factor_kernel(nb, gram, lower, inverse, work)

    states[...] = rotated(first[...], inverse[...])
    half = rotated(between[...], inverse[...])
    projected[...] = jnp.dot(
        inverse[...], half, precision=HIGHEST, preferred_element_type=jnp.float32
    )


def local_call(kernel, inputs, outputs, scratch):
    vmem = pl.BlockSpec(memory_space=pltpu.VMEM)
    return pl.pallas_call(
        kernel,
        out_shape=[jax.ShapeDtypeStruct(shape, jnp.float32) for shape in outputs],
        in_specs=[vmem] * len(inputs),
        out_specs=[vmem] * len(outputs),
        scratch_shapes=scratch,
        compiler_params=pltpu.CompilerParams(vmem_limit_bytes=32 << 20),
    )(*inputs)


def body(dims, block, onsite, hopping, cut_frac):
    shape = block.shape
    size_x, size_y, size_z, columns = shape
    count = size_x * size_y * size_z
    sites = count * dims[0] * dims[1] * dims[2]
    plane, column = dims[0] * dims[2], dims[1]
    sums = reduce_scratch(dims, columns)
    square = (columns, columns)
    work = pltpu.VMEM((2 * (columns // 128), columns, 128), jnp.float32)
    lanes = columns // HALVES
    part = (size_x, size_y, size_z, lanes)
    first, gram_two, between, lower_one = call(
        functools.partial(filter_kernel, dims, part, sites),
        [pltpu.with_memory_space_constraint(v, pltpu.HBM) for v in (block, onsite)],
        [hopping, cut_frac],
        [(count, columns), square, square, square],
        halo_scratch(part, 2) * HALVES
        + [
            pltpu.VMEM((size_x, size_y, size_z), jnp.float32),
            pltpu.VMEM(part, jnp.float32),
            pltpu.SemaphoreType.DMA((HALVES + 1,)),
            pltpu.VMEM((plane, 8, 128), jnp.float32),
            pltpu.VMEM((column, 8, 128), jnp.float32),
            pltpu.SemaphoreType.DMA((4,)),
            pltpu.VMEM((2 * DEG, 8, 128), jnp.float32),
        ]
        + [pltpu.VMEM((count, columns), jnp.float32)] * 3
        + [pltpu.VMEM(square, jnp.float32)] * 2
        + [work]
        + sums * 3,
        1,
        pltpu.HBM,
    )
    states, projected, factor = local_call(
        functools.partial(finish_kernel, PANEL),
        [gram_two, first, between, lower_one],
        [(count, columns), square, square],
        [pltpu.VMEM(square, jnp.float32), pltpu.VMEM(square, jnp.float32), work],
    )
    return (states.reshape(shape), projected, factor)


def solution(mesh):
    dims = (mesh.shape["gx"], mesh.shape["gy"], mesh.shape["gz"])
    return jax.shard_map(
        functools.partial(body, dims),
        mesh=mesh,
        in_specs=(P("gx", "gy", "gz", None), P("gx", "gy", "gz"), P(), P()),
        out_specs=(P("gx", "gy", "gz", None), P(), P()),
        check_vma=False,
    )
```

```python
import functools

import jax
import jax.numpy as jnp
from jax import lax
from jax.experimental import pallas as pl
from jax.experimental.pallas import tpu as pltpu
from jax.sharding import PartitionSpec as P

DEG = 4
PANEL = 16
NEAR_STEPS = 4
NEAR_LEFT = 1e-3
HALVES = 2
HALO_REFS = 9
MESH = pl.DeviceIdType.MESH
HIGHEST = lax.Precision.HIGHEST
AXES = ("gx", "gy", "gz")
OFFSETS = [
    (dx, dy, dz)
    for dx in (-1, 0, 1)
    for dy in (-1, 0, 1)
    for dz in (-1, 0, 1)
    if (dx, dy, dz) != (0, 0, 0)
]
POSITIVE = [offset for offset in OFFSETS if offset > (0, 0, 0)]


def hop_index(offset):
    return POSITIVE.index(max(offset, tuple(-d for d in offset)))


def plane_peer(dims, offset):
    size_x, _, size_z = dims
    place = lax.axis_index("gx") * size_z + lax.axis_index("gz")
    peer = lax.rem(place + offset, size_x * size_z)
    return peer, {"gx": peer // size_z, "gz": lax.rem(peer, size_z)}


def column_peer(dims, offset):
    peer = lax.rem(lax.axis_index("gy") + offset, dims[1])
    return peer, {"gy": peer}


def has_neighbour(dims, offset):
    valid = None
    for axis, size, step in zip(AXES, dims, offset):
        if step:
            place = lax.axis_index(axis)
            here = place < size - 1 if step > 0 else place > 0
            valid = here if valid is None else jnp.logical_and(valid, here)
    return valid


def neighbour(offset):
    return {axis: lax.axis_index(axis) + step for axis, step in zip(AXES, offset) if step}


def enter(dims, halo):
    barrier = pltpu.get_barrier_semaphore()

    @pl.loop(1, dims[0] * dims[2])
    def _(k):
        pl.semaphore_signal(barrier, inc=1, device_id=plane_peer(dims, k)[1], device_id_type=MESH)

    @pl.loop(1, dims[1])
    def _(k):
        pl.semaphore_signal(barrier, inc=1, device_id=column_peer(dims, k)[1], device_id_type=MESH)

    if halo:
        for offset in OFFSETS:

            @pl.when(has_neighbour(dims, offset))
            def _():
                pl.semaphore_signal(
                    barrier, inc=1, device_id=neighbour(offset), device_id_type=MESH
                )


def entered(dims, halo):
    count = dims[0] * dims[2] + dims[1] - 2
    if halo:
        boxes = 1
        for axis, size in zip(AXES, dims):
            place = lax.axis_index(axis)
            boxes = boxes * (3 - (place == 0).astype(jnp.int32) - (place == size - 1).astype(jnp.int32))
        count = count + boxes - 1
    pl.semaphore_wait(pltpu.get_barrier_semaphore(), count)


def wait_bytes(ref, sem):
    pltpu.make_async_copy(ref, ref, sem).wait()


def send(src, dst, send_sem, recv_sem, device):
    pltpu.make_async_remote_copy(
        src_ref=src,
        dst_ref=dst,
        send_sem=send_sem,
        recv_sem=recv_sem,
        device_id=device,
        device_id_type=MESH,
    ).start()


def place_of(dims):
    return lax.axis_index("gx") * dims[2] + lax.axis_index("gz")


class AllReduce:
    def __init__(self, dims, local, total, plane_buf, column_buf, sems):
        self.dims, self.local, self.total = dims, local, total
        self.plane_buf, self.column_buf, self.sems = plane_buf, column_buf, sems
        self.plane, self.column = dims[0] * dims[2], dims[1]
        self.rows = local.shape[0] // self.plane
        self.mine = pl.ds(pl.multiple_of(place_of(dims) * self.rows, self.rows), self.rows)

    def scatter(self):
        @pl.loop(1, self.plane)
        def _(k):
            peer, device = plane_peer(self.dims, k)
            theirs = pl.ds(pl.multiple_of(peer * self.rows, self.rows), self.rows)
            send(
                self.local.at[theirs], self.plane_buf.at[k - 1],
                self.sems.at[0], self.sems.at[1], device,
            )

    def across(self):
        level = lax.axis_index("gy")
        wait_bytes(self.plane_buf, self.sems.at[1])
        self.column_buf[level] = lax.fori_loop(
            0, self.plane - 1, lambda k, acc: acc + self.plane_buf[k], self.local[self.mine]
        )
        mine = self.column_buf.at[level]

        @pl.loop(1, self.column)
        def _(k):
            _, device = column_peer(self.dims, k)
            send(mine, mine, self.sems.at[2], self.sems.at[3], device)

    def gather(self):
        wait_bytes(self.column_buf.at[pl.ds(0, self.column - 1)], self.sems.at[3])
        part = self.column_buf[0]
        for k in range(1, self.column):
            part = part + self.column_buf[k]
        self.total[self.mine] = part
        mine = self.total.at[self.mine]

        @pl.loop(1, self.plane)
        def _(k):
            _, device = plane_peer(self.dims, k)
            send(mine, mine, self.sems.at[4], self.sems.at[5], device)

    def finish(self):
        others = self.total.at[pl.ds(0, (self.plane - 1) * self.rows)]
        wait_bytes(others, self.sems.at[5])
        wait_bytes(self.plane_buf, self.sems.at[0])
        wait_bytes(self.column_buf.at[pl.ds(0, self.column - 1)], self.sems.at[2])
        wait_bytes(others, self.sems.at[4])


def reduce_scratch(dims, size):
    plane, column = dims[0] * dims[2], dims[1]
    rows = size // plane
    return [
        pltpu.VMEM((size, size), jnp.float32),
        pltpu.VMEM((size, size), jnp.float32),
        pltpu.VMEM((plane - 1, rows, size), jnp.float32),
        pltpu.VMEM((column, rows, size), jnp.float32),
        pltpu.SemaphoreType.DMA((6,)),
    ]


def max_start(dims, plane_buf, sems):
    plane = dims[0] * dims[2]
    place = lax.axis_index("gx") * dims[2] + lax.axis_index("gz")

    @pl.loop(1, plane)
    def _(k):
        _, device = plane_peer(dims, k)
        send(plane_buf.at[place], plane_buf.at[place], sems.at[0], sems.at[1], device)


def max_middle(dims, plane_buf, column_buf, sems):
    plane, column = dims[0] * dims[2], dims[1]
    level = lax.axis_index("gy")
    wait_bytes(plane_buf.at[pl.ds(0, plane - 1)], sems.at[1])
    column_buf[level] = jnp.max(plane_buf[...], axis=0)

    @pl.loop(1, column)
    def _(k):
        _, device = column_peer(dims, k)
        send(column_buf.at[level], column_buf.at[level], sems.at[2], sems.at[3], device)


def max_end(dims, plane_buf, column_buf, sems):
    plane, column = dims[0] * dims[2], dims[1]
    wait_bytes(column_buf.at[pl.ds(0, column - 1)], sems.at[3])
    wait_bytes(plane_buf.at[pl.ds(0, plane - 1)], sems.at[0])
    wait_bytes(column_buf.at[pl.ds(0, column - 1)], sems.at[2])
    return jnp.max(column_buf[...], axis=0)


def halo_scratch(shape, slots):
    size_x, size_y, size_z, columns = shape
    f32 = jnp.float32
    return [
        pltpu.VMEM((slots, size_x + 2, size_y + 2, size_z, columns), f32),
        pltpu.VMEM((slots, 2, size_x + 2, size_y, columns), f32),
        pltpu.VMEM((slots, 2, 2, size_x, columns), f32),
        pltpu.VMEM((slots, 2, 2, 2, 8, columns), f32),
        pltpu.VMEM((slots, 2, size_x, size_y, columns), f32),
        pltpu.VMEM((slots, 2, 2, size_x, columns), f32),
        pltpu.VMEM((slots, 2, 2, 2, 8, columns), f32),
        pltpu.VMEM((2, size_x + 2, size_y + 2, size_z, columns), f32),
        pltpu.SemaphoreType.DMA((slots, 2, len(OFFSETS))),
    ]


def halo_parts(shape, slot, offset, field, face, edge, corner, face_out, edge_out, corner_out):
    size_x, size_y, _, _ = shape
    sx, sy, sz = offset
    low = {1: 0, -1: 1}

    def ends(step, size):
        if step == 0:
            return pl.ds(1, size), pl.ds(1, size)
        return (size, 0) if step > 0 else (1, size + 1)

    from_x, to_x = ends(sx, size_x)
    from_y, to_y = ends(sy, size_y)
    if sz == 0:
        return field.at[slot, from_x, from_y], field.at[slot, to_x, to_y]
    top = 1 if sz > 0 else 0
    if sy == 0:
        source = pl.ds(0, size_x) if sx == 0 else from_x - 1
        return face_out.at[slot, top, source], face.at[slot, 1 - top, to_x]
    far = 1 if sy > 0 else 0
    if sx == 0:
        return edge_out.at[slot, top, far], edge.at[slot, 1 - top, 1 - far]
    right = 1 if sx > 0 else 0
    return (
        corner_out.at[slot, top, far, right],
        corner.at[slot, 1 - top, 1 - far, 1 - right],
    )


def zero_border(dims, shape, slots, field, face, edge, corner):
    size_x, size_y, size_z, columns = shape
    for slot in range(slots):
        for side in (0, 1):
            step = 1 if side else -1
            row = size_x + 1 if side else 0

            @pl.when(jnp.logical_not(has_neighbour(dims, (step, 0, 0))))
            def _():
                field[slot, row] = jnp.zeros((size_y + 2, size_z, columns), jnp.float32)
                for top in (0, 1):
                    face[slot, top, row] = jnp.zeros((size_y, columns), jnp.float32)
                    for far in (0, 1):
                        corner[slot, top, far, side] = jnp.zeros((8, columns), jnp.float32)

            row_y = size_y + 1 if side else 0

            @pl.when(jnp.logical_not(has_neighbour(dims, (0, step, 0))))
            def _():
                field[slot, :, row_y] = jnp.zeros((size_x + 2, size_z, columns), jnp.float32)
                for top in (0, 1):
                    edge[slot, top, side] = jnp.zeros((size_x, columns), jnp.float32)
                    for right in (0, 1):
                        corner[slot, top, side, right] = jnp.zeros((8, columns), jnp.float32)

            @pl.when(jnp.logical_not(has_neighbour(dims, (0, 0, step))))
            def _():
                face[slot, side] = jnp.zeros((size_x + 2, size_y, columns), jnp.float32)
                edge[slot, side] = jnp.zeros((2, size_x, columns), jnp.float32)
                corner[slot, side] = jnp.zeros((2, 2, 8, columns), jnp.float32)


def pack_column(shape, slot, x, y, value, face_out, edge_out):
    size_y, size_z = shape[1], shape[2]
    for top, z in ((0, 0), (1, size_z - 1)):
        row = value[z : z + 1]
        face_out[slot, top, x, y : y + 1] = row
        if y in (0, size_y - 1):
            edge_out[slot, top, 1 if y else 0, pl.ds(x, 1)] = row


def pack_corners(shape, slot, field, corner_out):
    size_x, size_y, size_z, columns = shape
    for top in (0, 1):
        for far in (0, 1):
            for right in (0, 1):
                z = (size_z - 1) * top
                corner_out[slot, top, far, right] = jnp.broadcast_to(
                    field[slot, size_x if right else 1, size_y if far else 1, z : z + 1],
                    (8, columns),
                )


def halo_send(dims, shape, slot, refs, sems):
    for index, offset in enumerate(OFFSETS):

        @pl.when(has_neighbour(dims, offset))
        def _():
            src, dst = halo_parts(shape, slot, offset, *refs)
            send(src, dst, sems.at[slot, 0, index], sems.at[slot, 1, index], neighbour(offset))


def halo_wait(dims, shape, slot, refs, sems, received):
    for index, offset in enumerate(OFFSETS):
        from_there = tuple(-step for step in offset)

        @pl.when(has_neighbour(dims, from_there if received else offset))
        def _():
            src, dst = halo_parts(shape, slot, offset, *refs)
            if received:
                wait_bytes(dst, sems.at[slot, 1, index])
            else:
                wait_bytes(src, sems.at[slot, 0, index])


def shift_columns(shape, slot, field, face, edge, corner, shifted):
    size_x, size_y, size_z, columns = shape
    place = lax.broadcasted_iota(jnp.int32, (size_z, columns), 0)

    def put(x, y, below, above):
        value = field[slot, x, y]
        shifted[0, x, y] = jnp.where(place == 0, below, pltpu.roll(value, 1, 0))
        shifted[1, x, y] = jnp.where(place == size_z - 1, above, pltpu.roll(value, size_z - 1, 0))

    @pl.loop(0, size_x + 2)
    def _(x):
        for y in range(size_y):
            put(x, y + 1, face[slot, 0, x, y : y + 1], face[slot, 1, x, y : y + 1])

    for far in (0, 1):
        y = size_y + 1 if far else 0

        @pl.loop(0, size_x)
        def _(x):
            put(x + 1, y, edge[slot, 0, far, pl.ds(x, 1)], edge[slot, 1, far, pl.ds(x, 1)])

        for right in (0, 1):
            x = size_x + 1 if right else 0
            put(x, y, corner[slot, 0, far, right], corner[slot, 1, far, right])


def apply_rows(shape, slot, x, field, shifted, onsite, hopping):
    size_y = shape[1]
    totals = [None] * size_y
    centres = [None] * size_y
    for dx in (-1, 0, 1):
        for y in range(-1, size_y + 1):
            for dz in (-1, 0, 1):
                if dz == 0:
                    value = field[slot, x + 1 + dx, y + 1]
                else:
                    value = shifted[0 if dz < 0 else 1, x + 1 + dx, y + 1]
                for dy in (-1, 0, 1):
                    target = y - dy
                    if not 0 <= target < size_y:
                        continue
                    if (dx, dy, dz) == (0, 0, 0):
                        centres[target] = value
                        level = onsite[x, target]
                        term = level * value
                    else:
                        term = hopping[hop_index((dx, dy, dz))] * value
                    totals[target] = term if totals[target] is None else totals[target] + term
    return totals, centres


def spread(onsite, levels):
    size_x, size_y, size_z, lanes = levels.shape
    diagonal = lax.broadcasted_iota(jnp.int32, (size_z, size_z), 0) == lax.broadcasted_iota(
        jnp.int32, (size_z, size_z), 1
    )

    @pl.loop(0, size_x)
    def _(x):
        for y in range(size_y):
            row = jnp.broadcast_to(onsite[x, y : y + 1], (size_z, size_z))
            column = jnp.sum(jnp.where(diagonal, row, 0.0), axis=1, keepdims=True)
            levels[x, y] = jnp.broadcast_to(column, (size_z, lanes))


def filter_coefficients(bound, cut_frac, coef):
    cut = cut_frac * bound
    half_width = (bound - cut) / 2.0
    center = (bound + cut) / 2.0
    sigma_one = half_width / (-bound - center)
    sigma = sigma_one
    coef[0] = center
    coef[1] = sigma / half_width
    for k in range(1, DEG):
        sigma_next = 1.0 / (2.0 / sigma_one - sigma)
        coef[2 * k] = 2.0 * sigma_next / half_width
        coef[2 * k + 1] = sigma * sigma_next
        sigma = sigma_next


def filter_kernel(
    dims, shape, sites,
    block, onsite, hopping, cut_frac,
    first, gram_two, between, lower,
    *scratch,
):
    size_x, size_y, size_z, lanes = shape
    per_half = HALO_REFS
    halves = []
    for half in range(HALVES):
        *refs, shifted, sems = scratch[half * per_half : (half + 1) * per_half]
        halves.append((tuple(refs), shifted, sems))
    (
        onsite_here, levels, input_sems,
        max_plane, max_column, max_sems, coef,
        flat, image, moved, gram, inverse, work,
        *sum_refs,
    ) = scratch[HALVES * per_half :]
    early = moved
    copies = [pltpu.make_async_copy(onsite, onsite_here, input_sems.at[HALVES])]
    for half, (refs, _, _) in enumerate(halves):
        inside = refs[0].at[0, pl.ds(1, size_x), pl.ds(1, size_y)]
        source = block.at[:, :, :, pl.ds(lanes * half, lanes)]
        copies.append(pltpu.make_async_copy(source, inside, input_sems.at[half]))
    for copy in copies:
        copy.start()
    enter(dims, True)
    for copy, (refs, _, _) in zip(copies[1:], halves):
        copy.wait()
        field, face_out, edge_out, corner_out = refs[0], *refs[4:]

        @pl.loop(0, size_x)
        def _(x):
            for y in range(size_y):
                pack_column(shape, 0, x, y, field[0, x + 1, y + 1], face_out, edge_out)

        pack_corners(shape, 0, field, corner_out)
    copies[0].wait()
    place = place_of(dims)
    max_plane[place] = jnp.full((8, 128), jnp.max(jnp.abs(onsite_here[...])), jnp.float32)
    entered(dims, True)
    for refs, _, sems in halves:
        halo_send(dims, shape, 0, refs, sems)
    max_start(dims, max_plane, max_sems)
    for refs, _, _ in halves:
        zero_border(dims, shape, 2, *refs[:4])
    spread(onsite_here, levels)
    for step in range(DEG):
        slot, after = step % 2, (step + 1) % 2
        for half, (refs, shifted, sems) in enumerate(halves):
            field, face, edge, corner, face_out, edge_out, corner_out = refs
            halo_wait(dims, shape, slot, refs, sems, True)
            shift_columns(shape, slot, field, face, edge, corner, shifted)
            if step == 1 and half == 0:
                reach = jnp.abs(hopping[0])
                for k in range(1, len(POSITIVE)):
                    reach = reach + jnp.abs(hopping[k])
                bound = max_end(dims, max_plane, max_column, max_sems) + 2.0 * reach
                filter_coefficients(bound, cut_frac[0], coef)

            @pl.loop(0, size_x)
            def _(x):
                totals, centres = apply_rows(shape, slot, x, field, shifted, levels, hopping)
                for y in range(size_y):
                    mine = (site_rows(shape, x, y), slice(lanes * half, lanes * (half + 1)))
                    value = totals[y]
                    if step == 1:
                        older = field[after, x + 1, y + 1]
                        newer = coef[1] * (centres[y] - coef[0] * older)
                        early[mine] = newer
                        value = coef[1] * (value - coef[0] * centres[y])
                    elif step > 1:
                        newer = centres[y]
                        older = early[mine] if step == 2 else field[after, x + 1, y + 1]
                    if step:
                        value = coef[2 * step] * (value - coef[0] * newer)
                        value = value - coef[2 * step + 1] * older
                    if step == DEG - 1:
                        flat[mine] = value
                    field[after, x + 1, y + 1] = value
                    pack_column(shape, after, x, y, value, face_out, edge_out)

            pack_corners(shape, after, field, corner_out)
            halo_send(dims, shape, after, refs, sems)
            halo_wait(dims, shape, slot, refs, sems, False)
            if step == 0 and half == 0:
                max_middle(dims, max_plane, max_column, max_sems)
    slot = DEG % 2
    per_sum = len(sum_refs) // 3
    sums, sums_two, sums_between = [
        AllReduce(dims, *sum_refs[k * per_sum : (k + 1) * per_sum]) for k in range(3)
    ]
    sums.local[...] = product(flat[...], flat[...])
    sums.scatter()
    for refs, shifted, sems in halves:
        halo_wait(dims, shape, slot, refs, sems, True)
        shift_columns(shape, slot, *refs[:4], shifted)
    sums.across()
    for half, (refs, shifted, sems) in enumerate(halves):

        @pl.loop(0, size_x)
        def _(x):
            totals, _ = apply_rows(shape, slot, x, refs[0], shifted, levels, hopping)
            for y in range(size_y):
                image[site_rows(shape, x, y), lanes * half : lanes * (half + 1)] = totals[y]

    sums.gather()
    for refs, _, sems in halves:
        halo_wait(dims, shape, slot, refs, sems, False)
    sums.finish()
    gram[...] = sums.total[...] / sites
    factor_kernel(PANEL, gram, lower, inverse, work)
    rotate_and_sum(
        dims, sites, flat, image, inverse, first, gram_two, between, moved, sums_two, sums_between
    )


def site_rows(shape, x, y):
    _, size_y, size_z, _ = shape
    return pl.ds(pl.multiple_of((x * size_y + y) * size_z, size_z), size_z)


def product(left, right):
    return lax.dot_general(
        left,
        right,
        (((0,), (0,)), ((), ())),
        precision=HIGHEST,
        preferred_element_type=jnp.float32,
    )


def rotated(flat, factor):
    return lax.dot_general(
        flat,
        factor,
        (((1,), (1,)), ((), ())),
        precision=HIGHEST,
        preferred_element_type=jnp.float32,
    )


def rotate_and_sum(dims, sites, flat, image, inverse, first, gram, between, moved, sums, sums_b):
    first[...] = rotated(flat[...], inverse[...])
    sums.local[...] = product(first[...], first[...])
    sums.scatter()
    moved[...] = rotated(image[...], inverse[...])
    sums_b.local[...] = product(first[...], moved[...])
    sums_b.scatter()
    sums.across()
    sums_b.across()
    sums.gather()
    sums_b.gather()
    sums.finish()
    gram[...] = sums.total[...] / sites
    sums_b.finish()
    between[...] = sums_b.total[...] / sites


def call(kernel, inputs, scalars, outputs, scratch, ident, space=pltpu.VMEM):
    vmem = pl.BlockSpec(memory_space=pltpu.VMEM)
    smem = pl.BlockSpec(memory_space=pltpu.SMEM)
    return pl.pallas_call(
        kernel,
        out_shape=[jax.ShapeDtypeStruct(shape, jnp.float32) for shape in outputs],
        in_specs=[pl.BlockSpec(memory_space=space)] * len(inputs) + [smem] * len(scalars),
        out_specs=[vmem] * len(outputs),
        scratch_shapes=scratch,
        compiler_params=pltpu.CompilerParams(
            collective_id=ident, has_side_effects=True, vmem_limit_bytes=48 << 20
        ),
    )(*inputs, *scalars)


def factor_kernel(nb, gram, lower, inverse, work):
    size = gram.shape[0]
    tiles = size // 128
    groups = nb // 8
    lane = lax.broadcasted_iota(jnp.int32, (8, 128), 1)
    sub = lax.broadcasted_iota(jnp.int32, (8, 128), 0)
    for t in range(tiles):
        work[t] = gram[:, 128 * t : 128 * (t + 1)]
    for t in range(tiles):
        r = lax.broadcasted_iota(jnp.int32, (size, 128), 0)
        c = lax.broadcasted_iota(jnp.int32, (size, 128), 1) + 128 * t
        work[tiles + t] = jnp.where(r == c, 1.0, 0.0)

    def row(v, j):
        return jnp.broadcast_to(v[j % 8 : j % 8 + 1], (8, 128))

    for start in range(0, size, nb):
        stop = start + nb
        active = [t for t in range(tiles) if 128 * (t + 1) > start]
        active += [tiles + t for t in range(tiles) if 128 * t < stop]
        home = start // 128
        panel = {
            t: [work[t, start + 8 * g : start + 8 * g + 8] for g in range(groups)] for t in active
        }
        cols = [
            [
                jnp.broadcast_to(
                    panel[home][g][:, start % 128 + k : start % 128 + k + 1], (8, 128)
                )
                for g in range(groups)
            ]
            for k in range(nb)
        ]
        recip = [jnp.ones((8, 128), jnp.float32)] * groups
        pivots = [jnp.ones((8, 128), jnp.float32)] * groups
        for j in range(nb):
            home_group = j // 8
            pivot = row(cols[j][home_group], j)
            inv = 1.0 / pivot
            at = sub == j % 8
            recip[home_group] = jnp.where(at, inv, recip[home_group])
            pivots[home_group] = jnp.where(at, pivot, pivots[home_group])
            mult = [None] * groups
            for g in range(home_group, groups):
                mult[g] = cols[j][g] * inv
                if g == home_group:
                    mult[g] = jnp.where(sub > j % 8, mult[g], 0.0)
            for k in range(j + 1, nb):
                top = row(cols[k][home_group], j)
                for g in range(home_group, groups):
                    cols[k][g] = cols[k][g] - mult[g] * top
            for t in active:
                top = row(panel[t][home_group], j)
                for g in range(home_group, groups):
                    panel[t][g] = panel[t][g] - mult[g] * top
        if stop < size:
            full = {t: jnp.concatenate(panel[t], 0) if groups > 1 else panel[t][0] for t in active}
            recips = jnp.concatenate(recip, 0) if groups > 1 else recip[0]
            chunks = [(stop, stop + nb)] + [
                (max(128 * u, stop + nb), 128 * (u + 1)) for u in range(tiles)
            ]
            for low, high in chunks:
                if low >= high:
                    continue
                u = low // 128
                left = (full[u] * recips)[:, low - 128 * u : high - 128 * u]
                for t in active:
                    if t < u:
                        continue
                    work[t, low:high] -= lax.dot_general(
                        left, full[t], (((0,), (0,)), ((), ())),
                        precision=HIGHEST, preferred_element_type=jnp.float32)
        for g in range(groups):
            scale = 1.0 / jnp.sqrt(pivots[g])
            at = slice(start + 8 * g, start + 8 * g + 8)
            for t in range(tiles):
                if t in active:
                    keep = lane + 128 * t >= sub + (start + 8 * g)
                    work[t, at] = jnp.where(keep, panel[t][g] * scale, 0.0)
                else:
                    work[t, at] = jnp.zeros((8, 128), jnp.float32)
                if tiles + t in active:
                    inverse[at, 128 * t : 128 * t + 128] = panel[tiles + t][g] * scale
                else:
                    inverse[at, 128 * t : 128 * t + 128] = jnp.zeros((8, 128), jnp.float32)
    for t in range(tiles):
        lower[128 * t : 128 * t + 128, :] = work[t].T

def near_identity_kernel(gram, inverse):
    size = gram.shape[0]
    row = lax.broadcasted_iota(jnp.int32, (size, size), 0)
    col = lax.broadcasted_iota(jnp.int32, (size, size), 1)
    ident = jnp.where(row == col, 1.0, 0.0)
    weight = jnp.where(row > col, 1.0, 0.5 * ident)

    def times(left, right, across):
        return lax.dot_general(
            left, right, (((1,), (across,)), ((), ())),
            precision=HIGHEST, preferred_element_type=jnp.float32,
        )

    error = gram[...] - ident
    shift = None
    for step in range(NEAR_STEPS):
        low = weight * error
        shift = low if shift is None else shift + low - times(low, shift, 0)
        if step < NEAR_STEPS - 1:
            cross = times(low, error, 0)
            error = times(low + cross, low, 1) - cross - cross.T
    inverse[...] = ident - shift
    return jnp.sum(error * error)


def finish_kernel(
    nb, gram, first, between, lower_one, states, projected, factor, lower, inverse, work
):
    factor[...] = lower_one[...]
    left = near_identity_kernel(gram, inverse)

    @pl.when(jnp.logical_not(left < NEAR_LEFT * NEAR_LEFT))
    def _():
        factor_kernel(nb, gram, lower, inverse, work)

    states[...] = rotated(first[...], inverse[...])
    half = rotated(between[...], inverse[...])
    projected[...] = jnp.dot(
        inverse[...], half, precision=HIGHEST, preferred_element_type=jnp.float32
    )


def local_call(kernel, inputs, outputs, scratch):
    vmem = pl.BlockSpec(memory_space=pltpu.VMEM)
    return pl.pallas_call(
        kernel,
        out_shape=[jax.ShapeDtypeStruct(shape, jnp.float32) for shape in outputs],
        in_specs=[vmem] * len(inputs),
        out_specs=[vmem] * len(outputs),
        scratch_shapes=scratch,
        compiler_params=pltpu.CompilerParams(vmem_limit_bytes=32 << 20),
    )(*inputs)


def body(dims, block, onsite, hopping, cut_frac):
    shape = block.shape
    size_x, size_y, size_z, columns = shape
    count = size_x * size_y * size_z
    sites = count * dims[0] * dims[1] * dims[2]
    plane, column = dims[0] * dims[2], dims[1]
    sums = reduce_scratch(dims, columns)
    square = (columns, columns)
    work = pltpu.VMEM((2 * (columns // 128), columns, 128), jnp.float32)
    lanes = columns // HALVES
    part = (size_x, size_y, size_z, lanes)
    first, gram_two, between, lower_one = call(
        functools.partial(filter_kernel, dims, part, sites),
        [pltpu.with_memory_space_constraint(v, pltpu.HBM) for v in (block, onsite)],
        [hopping, cut_frac],
        [(count, columns), square, square, square],
        halo_scratch(part, 2) * HALVES
        + [
            pltpu.VMEM((size_x, size_y, size_z), jnp.float32),
            pltpu.VMEM(part, jnp.float32),
            pltpu.SemaphoreType.DMA((HALVES + 1,)),
            pltpu.VMEM((plane, 8, 128), jnp.float32),
            pltpu.VMEM((column, 8, 128), jnp.float32),
            pltpu.SemaphoreType.DMA((4,)),
            pltpu.VMEM((2 * DEG, 8, 128), jnp.float32),
        ]
        + [pltpu.VMEM((count, columns), jnp.float32)] * 3
        + [pltpu.VMEM(square, jnp.float32)] * 2
        + [work]
        + sums * 3,
        1,
        pltpu.HBM,
    )
    states, projected, factor = local_call(
        functools.partial(finish_kernel, PANEL),
        [gram_two, first, between, lower_one],
        [(count, columns), square, square],
        [pltpu.VMEM(square, jnp.float32), pltpu.VMEM(square, jnp.float32), work],
    )
    return (states.reshape(shape), projected, factor)


def solution(mesh):
    dims = (mesh.shape["gx"], mesh.shape["gy"], mesh.shape["gz"])
    return jax.shard_map(
        functools.partial(body, dims),
        mesh=mesh,
        in_specs=(P("gx", "gy", "gz", None), P("gx", "gy", "gz"), P(), P()),
        out_specs=(P("gx", "gy", "gz", None), P(), P()),
        check_vma=False,
    )
```

```python
import functools

import jax
import jax.numpy as jnp
from jax import lax
from jax.experimental import pallas as pl
from jax.experimental.pallas import tpu as pltpu
from jax.sharding import PartitionSpec as P

DEG = 4
PANEL = 16
NEAR_STEPS = 4
NEAR_LEFT = 1e-3
HALVES = 2
HALO_REFS = 9
MESH = pl.DeviceIdType.MESH
HIGHEST = lax.Precision.HIGHEST
AXES = ("gx", "gy", "gz")
OFFSETS = [
    (dx, dy, dz)
    for dx in (-1, 0, 1)
    for dy in (-1, 0, 1)
    for dz in (-1, 0, 1)
    if (dx, dy, dz) != (0, 0, 0)
]
POSITIVE = [offset for offset in OFFSETS if offset > (0, 0, 0)]


def hop_index(offset):
    return POSITIVE.index(max(offset, tuple(-d for d in offset)))


def plane_peer(dims, offset):
    size_x, _, size_z = dims
    place = lax.axis_index("gx") * size_z + lax.axis_index("gz")
    peer = lax.rem(place + offset, size_x * size_z)
    return peer, {"gx": peer // size_z, "gz": lax.rem(peer, size_z)}


def column_peer(dims, offset):
    peer = lax.rem(lax.axis_index("gy") + offset, dims[1])
    return peer, {"gy": peer}


def has_neighbour(dims, offset):
    valid = None
    for axis, size, step in zip(AXES, dims, offset):
        if step:
            place = lax.axis_index(axis)
            here = place < size - 1 if step > 0 else place > 0
            valid = here if valid is None else jnp.logical_and(valid, here)
    return valid


def neighbour(offset):
    return {axis: lax.axis_index(axis) + step for axis, step in zip(AXES, offset) if step}


def enter(dims, halo):
    barrier = pltpu.get_barrier_semaphore()

    @pl.loop(1, dims[0] * dims[2])
    def _(k):
        pl.semaphore_signal(barrier, inc=1, device_id=plane_peer(dims, k)[1], device_id_type=MESH)

    @pl.loop(1, dims[1])
    def _(k):
        pl.semaphore_signal(barrier, inc=1, device_id=column_peer(dims, k)[1], device_id_type=MESH)

    if halo:
        for offset in OFFSETS:

            @pl.when(has_neighbour(dims, offset))
            def _():
                pl.semaphore_signal(
                    barrier, inc=1, device_id=neighbour(offset), device_id_type=MESH
                )


def entered(dims, halo):
    count = dims[0] * dims[2] + dims[1] - 2
    if halo:
        boxes = 1
        for axis, size in zip(AXES, dims):
            place = lax.axis_index(axis)
            boxes = boxes * (3 - (place == 0).astype(jnp.int32) - (place == size - 1).astype(jnp.int32))
        count = count + boxes - 1
    pl.semaphore_wait(pltpu.get_barrier_semaphore(), count)


def wait_bytes(ref, sem):
    pltpu.make_async_copy(ref, ref, sem).wait()


def send(src, dst, send_sem, recv_sem, device):
    pltpu.make_async_remote_copy(
        src_ref=src,
        dst_ref=dst,
        send_sem=send_sem,
        recv_sem=recv_sem,
        device_id=device,
        device_id_type=MESH,
    ).start()


def place_of(dims):
    return lax.axis_index("gx") * dims[2] + lax.axis_index("gz")


class AllReduce:
    def __init__(self, dims, local, total, plane_buf, column_buf, sems):
        self.dims, self.local, self.total = dims, local, total
        self.plane_buf, self.column_buf, self.sems = plane_buf, column_buf, sems
        self.plane, self.column = dims[0] * dims[2], dims[1]
        self.rows = local.shape[0] // self.plane
        self.mine = pl.ds(pl.multiple_of(place_of(dims) * self.rows, self.rows), self.rows)

    def scatter(self):
        @pl.loop(1, self.plane)
        def _(k):
            peer, device = plane_peer(self.dims, k)
            theirs = pl.ds(pl.multiple_of(peer * self.rows, self.rows), self.rows)
            send(
                self.local.at[theirs], self.plane_buf.at[k - 1],
                self.sems.at[0], self.sems.at[1], device,
            )

    def across(self):
        level = lax.axis_index("gy")
        wait_bytes(self.plane_buf, self.sems.at[1])
        self.column_buf[level] = lax.fori_loop(
            0, self.plane - 1, lambda k, acc: acc + self.plane_buf[k], self.local[self.mine]
        )
        mine = self.column_buf.at[level]

        @pl.loop(1, self.column)
        def _(k):
            _, device = column_peer(self.dims, k)
            send(mine, mine, self.sems.at[2], self.sems.at[3], device)

    def gather(self):
        wait_bytes(self.column_buf.at[pl.ds(0, self.column - 1)], self.sems.at[3])
        part = self.column_buf[0]
        for k in range(1, self.column):
            part = part + self.column_buf[k]
        self.total[self.mine] = part
        mine = self.total.at[self.mine]

        @pl.loop(1, self.plane)
        def _(k):
            _, device = plane_peer(self.dims, k)
            send(mine, mine, self.sems.at[4], self.sems.at[5], device)

    def finish(self):
        others = self.total.at[pl.ds(0, (self.plane - 1) * self.rows)]
        wait_bytes(others, self.sems.at[5])
        wait_bytes(self.plane_buf, self.sems.at[0])
        wait_bytes(self.column_buf.at[pl.ds(0, self.column - 1)], self.sems.at[2])
        wait_bytes(others, self.sems.at[4])


def reduce_scratch(dims, size):
    plane, column = dims[0] * dims[2], dims[1]
    rows = size // plane
    return [
        pltpu.VMEM((size, size), jnp.float32),
        pltpu.VMEM((size, size), jnp.float32),
        pltpu.VMEM((plane - 1, rows, size), jnp.float32),
        pltpu.VMEM((column, rows, size), jnp.float32),
        pltpu.SemaphoreType.DMA((6,)),
    ]


def max_start(dims, plane_buf, sems):
    plane = dims[0] * dims[2]
    place = lax.axis_index("gx") * dims[2] + lax.axis_index("gz")

    @pl.loop(1, plane)
    def _(k):
        _, device = plane_peer(dims, k)
        send(plane_buf.at[place], plane_buf.at[place], sems.at[0], sems.at[1], device)


def max_middle(dims, plane_buf, column_buf, sems):
    plane, column = dims[0] * dims[2], dims[1]
    level = lax.axis_index("gy")
    wait_bytes(plane_buf.at[pl.ds(0, plane - 1)], sems.at[1])
    column_buf[level] = jnp.max(plane_buf[...], axis=0)

    @pl.loop(1, column)
    def _(k):
        _, device = column_peer(dims, k)
        send(column_buf.at[level], column_buf.at[level], sems.at[2], sems.at[3], device)


def max_end(dims, plane_buf, column_buf, sems):
    plane, column = dims[0] * dims[2], dims[1]
    wait_bytes(column_buf.at[pl.ds(0, column - 1)], sems.at[3])
    wait_bytes(plane_buf.at[pl.ds(0, plane - 1)], sems.at[0])
    wait_bytes(column_buf.at[pl.ds(0, column - 1)], sems.at[2])
    return jnp.max(column_buf[...], axis=0)


def halo_scratch(shape, slots):
    size_x, size_y, size_z, columns = shape
    f32 = jnp.float32
    return [
        pltpu.VMEM((slots, size_x + 2, size_y + 2, size_z, columns), f32),
        pltpu.VMEM((slots, 2, size_x + 2, size_y, columns), f32),
        pltpu.VMEM((slots, 2, 2, size_x, columns), f32),
        pltpu.VMEM((slots, 2, 2, 2, 8, columns), f32),
        pltpu.VMEM((slots, 2, size_x, size_y, columns), f32),
        pltpu.VMEM((slots, 2, 2, size_x, columns), f32),
        pltpu.VMEM((slots, 2, 2, 2, 8, columns), f32),
        pltpu.VMEM((2, size_x + 2, size_y + 2, size_z, columns), f32),
        pltpu.SemaphoreType.DMA((slots, 2, len(OFFSETS))),
    ]


def halo_parts(shape, slot, offset, field, face, edge, corner, face_out, edge_out, corner_out):
    size_x, size_y, _, _ = shape
    sx, sy, sz = offset
    low = {1: 0, -1: 1}

    def ends(step, size):
        if step == 0:
            return pl.ds(1, size), pl.ds(1, size)
        return (size, 0) if step > 0 else (1, size + 1)

    from_x, to_x = ends(sx, size_x)
    from_y, to_y = ends(sy, size_y)
    if sz == 0:
        return field.at[slot, from_x, from_y], field.at[slot, to_x, to_y]
    top = 1 if sz > 0 else 0
    if sy == 0:
        source = pl.ds(0, size_x) if sx == 0 else from_x - 1
        return face_out.at[slot, top, source], face.at[slot, 1 - top, to_x]
    far = 1 if sy > 0 else 0
    if sx == 0:
        return edge_out.at[slot, top, far], edge.at[slot, 1 - top, 1 - far]
    right = 1 if sx > 0 else 0
    return (
        corner_out.at[slot, top, far, right],
        corner.at[slot, 1 - top, 1 - far, 1 - right],
    )


def zero_border(dims, shape, slots, field, face, edge, corner):
    size_x, size_y, size_z, columns = shape
    for slot in range(slots):
        for side in (0, 1):
            step = 1 if side else -1
            row = size_x + 1 if side else 0

            @pl.when(jnp.logical_not(has_neighbour(dims, (step, 0, 0))))
            def _():
                field[slot, row] = jnp.zeros((size_y + 2, size_z, columns), jnp.float32)
                for top in (0, 1):
                    face[slot, top, row] = jnp.zeros((size_y, columns), jnp.float32)
                    for far in (0, 1):
                        corner[slot, top, far, side] = jnp.zeros((8, columns), jnp.float32)

            row_y = size_y + 1 if side else 0

            @pl.when(jnp.logical_not(has_neighbour(dims, (0, step, 0))))
            def _():
                field[slot, :, row_y] = jnp.zeros((size_x + 2, size_z, columns), jnp.float32)
                for top in (0, 1):
                    edge[slot, top, side] = jnp.zeros((size_x, columns), jnp.float32)
                    for right in (0, 1):
                        corner[slot, top, side, right] = jnp.zeros((8, columns), jnp.float32)

            @pl.when(jnp.logical_not(has_neighbour(dims, (0, 0, step))))
            def _():
                face[slot, side] = jnp.zeros((size_x + 2, size_y, columns), jnp.float32)
                edge[slot, side] = jnp.zeros((2, size_x, columns), jnp.float32)
                corner[slot, side] = jnp.zeros((2, 2, 8, columns), jnp.float32)


def pack_column(shape, slot, x, y, value, face_out, edge_out):
    size_y, size_z = shape[1], shape[2]
    for top, z in ((0, 0), (1, size_z - 1)):
        row = value[z : z + 1]
        face_out[slot, top, x, y : y + 1] = row
        if y in (0, size_y - 1):
            edge_out[slot, top, 1 if y else 0, pl.ds(x, 1)] = row


def pack_corners(shape, slot, field, corner_out):
    size_x, size_y, size_z, columns = shape
    for top in (0, 1):
        for far in (0, 1):
            for right in (0, 1):
                z = (size_z - 1) * top
                corner_out[slot, top, far, right] = jnp.broadcast_to(
                    field[slot, size_x if right else 1, size_y if far else 1, z : z + 1],
                    (8, columns),
                )


def halo_send(dims, shape, slot, refs, sems):
    for index, offset in enumerate(OFFSETS):

        @pl.when(has_neighbour(dims, offset))
        def _():
            src, dst = halo_parts(shape, slot, offset, *refs)
            send(src, dst, sems.at[slot, 0, index], sems.at[slot, 1, index], neighbour(offset))


def halo_wait(dims, shape, slot, refs, sems, received):
    for index, offset in enumerate(OFFSETS):
        from_there = tuple(-step for step in offset)

        @pl.when(has_neighbour(dims, from_there if received else offset))
        def _():
            src, dst = halo_parts(shape, slot, offset, *refs)
            if received:
                wait_bytes(dst, sems.at[slot, 1, index])
            else:
                wait_bytes(src, sems.at[slot, 0, index])


def shift_columns(shape, slot, field, face, edge, corner, shifted):
    size_x, size_y, size_z, columns = shape
    place = lax.broadcasted_iota(jnp.int32, (size_z, columns), 0)

    def put(x, y, below, above):
        value = field[slot, x, y]
        shifted[0, x, y] = jnp.where(place == 0, below, pltpu.roll(value, 1, 0))
        shifted[1, x, y] = jnp.where(place == size_z - 1, above, pltpu.roll(value, size_z - 1, 0))

    def row(x, y):
        return face[slot, 0, x, y : y + 1], face[slot, 1, x, y : y + 1]

    for x in (0, size_x + 1):
        for y in range(size_y):
            put(x, y + 1, *row(x, y))

    @pl.loop(1, size_x + 1)
    def _(x):
        for y in range(size_y):
            below, above = row(x, y)
            shifted[0, x, y + 1, 0:1] = below
            shifted[1, x, y + 1, size_z - 1 : size_z] = above

    for far in (0, 1):
        y = size_y + 1 if far else 0

        @pl.loop(0, size_x)
        def _(x):
            put(x + 1, y, edge[slot, 0, far, pl.ds(x, 1)], edge[slot, 1, far, pl.ds(x, 1)])

        for right in (0, 1):
            x = size_x + 1 if right else 0
            put(x, y, corner[slot, 0, far, right], corner[slot, 1, far, right])


def shift_inside(shape, slot, field, shifted):
    size_x, size_y, size_z, _ = shape

    @pl.loop(1, size_x + 1)
    def _(x):
        for y in range(1, size_y + 1):
            value = field[slot, x, y]
            shifted[0, x, y] = pltpu.roll(value, 1, 0)
            shifted[1, x, y] = pltpu.roll(value, size_z - 1, 0)


def apply_rows(shape, slot, x, field, shifted, onsite, hopping):
    size_y = shape[1]
    totals = [None] * size_y
    centres = [None] * size_y
    for dx in (-1, 0, 1):
        for y in range(-1, size_y + 1):
            for dz in (-1, 0, 1):
                if dz == 0:
                    value = field[slot, x + 1 + dx, y + 1]
                else:
                    value = shifted[0 if dz < 0 else 1, x + 1 + dx, y + 1]
                for dy in (-1, 0, 1):
                    target = y - dy
                    if not 0 <= target < size_y:
                        continue
                    if (dx, dy, dz) == (0, 0, 0):
                        centres[target] = value
                        level = onsite[x, target]
                        term = level * value
                    else:
                        term = hopping[hop_index((dx, dy, dz))] * value
                    totals[target] = term if totals[target] is None else totals[target] + term
    return totals, centres


def spread(onsite, levels):
    size_x, size_y, size_z, lanes = levels.shape
    diagonal = lax.broadcasted_iota(jnp.int32, (size_z, size_z), 0) == lax.broadcasted_iota(
        jnp.int32, (size_z, size_z), 1
    )

    @pl.loop(0, size_x)
    def _(x):
        for y in range(size_y):
            row = jnp.broadcast_to(onsite[x, y : y + 1], (size_z, size_z))
            column = jnp.sum(jnp.where(diagonal, row, 0.0), axis=1, keepdims=True)
            levels[x, y] = jnp.broadcast_to(column, (size_z, lanes))


def filter_coefficients(bound, cut_frac, coef):
    cut = cut_frac * bound
    half_width = (bound - cut) / 2.0
    center = (bound + cut) / 2.0
    sigma_one = half_width / (-bound - center)
    sigma = sigma_one
    coef[0] = center
    coef[1] = sigma / half_width
    for k in range(1, DEG):
        sigma_next = 1.0 / (2.0 / sigma_one - sigma)
        coef[2 * k] = 2.0 * sigma_next / half_width
        coef[2 * k + 1] = sigma * sigma_next
        sigma = sigma_next


def filter_kernel(
    dims, shape, sites,
    block, onsite, hopping, cut_frac,
    first, gram_two, between, lower,
    *scratch,
):
    size_x, size_y, size_z, lanes = shape
    per_half = HALO_REFS
    halves = []
    for half in range(HALVES):
        *refs, shifted, sems = scratch[half * per_half : (half + 1) * per_half]
        halves.append((tuple(refs), shifted, sems))
    (
        onsite_here, levels, input_sems,
        max_plane, max_column, max_sems, coef,
        flat, image, moved, gram, inverse, work,
        *sum_refs,
    ) = scratch[HALVES * per_half :]
    early = moved
    copies = [pltpu.make_async_copy(onsite, onsite_here, input_sems.at[HALVES])]
    for half, (refs, _, _) in enumerate(halves):
        inside = refs[0].at[0, pl.ds(1, size_x), pl.ds(1, size_y)]
        source = block.at[:, :, :, pl.ds(lanes * half, lanes)]
        copies.append(pltpu.make_async_copy(source, inside, input_sems.at[half]))
    for copy in copies:
        copy.start()
    enter(dims, True)
    for copy, (refs, _, _) in zip(copies[1:], halves):
        copy.wait()
        field, face_out, edge_out, corner_out = refs[0], *refs[4:]

        @pl.loop(0, size_x)
        def _(x):
            for y in range(size_y):
                pack_column(shape, 0, x, y, field[0, x + 1, y + 1], face_out, edge_out)

        pack_corners(shape, 0, field, corner_out)
    copies[0].wait()
    place = place_of(dims)
    max_plane[place] = jnp.full((8, 128), jnp.max(jnp.abs(onsite_here[...])), jnp.float32)
    entered(dims, True)
    for refs, _, sems in halves:
        halo_send(dims, shape, 0, refs, sems)
    max_start(dims, max_plane, max_sems)
    for refs, shifted, _ in halves:
        zero_border(dims, shape, 2, *refs[:4])
        shift_inside(shape, 0, refs[0], shifted)
    spread(onsite_here, levels)
    for step in range(DEG):
        slot, after = step % 2, (step + 1) % 2
        for half, (refs, shifted, sems) in enumerate(halves):
            field, face, edge, corner, face_out, edge_out, corner_out = refs
            halo_wait(dims, shape, slot, refs, sems, True)
            shift_columns(shape, slot, field, face, edge, corner, shifted)
            if step == 1 and half == 0:
                reach = jnp.abs(hopping[0])
                for k in range(1, len(POSITIVE)):
                    reach = reach + jnp.abs(hopping[k])
                bound = max_end(dims, max_plane, max_column, max_sems) + 2.0 * reach
                filter_coefficients(bound, cut_frac[0], coef)

            @pl.loop(0, size_x)
            def _(x):
                totals, centres = apply_rows(shape, slot, x, field, shifted, levels, hopping)
                for y in range(size_y):
                    mine = (site_rows(shape, x, y), slice(lanes * half, lanes * (half + 1)))
                    value = totals[y]
                    if step == 1:
                        older = field[after, x + 1, y + 1]
                        newer = coef[1] * (centres[y] - coef[0] * older)
                        early[mine] = newer
                        value = coef[1] * (value - coef[0] * centres[y])
                    elif step > 1:
                        newer = centres[y]
                        older = early[mine] if step == 2 else field[after, x + 1, y + 1]
                    if step:
                        value = coef[2 * step] * (value - coef[0] * newer)
                        value = value - coef[2 * step + 1] * older
                    if step == DEG - 1:
                        flat[mine] = value
                    field[after, x + 1, y + 1] = value
                    pack_column(shape, after, x, y, value, face_out, edge_out)

            pack_corners(shape, after, field, corner_out)
            halo_send(dims, shape, after, refs, sems)
            shift_inside(shape, after, field, shifted)
            halo_wait(dims, shape, slot, refs, sems, False)
            if step == 0 and half == 0:
                max_middle(dims, max_plane, max_column, max_sems)
    slot = DEG % 2
    per_sum = len(sum_refs) // 3
    sums, sums_two, sums_between = [
        AllReduce(dims, *sum_refs[k * per_sum : (k + 1) * per_sum]) for k in range(3)
    ]
    sums.local[...] = product(flat[...], flat[...])
    sums.scatter()
    for refs, shifted, sems in halves:
        halo_wait(dims, shape, slot, refs, sems, True)
        shift_columns(shape, slot, *refs[:4], shifted)
    sums.across()
    for half, (refs, shifted, sems) in enumerate(halves):

        @pl.loop(0, size_x)
        def _(x):
            totals, _ = apply_rows(shape, slot, x, refs[0], shifted, levels, hopping)
            for y in range(size_y):
                image[site_rows(shape, x, y), lanes * half : lanes * (half + 1)] = totals[y]

    sums.gather()
    for refs, _, sems in halves:
        halo_wait(dims, shape, slot, refs, sems, False)
    sums.finish()
    gram[...] = sums.total[...] / sites
    factor_kernel(PANEL, gram, lower, inverse, work)
    rotate_and_sum(
        dims, sites, flat, image, inverse, first, gram_two, between, moved, sums_two, sums_between
    )


def site_rows(shape, x, y):
    _, size_y, size_z, _ = shape
    return pl.ds(pl.multiple_of((x * size_y + y) * size_z, size_z), size_z)


def product(left, right):
    return lax.dot_general(
        left,
        right,
        (((0,), (0,)), ((), ())),
        precision=HIGHEST,
        preferred_element_type=jnp.float32,
    )


def rotated(flat, factor):
    return lax.dot_general(
        flat,
        factor,
        (((1,), (1,)), ((), ())),
        precision=HIGHEST,
        preferred_element_type=jnp.float32,
    )


def rotate_and_sum(dims, sites, flat, image, inverse, first, gram, between, moved, sums, sums_b):
    first[...] = rotated(flat[...], inverse[...])
    sums.local[...] = product(first[...], first[...])
    sums.scatter()
    moved[...] = rotated(image[...], inverse[...])
    sums_b.local[...] = product(first[...], moved[...])
    sums_b.scatter()
    sums.across()
    sums_b.across()
    sums.gather()
    sums_b.gather()
    sums.finish()
    gram[...] = sums.total[...] / sites
    sums_b.finish()
    between[...] = sums_b.total[...] / sites


def call(kernel, inputs, scalars, outputs, scratch, ident, space=pltpu.VMEM):
    vmem = pl.BlockSpec(memory_space=pltpu.VMEM)
    smem = pl.BlockSpec(memory_space=pltpu.SMEM)
    return pl.pallas_call(
        kernel,
        out_shape=[jax.ShapeDtypeStruct(shape, jnp.float32) for shape in outputs],
        in_specs=[pl.BlockSpec(memory_space=space)] * len(inputs) + [smem] * len(scalars),
        out_specs=[vmem] * len(outputs),
        scratch_shapes=scratch,
        compiler_params=pltpu.CompilerParams(
            collective_id=ident, has_side_effects=True, vmem_limit_bytes=48 << 20
        ),
    )(*inputs, *scalars)


def factor_kernel(nb, gram, lower, inverse, work):
    size = gram.shape[0]
    tiles = size // 128
    groups = nb // 8
    lane = lax.broadcasted_iota(jnp.int32, (8, 128), 1)
    sub = lax.broadcasted_iota(jnp.int32, (8, 128), 0)
    for t in range(tiles):
        work[t] = gram[:, 128 * t : 128 * (t + 1)]
    for t in range(tiles):
        r = lax.broadcasted_iota(jnp.int32, (size, 128), 0)
        c = lax.broadcasted_iota(jnp.int32, (size, 128), 1) + 128 * t
        work[tiles + t] = jnp.where(r == c, 1.0, 0.0)

    def row(v, j):
        return jnp.broadcast_to(v[j % 8 : j % 8 + 1], (8, 128))

    for start in range(0, size, nb):
        stop = start + nb
        active = [t for t in range(tiles) if 128 * (t + 1) > start]
        active += [tiles + t for t in range(tiles) if 128 * t < stop]
        home = start // 128
        panel = {
            t: [work[t, start + 8 * g : start + 8 * g + 8] for g in range(groups)] for t in active
        }
        cols = [
            [
                jnp.broadcast_to(
                    panel[home][g][:, start % 128 + k : start % 128 + k + 1], (8, 128)
                )
                for g in range(groups)
            ]
            for k in range(nb)
        ]
        recip = [jnp.ones((8, 128), jnp.float32)] * groups
        pivots = [jnp.ones((8, 128), jnp.float32)] * groups
        for j in range(nb):
            home_group = j // 8
            pivot = row(cols[j][home_group], j)
            inv = 1.0 / pivot
            at = sub == j % 8
            recip[home_group] = jnp.where(at, inv, recip[home_group])
            pivots[home_group] = jnp.where(at, pivot, pivots[home_group])
            mult = [None] * groups
            for g in range(home_group, groups):
                mult[g] = cols[j][g] * inv
                if g == home_group:
                    mult[g] = jnp.where(sub > j % 8, mult[g], 0.0)
            for k in range(j + 1, nb):
                top = row(cols[k][home_group], j)
                for g in range(home_group, groups):
                    cols[k][g] = cols[k][g] - mult[g] * top
            for t in active:
                top = row(panel[t][home_group], j)
                for g in range(home_group, groups):
                    panel[t][g] = panel[t][g] - mult[g] * top
        if stop < size:
            full = {t: jnp.concatenate(panel[t], 0) if groups > 1 else panel[t][0] for t in active}
            recips = jnp.concatenate(recip, 0) if groups > 1 else recip[0]
            chunks = [(stop, stop + nb)] + [
                (max(128 * u, stop + nb), 128 * (u + 1)) for u in range(tiles)
            ]
            for low, high in chunks:
                if low >= high:
                    continue
                u = low // 128
                left = (full[u] * recips)[:, low - 128 * u : high - 128 * u]
                for t in active:
                    if t < u:
                        continue
                    work[t, low:high] -= lax.dot_general(
                        left, full[t], (((0,), (0,)), ((), ())),
                        precision=HIGHEST, preferred_element_type=jnp.float32)
        for g in range(groups):
            scale = 1.0 / jnp.sqrt(pivots[g])
            at = slice(start + 8 * g, start + 8 * g + 8)
            for t in range(tiles):
                if t in active:
                    keep = lane + 128 * t >= sub + (start + 8 * g)
                    work[t, at] = jnp.where(keep, panel[t][g] * scale, 0.0)
                else:
                    work[t, at] = jnp.zeros((8, 128), jnp.float32)
                if tiles + t in active:
                    inverse[at, 128 * t : 128 * t + 128] = panel[tiles + t][g] * scale
                else:
                    inverse[at, 128 * t : 128 * t + 128] = jnp.zeros((8, 128), jnp.float32)
    for t in range(tiles):
        lower[128 * t : 128 * t + 128, :] = work[t].T

def near_identity_kernel(gram, inverse):
    size = gram.shape[0]
    row = lax.broadcasted_iota(jnp.int32, (size, size), 0)
    col = lax.broadcasted_iota(jnp.int32, (size, size), 1)
    ident = jnp.where(row == col, 1.0, 0.0)
    weight = jnp.where(row > col, 1.0, 0.5 * ident)

    def times(left, right, across):
        return lax.dot_general(
            left, right, (((1,), (across,)), ((), ())),
            precision=HIGHEST, preferred_element_type=jnp.float32,
        )

    error = gram[...] - ident
    shift = None
    for step in range(NEAR_STEPS):
        low = weight * error
        shift = low if shift is None else shift + low - times(low, shift, 0)
        if step < NEAR_STEPS - 1:
            cross = times(low, error, 0)
            error = times(low + cross, low, 1) - cross - cross.T
    inverse[...] = ident - shift
    return jnp.sum(error * error)


def finish_kernel(
    nb, gram, first, between, lower_one, states, projected, factor, lower, inverse, work
):
    factor[...] = lower_one[...]
    left = near_identity_kernel(gram, inverse)

    @pl.when(jnp.logical_not(left < NEAR_LEFT * NEAR_LEFT))
    def _():
        factor_kernel(nb, gram, lower, inverse, work)

    states[...] = rotated(first[...], inverse[...])
    half = rotated(between[...], inverse[...])
    projected[...] = jnp.dot(
        inverse[...], half, precision=HIGHEST, preferred_element_type=jnp.float32
    )


def local_call(kernel, inputs, outputs, scratch):
    vmem = pl.BlockSpec(memory_space=pltpu.VMEM)
    return pl.pallas_call(
        kernel,
        out_shape=[jax.ShapeDtypeStruct(shape, jnp.float32) for shape in outputs],
        in_specs=[vmem] * len(inputs),
        out_specs=[vmem] * len(outputs),
        scratch_shapes=scratch,
        compiler_params=pltpu.CompilerParams(vmem_limit_bytes=32 << 20),
    )(*inputs)


def body(dims, block, onsite, hopping, cut_frac):
    shape = block.shape
    size_x, size_y, size_z, columns = shape
    count = size_x * size_y * size_z
    sites = count * dims[0] * dims[1] * dims[2]
    plane, column = dims[0] * dims[2], dims[1]
    sums = reduce_scratch(dims, columns)
    square = (columns, columns)
    work = pltpu.VMEM((2 * (columns // 128), columns, 128), jnp.float32)
    lanes = columns // HALVES
    part = (size_x, size_y, size_z, lanes)
    first, gram_two, between, lower_one = call(
        functools.partial(filter_kernel, dims, part, sites),
        [pltpu.with_memory_space_constraint(v, pltpu.HBM) for v in (block, onsite)],
        [hopping, cut_frac],
        [(count, columns), square, square, square],
        halo_scratch(part, 2) * HALVES
        + [
            pltpu.VMEM((size_x, size_y, size_z), jnp.float32),
            pltpu.VMEM(part, jnp.float32),
            pltpu.SemaphoreType.DMA((HALVES + 1,)),
            pltpu.VMEM((plane, 8, 128), jnp.float32),
            pltpu.VMEM((column, 8, 128), jnp.float32),
            pltpu.SemaphoreType.DMA((4,)),
            pltpu.VMEM((2 * DEG, 8, 128), jnp.float32),
        ]
        + [pltpu.VMEM((count, columns), jnp.float32)] * 3
        + [pltpu.VMEM(square, jnp.float32)] * 2
        + [work]
        + sums * 3,
        1,
        pltpu.HBM,
    )
    states, projected, factor = local_call(
        functools.partial(finish_kernel, PANEL),
        [gram_two, first, between, lower_one],
        [(count, columns), square, square],
        [pltpu.VMEM(square, jnp.float32), pltpu.VMEM(square, jnp.float32), work],
    )
    return (states.reshape(shape), projected, factor)


def solution(mesh):
    dims = (mesh.shape["gx"], mesh.shape["gy"], mesh.shape["gz"])
    return jax.shard_map(
        functools.partial(body, dims),
        mesh=mesh,
        in_specs=(P("gx", "gy", "gz", None), P("gx", "gy", "gz"), P(), P()),
        out_specs=(P("gx", "gy", "gz", None), P(), P()),
        check_vma=False,
    )
```

```python
import functools

import jax
import jax.numpy as jnp
from jax import lax
from jax.experimental import pallas as pl
from jax.experimental.pallas import tpu as pltpu
from jax.sharding import PartitionSpec as P

DEG = 4
PANEL = 16
NEAR_STEPS = 4
NEAR_LEFT = 1e-3
HALVES = 2
HALO_REFS = 9
MESH = pl.DeviceIdType.MESH
HIGHEST = lax.Precision.HIGHEST
AXES = ("gx", "gy", "gz")
OFFSETS = [
    (dx, dy, dz)
    for dx in (-1, 0, 1)
    for dy in (-1, 0, 1)
    for dz in (-1, 0, 1)
    if (dx, dy, dz) != (0, 0, 0)
]
POSITIVE = [offset for offset in OFFSETS if offset > (0, 0, 0)]


def hop_index(offset):
    return POSITIVE.index(max(offset, tuple(-d for d in offset)))


def plane_peer(dims, offset):
    size_x, _, size_z = dims
    place = lax.axis_index("gx") * size_z + lax.axis_index("gz")
    peer = lax.rem(place + offset, size_x * size_z)
    return peer, {"gx": peer // size_z, "gz": lax.rem(peer, size_z)}


def bits(value, count):
    return [lax.rem(value // (1 << k), 2) for k in range(count)]


def plane_order(dims):
    hops = (0, 1, 2, 1)
    flips = [(a, b) for a in range(dims[0]) for b in range(dims[2]) if (a, b) != (0, 0)]
    return sorted(flips, key=lambda f: -hops[f[1] % 4] - hops[f[1] // 4 * 2 + f[0] // 2])


def plane_peers(dims):
    bits_x, bits_z = [bits(lax.axis_index(axis), size.bit_length() - 1)
                      for axis, size in (("gx", dims[0]), ("gz", dims[2]))]

    def flipped(values, mask):
        return sum((1 - v if mask >> k & 1 else v) * (1 << k) for k, v in enumerate(values))

    for a, b in plane_order(dims):
        gx, gz = flipped(bits_x, a), flipped(bits_z, b)
        yield gx * dims[2] + gz, {"gx": gx, "gz": gz}


def column_peer(dims, offset):
    peer = lax.rem(lax.axis_index("gy") + offset, dims[1])
    return peer, {"gy": peer}


def has_neighbour(dims, offset):
    valid = None
    for axis, size, step in zip(AXES, dims, offset):
        if step:
            place = lax.axis_index(axis)
            here = place < size - 1 if step > 0 else place > 0
            valid = here if valid is None else jnp.logical_and(valid, here)
    return valid


def neighbour(offset):
    return {axis: lax.axis_index(axis) + step for axis, step in zip(AXES, offset) if step}


def enter(dims, halo):
    barrier = pltpu.get_barrier_semaphore()

    @pl.loop(1, dims[0] * dims[2])
    def _(k):
        pl.semaphore_signal(barrier, inc=1, device_id=plane_peer(dims, k)[1], device_id_type=MESH)

    @pl.loop(1, dims[1])
    def _(k):
        pl.semaphore_signal(barrier, inc=1, device_id=column_peer(dims, k)[1], device_id_type=MESH)

    if halo:
        for offset in OFFSETS:

            @pl.when(has_neighbour(dims, offset))
            def _():
                pl.semaphore_signal(
                    barrier, inc=1, device_id=neighbour(offset), device_id_type=MESH
                )


def entered(dims, halo):
    count = dims[0] * dims[2] + dims[1] - 2
    if halo:
        boxes = 1
        for axis, size in zip(AXES, dims):
            place = lax.axis_index(axis)
            boxes = boxes * (3 - (place == 0).astype(jnp.int32) - (place == size - 1).astype(jnp.int32))
        count = count + boxes - 1
    pl.semaphore_wait(pltpu.get_barrier_semaphore(), count)


def wait_bytes(ref, sem):
    pltpu.make_async_copy(ref, ref, sem).wait()


def send(src, dst, send_sem, recv_sem, device):
    pltpu.make_async_remote_copy(
        src_ref=src,
        dst_ref=dst,
        send_sem=send_sem,
        recv_sem=recv_sem,
        device_id=device,
        device_id_type=MESH,
    ).start()


def place_of(dims):
    return lax.axis_index("gx") * dims[2] + lax.axis_index("gz")


class AllReduce:
    def __init__(self, dims, local, total, plane_buf, column_buf, sems):
        self.dims, self.local, self.total = dims, local, total
        self.plane_buf, self.column_buf, self.sems = plane_buf, column_buf, sems
        self.plane, self.column = dims[0] * dims[2], dims[1]
        self.rows = local.shape[0] // self.plane
        self.mine = pl.ds(pl.multiple_of(place_of(dims) * self.rows, self.rows), self.rows)

    def scatter(self):
        for k, (peer, device) in enumerate(plane_peers(self.dims)):
            theirs = pl.ds(pl.multiple_of(peer * self.rows, self.rows), self.rows)
            send(
                self.local.at[theirs], self.plane_buf.at[k],
                self.sems.at[0], self.sems.at[1], device,
            )

    def across(self):
        level = lax.axis_index("gy")
        wait_bytes(self.plane_buf, self.sems.at[1])
        self.column_buf[level] = lax.fori_loop(
            0, self.plane - 1, lambda k, acc: acc + self.plane_buf[k], self.local[self.mine]
        )
        mine = self.column_buf.at[level]
        for k in sorted(range(1, self.column), key=lambda k: -min(k, self.column - k)):
            _, device = column_peer(self.dims, k)
            send(mine, mine, self.sems.at[2], self.sems.at[3], device)

    def gather(self):
        wait_bytes(self.column_buf.at[pl.ds(0, self.column - 1)], self.sems.at[3])
        part = self.column_buf[0]
        for k in range(1, self.column):
            part = part + self.column_buf[k]
        self.total[self.mine] = part
        mine = self.total.at[self.mine]

        for _, device in plane_peers(self.dims):
            send(mine, mine, self.sems.at[4], self.sems.at[5], device)

    def finish(self):
        others = self.total.at[pl.ds(0, (self.plane - 1) * self.rows)]
        wait_bytes(others, self.sems.at[5])
        wait_bytes(self.plane_buf, self.sems.at[0])
        wait_bytes(self.column_buf.at[pl.ds(0, self.column - 1)], self.sems.at[2])
        wait_bytes(others, self.sems.at[4])


def reduce_scratch(dims, size):
    plane, column = dims[0] * dims[2], dims[1]
    rows = size // plane
    return [
        pltpu.VMEM((size, size), jnp.float32),
        pltpu.VMEM((size, size), jnp.float32),
        pltpu.VMEM((plane - 1, rows, size), jnp.float32),
        pltpu.VMEM((column, rows, size), jnp.float32),
        pltpu.SemaphoreType.DMA((6,)),
    ]


def max_start(dims, plane_buf, sems):
    plane = dims[0] * dims[2]
    place = lax.axis_index("gx") * dims[2] + lax.axis_index("gz")

    @pl.loop(1, plane)
    def _(k):
        _, device = plane_peer(dims, k)
        send(plane_buf.at[place], plane_buf.at[place], sems.at[0], sems.at[1], device)


def max_middle(dims, plane_buf, column_buf, sems):
    plane, column = dims[0] * dims[2], dims[1]
    level = lax.axis_index("gy")
    wait_bytes(plane_buf.at[pl.ds(0, plane - 1)], sems.at[1])
    column_buf[level] = jnp.max(plane_buf[...], axis=0)

    @pl.loop(1, column)
    def _(k):
        _, device = column_peer(dims, k)
        send(column_buf.at[level], column_buf.at[level], sems.at[2], sems.at[3], device)


def max_end(dims, plane_buf, column_buf, sems):
    plane, column = dims[0] * dims[2], dims[1]
    wait_bytes(column_buf.at[pl.ds(0, column - 1)], sems.at[3])
    wait_bytes(plane_buf.at[pl.ds(0, plane - 1)], sems.at[0])
    wait_bytes(column_buf.at[pl.ds(0, column - 1)], sems.at[2])
    return jnp.max(column_buf[...], axis=0)


def halo_scratch(shape, slots):
    size_x, size_y, size_z, columns = shape
    f32 = jnp.float32
    return [
        pltpu.VMEM((slots, size_x + 2, size_y + 2, size_z, columns), f32),
        pltpu.VMEM((slots, 2, size_x + 2, size_y, columns), f32),
        pltpu.VMEM((slots, 2, 2, size_x, columns), f32),
        pltpu.VMEM((slots, 2, 2, 2, 8, columns), f32),
        pltpu.VMEM((slots, 2, size_x, size_y, columns), f32),
        pltpu.VMEM((slots, 2, 2, size_x, columns), f32),
        pltpu.VMEM((slots, 2, 2, 2, 8, columns), f32),
        pltpu.VMEM((2, size_x + 2, size_y + 2, size_z, columns), f32),
        pltpu.SemaphoreType.DMA((slots, 2, len(OFFSETS))),
    ]


def halo_parts(shape, slot, offset, field, face, edge, corner, face_out, edge_out, corner_out):
    size_x, size_y, _, _ = shape
    sx, sy, sz = offset
    low = {1: 0, -1: 1}

    def ends(step, size):
        if step == 0:
            return pl.ds(1, size), pl.ds(1, size)
        return (size, 0) if step > 0 else (1, size + 1)

    from_x, to_x = ends(sx, size_x)
    from_y, to_y = ends(sy, size_y)
    if sz == 0:
        return field.at[slot, from_x, from_y], field.at[slot, to_x, to_y]
    top = 1 if sz > 0 else 0
    if sy == 0:
        source = pl.ds(0, size_x) if sx == 0 else from_x - 1
        return face_out.at[slot, top, source], face.at[slot, 1 - top, to_x]
    far = 1 if sy > 0 else 0
    if sx == 0:
        return edge_out.at[slot, top, far], edge.at[slot, 1 - top, 1 - far]
    right = 1 if sx > 0 else 0
    return (
        corner_out.at[slot, top, far, right],
        corner.at[slot, 1 - top, 1 - far, 1 - right],
    )


def zero_border(dims, shape, slots, field, face, edge, corner):
    size_x, size_y, size_z, columns = shape
    for slot in range(slots):
        for side in (0, 1):
            step = 1 if side else -1
            row = size_x + 1 if side else 0

            @pl.when(jnp.logical_not(has_neighbour(dims, (step, 0, 0))))
            def _():
                field[slot, row] = jnp.zeros((size_y + 2, size_z, columns), jnp.float32)
                for top in (0, 1):
                    face[slot, top, row] = jnp.zeros((size_y, columns), jnp.float32)
                    for far in (0, 1):
                        corner[slot, top, far, side] = jnp.zeros((8, columns), jnp.float32)

            row_y = size_y + 1 if side else 0

            @pl.when(jnp.logical_not(has_neighbour(dims, (0, step, 0))))
            def _():
                field[slot, :, row_y] = jnp.zeros((size_x + 2, size_z, columns), jnp.float32)
                for top in (0, 1):
                    edge[slot, top, side] = jnp.zeros((size_x, columns), jnp.float32)
                    for right in (0, 1):
                        corner[slot, top, side, right] = jnp.zeros((8, columns), jnp.float32)

            @pl.when(jnp.logical_not(has_neighbour(dims, (0, 0, step))))
            def _():
                face[slot, side] = jnp.zeros((size_x + 2, size_y, columns), jnp.float32)
                edge[slot, side] = jnp.zeros((2, size_x, columns), jnp.float32)
                corner[slot, side] = jnp.zeros((2, 2, 8, columns), jnp.float32)


def pack_column(shape, slot, x, y, value, face_out, edge_out):
    size_y, size_z = shape[1], shape[2]
    for top, z in ((0, 0), (1, size_z - 1)):
        row = value[z : z + 1]
        face_out[slot, top, x, y : y + 1] = row
        if y in (0, size_y - 1):
            edge_out[slot, top, 1 if y else 0, pl.ds(x, 1)] = row


def pack_corners(shape, slot, field, corner_out):
    size_x, size_y, size_z, columns = shape
    for top in (0, 1):
        for far in (0, 1):
            for right in (0, 1):
                z = (size_z - 1) * top
                corner_out[slot, top, far, right] = jnp.broadcast_to(
                    field[slot, size_x if right else 1, size_y if far else 1, z : z + 1],
                    (8, columns),
                )


def halo_send(dims, shape, slot, refs, sems):
    for index, offset in enumerate(OFFSETS):

        @pl.when(has_neighbour(dims, offset))
        def _():
            src, dst = halo_parts(shape, slot, offset, *refs)
            send(src, dst, sems.at[slot, 0, index], sems.at[slot, 1, index], neighbour(offset))


def halo_wait(dims, shape, slot, refs, sems, received):
    for index, offset in enumerate(OFFSETS):
        from_there = tuple(-step for step in offset)

        @pl.when(has_neighbour(dims, from_there if received else offset))
        def _():
            src, dst = halo_parts(shape, slot, offset, *refs)
            if received:
                wait_bytes(dst, sems.at[slot, 1, index])
            else:
                wait_bytes(src, sems.at[slot, 0, index])


def shift_columns(shape, slot, field, face, edge, corner, shifted):
    size_x, size_y, size_z, columns = shape
    place = lax.broadcasted_iota(jnp.int32, (size_z, columns), 0)

    def put(x, y, below, above):
        value = field[slot, x, y]
        shifted[0, x, y] = jnp.where(place == 0, below, pltpu.roll(value, 1, 0))
        shifted[1, x, y] = jnp.where(place == size_z - 1, above, pltpu.roll(value, size_z - 1, 0))

    @pl.loop(0, size_x + 2)
    def _(x):
        for y in range(size_y):
            put(x, y + 1, face[slot, 0, x, y : y + 1], face[slot, 1, x, y : y + 1])

    for far in (0, 1):
        y = size_y + 1 if far else 0

        @pl.loop(0, size_x)
        def _(x):
            put(x + 1, y, edge[slot, 0, far, pl.ds(x, 1)], edge[slot, 1, far, pl.ds(x, 1)])

        for right in (0, 1):
            x = size_x + 1 if right else 0
            put(x, y, corner[slot, 0, far, right], corner[slot, 1, far, right])


def apply_rows(shape, slot, x, field, shifted, onsite, hopping):
    size_y = shape[1]
    totals = [None] * size_y
    centres = [None] * size_y
    for dx in (-1, 0, 1):
        for y in range(-1, size_y + 1):
            for dz in (-1, 0, 1):
                if dz == 0:
                    value = field[slot, x + 1 + dx, y + 1]
                else:
                    value = shifted[0 if dz < 0 else 1, x + 1 + dx, y + 1]
                for dy in (-1, 0, 1):
                    target = y - dy
                    if not 0 <= target < size_y:
                        continue
                    if (dx, dy, dz) == (0, 0, 0):
                        centres[target] = value
                        level = onsite[x, target]
                        term = level * value
                    else:
                        term = hopping[hop_index((dx, dy, dz))] * value
                    totals[target] = term if totals[target] is None else totals[target] + term
    return totals, centres


def spread(onsite, levels):
    size_x, size_y, size_z, lanes = levels.shape
    diagonal = lax.broadcasted_iota(jnp.int32, (size_z, size_z), 0) == lax.broadcasted_iota(
        jnp.int32, (size_z, size_z), 1
    )

    @pl.loop(0, size_x)
    def _(x):
        for y in range(size_y):
            row = jnp.broadcast_to(onsite[x, y : y + 1], (size_z, size_z))
            column = jnp.sum(jnp.where(diagonal, row, 0.0), axis=1, keepdims=True)
            levels[x, y] = jnp.broadcast_to(column, (size_z, lanes))


def filter_coefficients(bound, cut_frac, coef):
    cut = cut_frac * bound
    half_width = (bound - cut) / 2.0
    center = (bound + cut) / 2.0
    sigma_one = half_width / (-bound - center)
    sigma = sigma_one
    coef[0] = center
    coef[1] = sigma / half_width
    for k in range(1, DEG):
        sigma_next = 1.0 / (2.0 / sigma_one - sigma)
        coef[2 * k] = 2.0 * sigma_next / half_width
        coef[2 * k + 1] = sigma * sigma_next
        sigma = sigma_next


def filter_kernel(
    dims, shape, sites,
    block, onsite, hopping, cut_frac,
    first, gram_two, between, lower,
    *scratch,
):
    size_x, size_y, size_z, lanes = shape
    per_half = HALO_REFS
    halves = []
    for half in range(HALVES):
        *refs, shifted, sems = scratch[half * per_half : (half + 1) * per_half]
        halves.append((tuple(refs), shifted, sems))
    (
        onsite_here, levels, input_sems,
        max_plane, max_column, max_sems, coef,
        flat, image, moved, gram, inverse, work,
        *sum_refs,
    ) = scratch[HALVES * per_half :]
    early = moved
    copies = [pltpu.make_async_copy(onsite, onsite_here, input_sems.at[HALVES])]
    for half, (refs, _, _) in enumerate(halves):
        inside = refs[0].at[0, pl.ds(1, size_x), pl.ds(1, size_y)]
        source = block.at[:, :, :, pl.ds(lanes * half, lanes)]
        copies.append(pltpu.make_async_copy(source, inside, input_sems.at[half]))
    for copy in copies:
        copy.start()
    enter(dims, True)
    for copy, (refs, _, _) in zip(copies[1:], halves):
        copy.wait()
        field, face_out, edge_out, corner_out = refs[0], *refs[4:]

        @pl.loop(0, size_x)
        def _(x):
            for y in range(size_y):
                pack_column(shape, 0, x, y, field[0, x + 1, y + 1], face_out, edge_out)

        pack_corners(shape, 0, field, corner_out)
    copies[0].wait()
    place = place_of(dims)
    max_plane[place] = jnp.full((8, 128), jnp.max(jnp.abs(onsite_here[...])), jnp.float32)
    entered(dims, True)
    for refs, _, sems in halves:
        halo_send(dims, shape, 0, refs, sems)
    max_start(dims, max_plane, max_sems)
    for refs, _, _ in halves:
        zero_border(dims, shape, 2, *refs[:4])
    spread(onsite_here, levels)
    for step in range(DEG):
        slot, after = step % 2, (step + 1) % 2
        for half, (refs, shifted, sems) in enumerate(halves):
            field, face, edge, corner, face_out, edge_out, corner_out = refs
            halo_wait(dims, shape, slot, refs, sems, True)
            shift_columns(shape, slot, field, face, edge, corner, shifted)
            if step == 1 and half == 0:
                reach = jnp.abs(hopping[0])
                for k in range(1, len(POSITIVE)):
                    reach = reach + jnp.abs(hopping[k])
                bound = max_end(dims, max_plane, max_column, max_sems) + 2.0 * reach
                filter_coefficients(bound, cut_frac[0], coef)

            @pl.loop(0, size_x)
            def _(x):
                totals, centres = apply_rows(shape, slot, x, field, shifted, levels, hopping)
                for y in range(size_y):
                    mine = (site_rows(shape, x, y), slice(lanes * half, lanes * (half + 1)))
                    value = totals[y]
                    if step == 1:
                        older = field[after, x + 1, y + 1]
                        newer = coef[1] * (centres[y] - coef[0] * older)
                        early[mine] = newer
                        value = coef[1] * (value - coef[0] * centres[y])
                    elif step > 1:
                        newer = centres[y]
                        older = early[mine] if step == 2 else field[after, x + 1, y + 1]
                    if step:
                        value = coef[2 * step] * (value - coef[0] * newer)
                        value = value - coef[2 * step + 1] * older
                    if step == DEG - 1:
                        flat[mine] = value
                    field[after, x + 1, y + 1] = value
                    pack_column(shape, after, x, y, value, face_out, edge_out)

            pack_corners(shape, after, field, corner_out)
            halo_send(dims, shape, after, refs, sems)
            halo_wait(dims, shape, slot, refs, sems, False)
            if step == 0 and half == 0:
                max_middle(dims, max_plane, max_column, max_sems)
    slot = DEG % 2
    per_sum = len(sum_refs) // 3
    sums, sums_two, sums_between = [
        AllReduce(dims, *sum_refs[k * per_sum : (k + 1) * per_sum]) for k in range(3)
    ]
    sums.local[...] = product(flat[...], flat[...])
    sums.scatter()
    for refs, shifted, sems in halves:
        halo_wait(dims, shape, slot, refs, sems, True)
        shift_columns(shape, slot, *refs[:4], shifted)
    sums.across()
    for half, (refs, shifted, sems) in enumerate(halves):

        @pl.loop(0, size_x)
        def _(x):
            totals, _ = apply_rows(shape, slot, x, refs[0], shifted, levels, hopping)
            for y in range(size_y):
                image[site_rows(shape, x, y), lanes * half : lanes * (half + 1)] = totals[y]

    sums.gather()
    for refs, _, sems in halves:
        halo_wait(dims, shape, slot, refs, sems, False)
    sums.finish()
    gram[...] = sums.total[...] / sites
    factor_kernel(PANEL, gram, lower, inverse, work)
    rotate_and_sum(
        dims, sites, flat, image, inverse, first, gram_two, between, moved, sums_two, sums_between
    )


def site_rows(shape, x, y):
    _, size_y, size_z, _ = shape
    return pl.ds(pl.multiple_of((x * size_y + y) * size_z, size_z), size_z)


def product(left, right):
    return lax.dot_general(
        left,
        right,
        (((0,), (0,)), ((), ())),
        precision=HIGHEST,
        preferred_element_type=jnp.float32,
    )


def rotated(flat, factor):
    return lax.dot_general(
        flat,
        factor,
        (((1,), (1,)), ((), ())),
        precision=HIGHEST,
        preferred_element_type=jnp.float32,
    )


def rotate_and_sum(dims, sites, flat, image, inverse, first, gram, between, moved, sums, sums_b):
    first[...] = rotated(flat[...], inverse[...])
    sums.local[...] = product(first[...], first[...])
    sums.scatter()
    moved[...] = rotated(image[...], inverse[...])
    sums_b.local[...] = product(first[...], moved[...])
    sums_b.scatter()
    sums.across()
    sums_b.across()
    sums.gather()
    sums_b.gather()
    sums.finish()
    gram[...] = sums.total[...] / sites
    sums_b.finish()
    between[...] = sums_b.total[...] / sites


def call(kernel, inputs, scalars, outputs, scratch, ident, space=pltpu.VMEM):
    vmem = pl.BlockSpec(memory_space=pltpu.VMEM)
    smem = pl.BlockSpec(memory_space=pltpu.SMEM)
    return pl.pallas_call(
        kernel,
        out_shape=[jax.ShapeDtypeStruct(shape, jnp.float32) for shape in outputs],
        in_specs=[pl.BlockSpec(memory_space=space)] * len(inputs) + [smem] * len(scalars),
        out_specs=[vmem] * len(outputs),
        scratch_shapes=scratch,
        compiler_params=pltpu.CompilerParams(
            collective_id=ident, has_side_effects=True, vmem_limit_bytes=48 << 20
        ),
    )(*inputs, *scalars)


def factor_kernel(nb, gram, lower, inverse, work):
    size = gram.shape[0]
    tiles = size // 128
    groups = nb // 8
    lane = lax.broadcasted_iota(jnp.int32, (8, 128), 1)
    sub = lax.broadcasted_iota(jnp.int32, (8, 128), 0)
    for t in range(tiles):
        work[t] = gram[:, 128 * t : 128 * (t + 1)]
    for t in range(tiles):
        r = lax.broadcasted_iota(jnp.int32, (size, 128), 0)
        c = lax.broadcasted_iota(jnp.int32, (size, 128), 1) + 128 * t
        work[tiles + t] = jnp.where(r == c, 1.0, 0.0)

    def row(v, j):
        return jnp.broadcast_to(v[j % 8 : j % 8 + 1], (8, 128))

    for start in range(0, size, nb):
        stop = start + nb
        active = [t for t in range(tiles) if 128 * (t + 1) > start]
        active += [tiles + t for t in range(tiles) if 128 * t < stop]
        home = start // 128
        panel = {
            t: [work[t, start + 8 * g : start + 8 * g + 8] for g in range(groups)] for t in active
        }
        cols = [
            [
                jnp.broadcast_to(
                    panel[home][g][:, start % 128 + k : start % 128 + k + 1], (8, 128)
                )
                for g in range(groups)
            ]
            for k in range(nb)
        ]
        recip = [jnp.ones((8, 128), jnp.float32)] * groups
        pivots = [jnp.ones((8, 128), jnp.float32)] * groups
        for j in range(nb):
            home_group = j // 8
            pivot = row(cols[j][home_group], j)
            inv = 1.0 / pivot
            at = sub == j % 8
            recip[home_group] = jnp.where(at, inv, recip[home_group])
            pivots[home_group] = jnp.where(at, pivot, pivots[home_group])
            mult = [None] * groups
            for g in range(home_group, groups):
                mult[g] = cols[j][g] * inv
                if g == home_group:
                    mult[g] = jnp.where(sub > j % 8, mult[g], 0.0)
            for k in range(j + 1, nb):
                top = row(cols[k][home_group], j)
                for g in range(home_group, groups):
                    cols[k][g] = cols[k][g] - mult[g] * top
            for t in active:
                top = row(panel[t][home_group], j)
                for g in range(home_group, groups):
                    panel[t][g] = panel[t][g] - mult[g] * top
        if stop < size:
            full = {t: jnp.concatenate(panel[t], 0) if groups > 1 else panel[t][0] for t in active}
            recips = jnp.concatenate(recip, 0) if groups > 1 else recip[0]
            chunks = [(stop, stop + nb)] + [
                (max(128 * u, stop + nb), 128 * (u + 1)) for u in range(tiles)
            ]
            for low, high in chunks:
                if low >= high:
                    continue
                u = low // 128
                left = (full[u] * recips)[:, low - 128 * u : high - 128 * u]
                for t in active:
                    if t < u:
                        continue
                    work[t, low:high] -= lax.dot_general(
                        left, full[t], (((0,), (0,)), ((), ())),
                        precision=HIGHEST, preferred_element_type=jnp.float32)
        for g in range(groups):
            scale = 1.0 / jnp.sqrt(pivots[g])
            at = slice(start + 8 * g, start + 8 * g + 8)
            for t in range(tiles):
                if t in active:
                    keep = lane + 128 * t >= sub + (start + 8 * g)
                    work[t, at] = jnp.where(keep, panel[t][g] * scale, 0.0)
                else:
                    work[t, at] = jnp.zeros((8, 128), jnp.float32)
                if tiles + t in active:
                    inverse[at, 128 * t : 128 * t + 128] = panel[tiles + t][g] * scale
                else:
                    inverse[at, 128 * t : 128 * t + 128] = jnp.zeros((8, 128), jnp.float32)
    for t in range(tiles):
        lower[128 * t : 128 * t + 128, :] = work[t].T

def near_identity_kernel(gram, inverse):
    size = gram.shape[0]
    row = lax.broadcasted_iota(jnp.int32, (size, size), 0)
    col = lax.broadcasted_iota(jnp.int32, (size, size), 1)
    ident = jnp.where(row == col, 1.0, 0.0)
    weight = jnp.where(row > col, 1.0, 0.5 * ident)

    def times(left, right, across):
        return lax.dot_general(
            left, right, (((1,), (across,)), ((), ())),
            precision=HIGHEST, preferred_element_type=jnp.float32,
        )

    error = gram[...] - ident
    shift = None
    for step in range(NEAR_STEPS):
        low = weight * error
        shift = low if shift is None else shift + low - times(low, shift, 0)
        if step < NEAR_STEPS - 1:
            cross = times(low, error, 0)
            error = times(low + cross, low, 1) - cross - cross.T
    inverse[...] = ident - shift
    return jnp.sum(error * error)


def finish_kernel(
    nb, gram, first, between, lower_one, states, projected, factor, lower, inverse, work
):
    factor[...] = lower_one[...]
    left = near_identity_kernel(gram, inverse)

    @pl.when(jnp.logical_not(left < NEAR_LEFT * NEAR_LEFT))
    def _():
        factor_kernel(nb, gram, lower, inverse, work)

    states[...] = rotated(first[...], inverse[...])
    half = rotated(between[...], inverse[...])
    projected[...] = jnp.dot(
        inverse[...], half, precision=HIGHEST, preferred_element_type=jnp.float32
    )


def local_call(kernel, inputs, outputs, scratch):
    vmem = pl.BlockSpec(memory_space=pltpu.VMEM)
    return pl.pallas_call(
        kernel,
        out_shape=[jax.ShapeDtypeStruct(shape, jnp.float32) for shape in outputs],
        in_specs=[vmem] * len(inputs),
        out_specs=[vmem] * len(outputs),
        scratch_shapes=scratch,
        compiler_params=pltpu.CompilerParams(vmem_limit_bytes=32 << 20),
    )(*inputs)


def body(dims, block, onsite, hopping, cut_frac):
    shape = block.shape
    size_x, size_y, size_z, columns = shape
    count = size_x * size_y * size_z
    sites = count * dims[0] * dims[1] * dims[2]
    plane, column = dims[0] * dims[2], dims[1]
    sums = reduce_scratch(dims, columns)
    square = (columns, columns)
    work = pltpu.VMEM((2 * (columns // 128), columns, 128), jnp.float32)
    lanes = columns // HALVES
    part = (size_x, size_y, size_z, lanes)
    first, gram_two, between, lower_one = call(
        functools.partial(filter_kernel, dims, part, sites),
        [pltpu.with_memory_space_constraint(v, pltpu.HBM) for v in (block, onsite)],
        [hopping, cut_frac],
        [(count, columns), square, square, square],
        halo_scratch(part, 2) * HALVES
        + [
            pltpu.VMEM((size_x, size_y, size_z), jnp.float32),
            pltpu.VMEM(part, jnp.float32),
            pltpu.SemaphoreType.DMA((HALVES + 1,)),
            pltpu.VMEM((plane, 8, 128), jnp.float32),
            pltpu.VMEM((column, 8, 128), jnp.float32),
            pltpu.SemaphoreType.DMA((4,)),
            pltpu.VMEM((2 * DEG, 8, 128), jnp.float32),
        ]
        + [pltpu.VMEM((count, columns), jnp.float32)] * 3
        + [pltpu.VMEM(square, jnp.float32)] * 2
        + [work]
        + sums * 3,
        1,
        pltpu.HBM,
    )
    states, projected, factor = local_call(
        functools.partial(finish_kernel, PANEL),
        [gram_two, first, between, lower_one],
        [(count, columns), square, square],
        [pltpu.VMEM(square, jnp.float32), pltpu.VMEM(square, jnp.float32), work],
    )
    return (states.reshape(shape), projected, factor)


def solution(mesh):
    dims = (mesh.shape["gx"], mesh.shape["gy"], mesh.shape["gz"])
    return jax.shard_map(
        functools.partial(body, dims),
        mesh=mesh,
        in_specs=(P("gx", "gy", "gz", None), P("gx", "gy", "gz"), P(), P()),
        out_specs=(P("gx", "gy", "gz", None), P(), P()),
        check_vma=False,
    )
```

```python
import functools

import jax
import jax.numpy as jnp
from jax import lax
from jax.experimental import pallas as pl
from jax.experimental.pallas import tpu as pltpu
from jax.sharding import PartitionSpec as P

DEG = 4
PANEL = 16
NEAR_STEPS = 4
NEAR_LEFT = 1e-3
HALVES = 2
HALO_REFS = 9
MESH = pl.DeviceIdType.MESH
HIGHEST = lax.Precision.HIGHEST
AXES = ("gx", "gy", "gz")
OFFSETS = [
    (dx, dy, dz)
    for dx in (-1, 0, 1)
    for dy in (-1, 0, 1)
    for dz in (-1, 0, 1)
    if (dx, dy, dz) != (0, 0, 0)
]
POSITIVE = [offset for offset in OFFSETS if offset > (0, 0, 0)]


def hop_index(offset):
    return POSITIVE.index(max(offset, tuple(-d for d in offset)))


def plane_peer(dims, offset):
    size_x, _, size_z = dims
    place = lax.axis_index("gx") * size_z + lax.axis_index("gz")
    peer = lax.rem(place + offset, size_x * size_z)
    return peer, {"gx": peer // size_z, "gz": lax.rem(peer, size_z)}


def bits(value, count):
    return [lax.rem(value // (1 << k), 2) for k in range(count)]


def plane_order(dims):
    hops = (0, 1, 2, 1)
    flips = [(a, b) for a in range(dims[0]) for b in range(dims[2]) if (a, b) != (0, 0)]
    return sorted(flips, key=lambda f: -hops[f[1] % 4] - hops[f[1] // 4 * 2 + f[0] // 2])


def plane_peers(dims):
    bits_x, bits_z = [bits(lax.axis_index(axis), size.bit_length() - 1)
                      for axis, size in (("gx", dims[0]), ("gz", dims[2]))]

    def flipped(values, mask):
        return sum((1 - v if mask >> k & 1 else v) * (1 << k) for k, v in enumerate(values))

    for a, b in plane_order(dims):
        gx, gz = flipped(bits_x, a), flipped(bits_z, b)
        yield gx * dims[2] + gz, {"gx": gx, "gz": gz}


def column_peer(dims, offset):
    peer = lax.rem(lax.axis_index("gy") + offset, dims[1])
    return peer, {"gy": peer}


def has_neighbour(dims, offset):
    valid = None
    for axis, size, step in zip(AXES, dims, offset):
        if step:
            place = lax.axis_index(axis)
            here = place < size - 1 if step > 0 else place > 0
            valid = here if valid is None else jnp.logical_and(valid, here)
    return valid


def neighbour(offset):
    return {axis: lax.axis_index(axis) + step for axis, step in zip(AXES, offset) if step}


def enter(dims, halo):
    barrier = pltpu.get_barrier_semaphore()

    def tell(device):
        pl.semaphore_signal(barrier, inc=1, device_id=device, device_id_type=MESH)

    if halo:
        for offset in sorted(OFFSETS, key=lambda d: -3 * abs(d[2]) - abs(d[1]) - abs(d[0])):

            @pl.when(has_neighbour(dims, offset))
            def _():
                tell(neighbour(offset))

    for k in sorted(range(1, dims[1]), key=lambda k: -min(k, dims[1] - k)):
        tell(column_peer(dims, k)[1])
    for _, device in plane_peers(dims):
        tell(device)


def entered(dims, halo):
    count = dims[0] * dims[2] + dims[1] - 2
    if halo:
        boxes = 1
        for axis, size in zip(AXES, dims):
            place = lax.axis_index(axis)
            boxes = boxes * (3 - (place == 0).astype(jnp.int32) - (place == size - 1).astype(jnp.int32))
        count = count + boxes - 1
    pl.semaphore_wait(pltpu.get_barrier_semaphore(), count)


def wait_bytes(ref, sem):
    pltpu.make_async_copy(ref, ref, sem).wait()


def send(src, dst, send_sem, recv_sem, device):
    pltpu.make_async_remote_copy(
        src_ref=src,
        dst_ref=dst,
        send_sem=send_sem,
        recv_sem=recv_sem,
        device_id=device,
        device_id_type=MESH,
    ).start()


def place_of(dims):
    return lax.axis_index("gx") * dims[2] + lax.axis_index("gz")


class AllReduce:
    def __init__(self, dims, local, total, plane_buf, column_buf, sems):
        self.dims, self.local, self.total = dims, local, total
        self.plane_buf, self.column_buf, self.sems = plane_buf, column_buf, sems
        self.plane, self.column = dims[0] * dims[2], dims[1]
        self.rows = local.shape[0] // self.plane
        self.mine = pl.ds(pl.multiple_of(place_of(dims) * self.rows, self.rows), self.rows)

    def scatter(self):
        for k, (peer, device) in enumerate(plane_peers(self.dims)):
            theirs = pl.ds(pl.multiple_of(peer * self.rows, self.rows), self.rows)
            send(
                self.local.at[theirs], self.plane_buf.at[k],
                self.sems.at[0], self.sems.at[1], device,
            )

    def across(self):
        level = lax.axis_index("gy")
        wait_bytes(self.plane_buf, self.sems.at[1])
        self.column_buf[level] = lax.fori_loop(
            0, self.plane - 1, lambda k, acc: acc + self.plane_buf[k], self.local[self.mine]
        )
        mine = self.column_buf.at[level]
        for k in sorted(range(1, self.column), key=lambda k: -min(k, self.column - k)):
            _, device = column_peer(self.dims, k)
            send(mine, mine, self.sems.at[2], self.sems.at[3], device)

    def gather(self):
        wait_bytes(self.column_buf.at[pl.ds(0, self.column - 1)], self.sems.at[3])
        part = self.column_buf[0]
        for k in range(1, self.column):
            part = part + self.column_buf[k]
        self.total[self.mine] = part
        mine = self.total.at[self.mine]

        for _, device in plane_peers(self.dims):
            send(mine, mine, self.sems.at[4], self.sems.at[5], device)

    def finish(self):
        others = self.total.at[pl.ds(0, (self.plane - 1) * self.rows)]
        wait_bytes(others, self.sems.at[5])
        wait_bytes(self.plane_buf, self.sems.at[0])
        wait_bytes(self.column_buf.at[pl.ds(0, self.column - 1)], self.sems.at[2])
        wait_bytes(others, self.sems.at[4])


def reduce_scratch(dims, size):
    plane, column = dims[0] * dims[2], dims[1]
    rows = size // plane
    return [
        pltpu.VMEM((size, size), jnp.float32),
        pltpu.VMEM((size, size), jnp.float32),
        pltpu.VMEM((plane - 1, rows, size), jnp.float32),
        pltpu.VMEM((column, rows, size), jnp.float32),
        pltpu.SemaphoreType.DMA((6,)),
    ]


def max_start(dims, plane_buf, sems):
    plane = dims[0] * dims[2]
    place = lax.axis_index("gx") * dims[2] + lax.axis_index("gz")

    @pl.loop(1, plane)
    def _(k):
        _, device = plane_peer(dims, k)
        send(plane_buf.at[place], plane_buf.at[place], sems.at[0], sems.at[1], device)


def max_middle(dims, plane_buf, column_buf, sems):
    plane, column = dims[0] * dims[2], dims[1]
    level = lax.axis_index("gy")
    wait_bytes(plane_buf.at[pl.ds(0, plane - 1)], sems.at[1])
    column_buf[level] = jnp.max(plane_buf[...], axis=0)

    @pl.loop(1, column)
    def _(k):
        _, device = column_peer(dims, k)
        send(column_buf.at[level], column_buf.at[level], sems.at[2], sems.at[3], device)


def max_end(dims, plane_buf, column_buf, sems):
    plane, column = dims[0] * dims[2], dims[1]
    wait_bytes(column_buf.at[pl.ds(0, column - 1)], sems.at[3])
    wait_bytes(plane_buf.at[pl.ds(0, plane - 1)], sems.at[0])
    wait_bytes(column_buf.at[pl.ds(0, column - 1)], sems.at[2])
    return jnp.max(column_buf[...], axis=0)


def halo_scratch(shape, slots):
    size_x, size_y, size_z, columns = shape
    f32 = jnp.float32
    return [
        pltpu.VMEM((slots, size_x + 2, size_y + 2, size_z, columns), f32),
        pltpu.VMEM((slots, 2, size_x + 2, size_y, columns), f32),
        pltpu.VMEM((slots, 2, 2, size_x, columns), f32),
        pltpu.VMEM((slots, 2, 2, 2, 8, columns), f32),
        pltpu.VMEM((slots, 2, size_x, size_y, columns), f32),
        pltpu.VMEM((slots, 2, 2, size_x, columns), f32),
        pltpu.VMEM((slots, 2, 2, 2, 8, columns), f32),
        pltpu.VMEM((2, size_x + 2, size_y + 2, size_z, columns), f32),
        pltpu.SemaphoreType.DMA((slots, 2, len(OFFSETS))),
    ]


def halo_parts(shape, slot, offset, field, face, edge, corner, face_out, edge_out, corner_out):
    size_x, size_y, _, _ = shape
    sx, sy, sz = offset
    low = {1: 0, -1: 1}

    def ends(step, size):
        if step == 0:
            return pl.ds(1, size), pl.ds(1, size)
        return (size, 0) if step > 0 else (1, size + 1)

    from_x, to_x = ends(sx, size_x)
    from_y, to_y = ends(sy, size_y)
    if sz == 0:
        return field.at[slot, from_x, from_y], field.at[slot, to_x, to_y]
    top = 1 if sz > 0 else 0
    if sy == 0:
        source = pl.ds(0, size_x) if sx == 0 else from_x - 1
        return face_out.at[slot, top, source], face.at[slot, 1 - top, to_x]
    far = 1 if sy > 0 else 0
    if sx == 0:
        return edge_out.at[slot, top, far], edge.at[slot, 1 - top, 1 - far]
    right = 1 if sx > 0 else 0
    return (
        corner_out.at[slot, top, far, right],
        corner.at[slot, 1 - top, 1 - far, 1 - right],
    )


def zero_border(dims, shape, slots, field, face, edge, corner):
    size_x, size_y, size_z, columns = shape
    for slot in range(slots):
        for side in (0, 1):
            step = 1 if side else -1
            row = size_x + 1 if side else 0

            @pl.when(jnp.logical_not(has_neighbour(dims, (step, 0, 0))))
            def _():
                field[slot, row] = jnp.zeros((size_y + 2, size_z, columns), jnp.float32)
                for top in (0, 1):
                    face[slot, top, row] = jnp.zeros((size_y, columns), jnp.float32)
                    for far in (0, 1):
                        corner[slot, top, far, side] = jnp.zeros((8, columns), jnp.float32)

            row_y = size_y + 1 if side else 0

            @pl.when(jnp.logical_not(has_neighbour(dims, (0, step, 0))))
            def _():
                field[slot, :, row_y] = jnp.zeros((size_x + 2, size_z, columns), jnp.float32)
                for top in (0, 1):
                    edge[slot, top, side] = jnp.zeros((size_x, columns), jnp.float32)
                    for right in (0, 1):
                        corner[slot, top, side, right] = jnp.zeros((8, columns), jnp.float32)

            @pl.when(jnp.logical_not(has_neighbour(dims, (0, 0, step))))
            def _():
                face[slot, side] = jnp.zeros((size_x + 2, size_y, columns), jnp.float32)
                edge[slot, side] = jnp.zeros((2, size_x, columns), jnp.float32)
                corner[slot, side] = jnp.zeros((2, 2, 8, columns), jnp.float32)


def pack_column(shape, slot, x, y, value, face_out, edge_out):
    size_y, size_z = shape[1], shape[2]
    for top, z in ((0, 0), (1, size_z - 1)):
        row = value[z : z + 1]
        face_out[slot, top, x, y : y + 1] = row
        if y in (0, size_y - 1):
            edge_out[slot, top, 1 if y else 0, pl.ds(x, 1)] = row


def pack_corners(shape, slot, field, corner_out):
    size_x, size_y, size_z, columns = shape
    for top in (0, 1):
        for far in (0, 1):
            for right in (0, 1):
                z = (size_z - 1) * top
                corner_out[slot, top, far, right] = jnp.broadcast_to(
                    field[slot, size_x if right else 1, size_y if far else 1, z : z + 1],
                    (8, columns),
                )


def halo_send(dims, shape, slot, refs, sems):
    for index, offset in enumerate(OFFSETS):

        @pl.when(has_neighbour(dims, offset))
        def _():
            src, dst = halo_parts(shape, slot, offset, *refs)
            send(src, dst, sems.at[slot, 0, index], sems.at[slot, 1, index], neighbour(offset))


def halo_wait(dims, shape, slot, refs, sems, received):
    for index, offset in enumerate(OFFSETS):
        from_there = tuple(-step for step in offset)

        @pl.when(has_neighbour(dims, from_there if received else offset))
        def _():
            src, dst = halo_parts(shape, slot, offset, *refs)
            if received:
                wait_bytes(dst, sems.at[slot, 1, index])
            else:
                wait_bytes(src, sems.at[slot, 0, index])


def shift_columns(shape, slot, field, face, edge, corner, shifted):
    size_x, size_y, size_z, columns = shape
    place = lax.broadcasted_iota(jnp.int32, (size_z, columns), 0)

    def put(x, y, below, above):
        value = field[slot, x, y]
        shifted[0, x, y] = jnp.where(place == 0, below, pltpu.roll(value, 1, 0))
        shifted[1, x, y] = jnp.where(place == size_z - 1, above, pltpu.roll(value, size_z - 1, 0))

    @pl.loop(0, size_x + 2)
    def _(x):
        for y in range(size_y):
            put(x, y + 1, face[slot, 0, x, y : y + 1], face[slot, 1, x, y : y + 1])

    for far in (0, 1):
        y = size_y + 1 if far else 0

        @pl.loop(0, size_x)
        def _(x):
            put(x + 1, y, edge[slot, 0, far, pl.ds(x, 1)], edge[slot, 1, far, pl.ds(x, 1)])

        for right in (0, 1):
            x = size_x + 1 if right else 0
            put(x, y, corner[slot, 0, far, right], corner[slot, 1, far, right])


def apply_rows(shape, slot, x, field, shifted, onsite, hopping):
    size_y = shape[1]
    totals = [None] * size_y
    centres = [None] * size_y
    for dx in (-1, 0, 1):
        for y in range(-1, size_y + 1):
            for dz in (-1, 0, 1):
                if dz == 0:
                    value = field[slot, x + 1 + dx, y + 1]
                else:
                    value = shifted[0 if dz < 0 else 1, x + 1 + dx, y + 1]
                for dy in (-1, 0, 1):
                    target = y - dy
                    if not 0 <= target < size_y:
                        continue
                    if (dx, dy, dz) == (0, 0, 0):
                        centres[target] = value
                        level = onsite[x, target]
                        term = level * value
                    else:
                        term = hopping[hop_index((dx, dy, dz))] * value
                    totals[target] = term if totals[target] is None else totals[target] + term
    return totals, centres


def spread(onsite, levels):
    size_x, size_y, size_z, lanes = levels.shape
    diagonal = lax.broadcasted_iota(jnp.int32, (size_z, size_z), 0) == lax.broadcasted_iota(
        jnp.int32, (size_z, size_z), 1
    )

    @pl.loop(0, size_x)
    def _(x):
        for y in range(size_y):
            row = jnp.broadcast_to(onsite[x, y : y + 1], (size_z, size_z))
            column = jnp.sum(jnp.where(diagonal, row, 0.0), axis=1, keepdims=True)
            levels[x, y] = jnp.broadcast_to(column, (size_z, lanes))


def filter_coefficients(bound, cut_frac, coef):
    cut = cut_frac * bound
    half_width = (bound - cut) / 2.0
    center = (bound + cut) / 2.0
    sigma_one = half_width / (-bound - center)
    sigma = sigma_one
    coef[0] = center
    coef[1] = sigma / half_width
    for k in range(1, DEG):
        sigma_next = 1.0 / (2.0 / sigma_one - sigma)
        coef[2 * k] = 2.0 * sigma_next / half_width
        coef[2 * k + 1] = sigma * sigma_next
        sigma = sigma_next


def filter_kernel(
    dims, shape, sites,
    block, onsite, hopping, cut_frac,
    first, gram_two, between, lower,
    *scratch,
):
    size_x, size_y, size_z, lanes = shape
    per_half = HALO_REFS
    halves = []
    for half in range(HALVES):
        *refs, shifted, sems = scratch[half * per_half : (half + 1) * per_half]
        halves.append((tuple(refs), shifted, sems))
    (
        onsite_here, levels, input_sems,
        max_plane, max_column, max_sems, coef,
        flat, image, moved, gram, inverse, work,
        *sum_refs,
    ) = scratch[HALVES * per_half :]
    early = moved
    copies = [pltpu.make_async_copy(onsite, onsite_here, input_sems.at[HALVES])]
    for half, (refs, _, _) in enumerate(halves):
        inside = refs[0].at[0, pl.ds(1, size_x), pl.ds(1, size_y)]
        source = block.at[:, :, :, pl.ds(lanes * half, lanes)]
        copies.append(pltpu.make_async_copy(source, inside, input_sems.at[half]))
    for copy in copies:
        copy.start()
    enter(dims, True)
    for copy, (refs, _, _) in zip(copies[1:], halves):
        copy.wait()
        field, face_out, edge_out, corner_out = refs[0], *refs[4:]

        @pl.loop(0, size_x)
        def _(x):
            for y in range(size_y):
                pack_column(shape, 0, x, y, field[0, x + 1, y + 1], face_out, edge_out)

        pack_corners(shape, 0, field, corner_out)
    copies[0].wait()
    place = place_of(dims)
    max_plane[place] = jnp.full((8, 128), jnp.max(jnp.abs(onsite_here[...])), jnp.float32)
    entered(dims, True)
    for refs, _, sems in halves:
        halo_send(dims, shape, 0, refs, sems)
    max_start(dims, max_plane, max_sems)
    for refs, _, _ in halves:
        zero_border(dims, shape, 2, *refs[:4])
    spread(onsite_here, levels)
    for step in range(DEG):
        slot, after = step % 2, (step + 1) % 2
        for half, (refs, shifted, sems) in enumerate(halves):
            field, face, edge, corner, face_out, edge_out, corner_out = refs
            halo_wait(dims, shape, slot, refs, sems, True)
            shift_columns(shape, slot, field, face, edge, corner, shifted)
            if step == 1 and half == 0:
                reach = jnp.abs(hopping[0])
                for k in range(1, len(POSITIVE)):
                    reach = reach + jnp.abs(hopping[k])
                bound = max_end(dims, max_plane, max_column, max_sems) + 2.0 * reach
                filter_coefficients(bound, cut_frac[0], coef)

            @pl.loop(0, size_x)
            def _(x):
                totals, centres = apply_rows(shape, slot, x, field, shifted, levels, hopping)
                for y in range(size_y):
                    mine = (site_rows(shape, x, y), slice(lanes * half, lanes * (half + 1)))
                    value = totals[y]
                    if step == 1:
                        older = field[after, x + 1, y + 1]
                        newer = coef[1] * (centres[y] - coef[0] * older)
                        early[mine] = newer
                        value = coef[1] * (value - coef[0] * centres[y])
                    elif step > 1:
                        newer = centres[y]
                        older = early[mine] if step == 2 else field[after, x + 1, y + 1]
                    if step:
                        value = coef[2 * step] * (value - coef[0] * newer)
                        value = value - coef[2 * step + 1] * older
                    if step == DEG - 1:
                        flat[mine] = value
                    field[after, x + 1, y + 1] = value
                    pack_column(shape, after, x, y, value, face_out, edge_out)

            pack_corners(shape, after, field, corner_out)
            halo_send(dims, shape, after, refs, sems)
            halo_wait(dims, shape, slot, refs, sems, False)
            if step == 0 and half == 0:
                max_middle(dims, max_plane, max_column, max_sems)
    slot = DEG % 2
    per_sum = len(sum_refs) // 3
    sums, sums_two, sums_between = [
        AllReduce(dims, *sum_refs[k * per_sum : (k + 1) * per_sum]) for k in range(3)
    ]
    sums.local[...] = product(flat[...], flat[...])
    sums.scatter()
    for refs, shifted, sems in halves:
        halo_wait(dims, shape, slot, refs, sems, True)
        shift_columns(shape, slot, *refs[:4], shifted)
    sums.across()
    for half, (refs, shifted, sems) in enumerate(halves):

        @pl.loop(0, size_x)
        def _(x):
            totals, _ = apply_rows(shape, slot, x, refs[0], shifted, levels, hopping)
            for y in range(size_y):
                image[site_rows(shape, x, y), lanes * half : lanes * (half + 1)] = totals[y]

    sums.gather()
    for refs, _, sems in halves:
        halo_wait(dims, shape, slot, refs, sems, False)
    sums.finish()
    gram[...] = sums.total[...] / sites
    factor_kernel(PANEL, gram, lower, inverse, work)
    rotate_and_sum(
        dims, sites, flat, image, inverse, first, gram_two, between, moved, sums_two, sums_between
    )


def site_rows(shape, x, y):
    _, size_y, size_z, _ = shape
    return pl.ds(pl.multiple_of((x * size_y + y) * size_z, size_z), size_z)


def product(left, right):
    return lax.dot_general(
        left,
        right,
        (((0,), (0,)), ((), ())),
        precision=HIGHEST,
        preferred_element_type=jnp.float32,
    )


def rotated(flat, factor):
    return lax.dot_general(
        flat,
        factor,
        (((1,), (1,)), ((), ())),
        precision=HIGHEST,
        preferred_element_type=jnp.float32,
    )


def rotate_and_sum(dims, sites, flat, image, inverse, first, gram, between, moved, sums, sums_b):
    first[...] = rotated(flat[...], inverse[...])
    sums.local[...] = product(first[...], first[...])
    sums.scatter()
    moved[...] = rotated(image[...], inverse[...])
    sums_b.local[...] = product(first[...], moved[...])
    sums_b.scatter()
    sums.across()
    sums_b.across()
    sums.gather()
    sums_b.gather()
    sums.finish()
    gram[...] = sums.total[...] / sites
    sums_b.finish()
    between[...] = sums_b.total[...] / sites


def call(kernel, inputs, scalars, outputs, scratch, ident, space=pltpu.VMEM):
    vmem = pl.BlockSpec(memory_space=pltpu.VMEM)
    smem = pl.BlockSpec(memory_space=pltpu.SMEM)
    return pl.pallas_call(
        kernel,
        out_shape=[jax.ShapeDtypeStruct(shape, jnp.float32) for shape in outputs],
        in_specs=[pl.BlockSpec(memory_space=space)] * len(inputs) + [smem] * len(scalars),
        out_specs=[vmem] * len(outputs),
        scratch_shapes=scratch,
        compiler_params=pltpu.CompilerParams(
            collective_id=ident, has_side_effects=True, vmem_limit_bytes=48 << 20
        ),
    )(*inputs, *scalars)


def factor_kernel(nb, gram, lower, inverse, work):
    size = gram.shape[0]
    tiles = size // 128
    groups = nb // 8
    lane = lax.broadcasted_iota(jnp.int32, (8, 128), 1)
    sub = lax.broadcasted_iota(jnp.int32, (8, 128), 0)
    for t in range(tiles):
        work[t] = gram[:, 128 * t : 128 * (t + 1)]
    for t in range(tiles):
        r = lax.broadcasted_iota(jnp.int32, (size, 128), 0)
        c = lax.broadcasted_iota(jnp.int32, (size, 128), 1) + 128 * t
        work[tiles + t] = jnp.where(r == c, 1.0, 0.0)

    def row(v, j):
        return jnp.broadcast_to(v[j % 8 : j % 8 + 1], (8, 128))

    for start in range(0, size, nb):
        stop = start + nb
        active = [t for t in range(tiles) if 128 * (t + 1) > start]
        active += [tiles + t for t in range(tiles) if 128 * t < stop]
        home = start // 128
        panel = {
            t: [work[t, start + 8 * g : start + 8 * g + 8] for g in range(groups)] for t in active
        }
        cols = [
            [
                jnp.broadcast_to(
                    panel[home][g][:, start % 128 + k : start % 128 + k + 1], (8, 128)
                )
                for g in range(groups)
            ]
            for k in range(nb)
        ]
        recip = [jnp.ones((8, 128), jnp.float32)] * groups
        pivots = [jnp.ones((8, 128), jnp.float32)] * groups
        for j in range(nb):
            home_group = j // 8
            pivot = row(cols[j][home_group], j)
            inv = 1.0 / pivot
            at = sub == j % 8
            recip[home_group] = jnp.where(at, inv, recip[home_group])
            pivots[home_group] = jnp.where(at, pivot, pivots[home_group])
            mult = [None] * groups
            for g in range(home_group, groups):
                mult[g] = cols[j][g] * inv
                if g == home_group:
                    mult[g] = jnp.where(sub > j % 8, mult[g], 0.0)
            for k in range(j + 1, nb):
                top = row(cols[k][home_group], j)
                for g in range(home_group, groups):
                    cols[k][g] = cols[k][g] - mult[g] * top
            for t in active:
                top = row(panel[t][home_group], j)
                for g in range(home_group, groups):
                    panel[t][g] = panel[t][g] - mult[g] * top
        if stop < size:
            full = {t: jnp.concatenate(panel[t], 0) if groups > 1 else panel[t][0] for t in active}
            recips = jnp.concatenate(recip, 0) if groups > 1 else recip[0]
            chunks = [(stop, stop + nb)] + [
                (max(128 * u, stop + nb), 128 * (u + 1)) for u in range(tiles)
            ]
            for low, high in chunks:
                if low >= high:
                    continue
                u = low // 128
                left = (full[u] * recips)[:, low - 128 * u : high - 128 * u]
                for t in active:
                    if t < u:
                        continue
                    work[t, low:high] -= lax.dot_general(
                        left, full[t], (((0,), (0,)), ((), ())),
                        precision=HIGHEST, preferred_element_type=jnp.float32)
        for g in range(groups):
            scale = 1.0 / jnp.sqrt(pivots[g])
            at = slice(start + 8 * g, start + 8 * g + 8)
            for t in range(tiles):
                if t in active:
                    keep = lane + 128 * t >= sub + (start + 8 * g)
                    work[t, at] = jnp.where(keep, panel[t][g] * scale, 0.0)
                else:
                    work[t, at] = jnp.zeros((8, 128), jnp.float32)
                if tiles + t in active:
                    inverse[at, 128 * t : 128 * t + 128] = panel[tiles + t][g] * scale
                else:
                    inverse[at, 128 * t : 128 * t + 128] = jnp.zeros((8, 128), jnp.float32)
    for t in range(tiles):
        lower[128 * t : 128 * t + 128, :] = work[t].T

def near_identity_kernel(gram, inverse):
    size = gram.shape[0]
    row = lax.broadcasted_iota(jnp.int32, (size, size), 0)
    col = lax.broadcasted_iota(jnp.int32, (size, size), 1)
    ident = jnp.where(row == col, 1.0, 0.0)
    weight = jnp.where(row > col, 1.0, 0.5 * ident)

    def times(left, right, across):
        return lax.dot_general(
            left, right, (((1,), (across,)), ((), ())),
            precision=HIGHEST, preferred_element_type=jnp.float32,
        )

    error = gram[...] - ident
    shift = None
    for step in range(NEAR_STEPS):
        low = weight * error
        shift = low if shift is None else shift + low - times(low, shift, 0)
        if step < NEAR_STEPS - 1:
            cross = times(low, error, 0)
            error = times(low + cross, low, 1) - cross - cross.T
    inverse[...] = ident - shift
    return jnp.sum(error * error)


def finish_kernel(
    nb, gram, first, between, lower_one, states, projected, factor, lower, inverse, work
):
    factor[...] = lower_one[...]
    left = near_identity_kernel(gram, inverse)

    @pl.when(jnp.logical_not(left < NEAR_LEFT * NEAR_LEFT))
    def _():
        factor_kernel(nb, gram, lower, inverse, work)

    states[...] = rotated(first[...], inverse[...])
    half = rotated(between[...], inverse[...])
    projected[...] = jnp.dot(
        inverse[...], half, precision=HIGHEST, preferred_element_type=jnp.float32
    )


def local_call(kernel, inputs, outputs, scratch):
    vmem = pl.BlockSpec(memory_space=pltpu.VMEM)
    return pl.pallas_call(
        kernel,
        out_shape=[jax.ShapeDtypeStruct(shape, jnp.float32) for shape in outputs],
        in_specs=[vmem] * len(inputs),
        out_specs=[vmem] * len(outputs),
        scratch_shapes=scratch,
        compiler_params=pltpu.CompilerParams(vmem_limit_bytes=32 << 20),
    )(*inputs)


def body(dims, block, onsite, hopping, cut_frac):
    shape = block.shape
    size_x, size_y, size_z, columns = shape
    count = size_x * size_y * size_z
    sites = count * dims[0] * dims[1] * dims[2]
    plane, column = dims[0] * dims[2], dims[1]
    sums = reduce_scratch(dims, columns)
    square = (columns, columns)
    work = pltpu.VMEM((2 * (columns // 128), columns, 128), jnp.float32)
    lanes = columns // HALVES
    part = (size_x, size_y, size_z, lanes)
    first, gram_two, between, lower_one = call(
        functools.partial(filter_kernel, dims, part, sites),
        [pltpu.with_memory_space_constraint(v, pltpu.HBM) for v in (block, onsite)],
        [hopping, cut_frac],
        [(count, columns), square, square, square],
        halo_scratch(part, 2) * HALVES
        + [
            pltpu.VMEM((size_x, size_y, size_z), jnp.float32),
            pltpu.VMEM(part, jnp.float32),
            pltpu.SemaphoreType.DMA((HALVES + 1,)),
            pltpu.VMEM((plane, 8, 128), jnp.float32),
            pltpu.VMEM((column, 8, 128), jnp.float32),
            pltpu.SemaphoreType.DMA((4,)),
            pltpu.VMEM((2 * DEG, 8, 128), jnp.float32),
        ]
        + [pltpu.VMEM((count, columns), jnp.float32)] * 3
        + [pltpu.VMEM(square, jnp.float32)] * 2
        + [work]
        + sums * 3,
        1,
        pltpu.HBM,
    )
    states, projected, factor = local_call(
        functools.partial(finish_kernel, PANEL),
        [gram_two, first, between, lower_one],
        [(count, columns), square, square],
        [pltpu.VMEM(square, jnp.float32), pltpu.VMEM(square, jnp.float32), work],
    )
    return (states.reshape(shape), projected, factor)


def solution(mesh):
    dims = (mesh.shape["gx"], mesh.shape["gy"], mesh.shape["gz"])
    return jax.shard_map(
        functools.partial(body, dims),
        mesh=mesh,
        in_specs=(P("gx", "gy", "gz", None), P("gx", "gy", "gz"), P(), P()),
        out_specs=(P("gx", "gy", "gz", None), P(), P()),
        check_vma=False,
    )
```
